32 devices in a mesh: row: 8 (over z, x), col: 4 (over y, core).
Axes of the slice: x: 2, y: 2, z: 4, core: 2. Of those that a mesh axis runs over, the one named last changes fastest.
Arguments:
- features: bfloat16 [32768, 1024], P(('row', 'col')), may hold values from -12 to 12
- cotangent: bfloat16 [32768, 1024], P(('row', 'col')), may hold values from -6 to 6
- loader: int32 [32768], replicated, may hold values from 0 to 32767, as said below
- w_query: bfloat16 [1024, 1024], replicated, may hold values from -2 to 2
- w_key: bfloat16 [1024, 1024], replicated, may hold values from -2 to 2
- w_value: bfloat16 [1024, 1024], replicated, may hold values from -0.1875 to 0.1875
- norm_gain: float32 [1024], replicated, may hold values from 0.25 to 1.75
- send_blocks: int32 [32, 4, 2], replicated, may hold values from -1 to 7, as said below
- tile_lists: int32 [256, 3], P(('row', 'col')), may hold values from 0 to 15, as said below
Outputs:
- layer_out: bfloat16 [32768, 1024], P(('row', 'col'))
- grad_features: bfloat16 [32768, 1024], P(('row', 'col'))
The draws below stay inside these ranges and needn't reach their ends.
Inputs may be any that keep to these rules, and one draw needn't show every extreme that they name: `loader`: a permutation of the 32768 node numbers; the 1024 rows of each device hold exactly 32 nodes owned by each device. `send_blocks`: entry [e, p, s] is a block of device e (a number below 8) sent to the device of e's row group with col index p in slot s, or -1 for an empty slot; the nonempty slots of one (e, p) come first and name distinct blocks; slots toward e's own col index are empty; all 2 slots toward the next col index (cyclically) are filled. `tile_lists`: row b names 3 distinct entries of the tile table of b's device, never b's own block and never an empty slot; every nonempty received slot is named by some block of its device.
All inputs are finite; a program needn't handle non-finite values.
Results may differ from the reference program's by a relative error of at most 0.012.
The reference program's roundings to bfloat16 on the way count: a program that leaves them out, or rounds other values in their place, can miss the bound.
Values may be sent and summed in bfloat16 or wider, within the bound.
No kernel may reach another device: no remote copies, remote signals or barrier semaphores. Data moves between devices by JAX's collectives and lax.ppermute only.
A program may use at most 256 MiB of HBM per device.

```python
import math
import jax
import jax.numpy as jnp
from jax import lax

HEADS = 8
HEAD_DIM = 128
D = 1024
BLOCK = 128
NBR = 3
CAP = 2
NB_DEV = 8
NODES_DEV = 1024
NODES = 32768
NBLOCKS = 256
SLOTS = 16
N_ROW = 8
N_COL = 4


def loader_table(key):
    devices = N_ROW * N_COL
    per_peer = NODES_DEV // devices
    first_key, second_key = jax.random.split(jax.random.fold_in(key, 31))
    owner_perm = jax.vmap(lambda sub_key: jax.random.permutation(sub_key, NODES_DEV))(jax.random.split(first_key, devices))
    node_ids = owner_perm.astype(jnp.int32) + (jnp.arange(devices).astype(jnp.int32) * NODES_DEV)[:, None]
    node_ids = node_ids.reshape(devices, devices, per_peer).transpose(1, 0, 2).reshape(devices, NODES_DEV)
    shuffle = jax.vmap(lambda sub_key: jax.random.permutation(sub_key, NODES_DEV))(jax.random.split(second_key, devices))
    node_ids = jnp.take_along_axis(node_ids, shuffle.astype(jnp.int32), axis=1)
    return node_ids.reshape(NODES_DEV * devices).astype(jnp.int32)


def draw_loader(key, part):
    return loader_table(key)


def graph_tables(key):
    devices = N_ROW * N_COL
    slots = NB_DEV + N_COL * CAP
    count_key, order_key, score_key = jax.random.split(jax.random.fold_in(key, 11), 3)
    counts = jax.random.randint(count_key, (devices, N_COL), 0, CAP + 1).astype(jnp.int32)
    col_ids = jnp.arange(devices).astype(jnp.int32) % N_COL
    row_ids = jnp.arange(devices).astype(jnp.int32) // N_COL
    peers = jnp.arange(N_COL).astype(jnp.int32)
    right_peer = (col_ids + 1) % N_COL
    counts = jnp.where(peers[None, :] == right_peer[:, None], CAP, counts)
    counts = jnp.where(peers[None, :] == col_ids[:, None], 0, counts)
    order = jax.vmap(lambda sub_key: jax.random.permutation(sub_key, NB_DEV))(jax.random.split(order_key, devices * N_COL))
    order = order.astype(jnp.int32).reshape(devices, N_COL, NB_DEV)[:, :, :CAP]
    slot_ids = jnp.arange(CAP).astype(jnp.int32)
    send_table = jnp.where(slot_ids[None, None, :] < counts[:, :, None], order, -1).astype(jnp.int32)
    sources = row_ids[:, None] * N_COL + peers[None, :]
    recv_counts = counts[sources, col_ids[:, None]]
    valid = (slot_ids[None, None, :] < recv_counts[:, :, None]).reshape(devices, N_COL * CAP)
    entry_ids = jnp.arange(slots).astype(jnp.int32)
    scores = jax.random.randint(score_key, (devices, NB_DEV, slots), 0, 1024).astype(jnp.int32) * slots + entry_ids
    block_ids = jnp.arange(NB_DEV).astype(jnp.int32)
    local_ok = jnp.broadcast_to((block_ids[:, None] != block_ids[None, :])[None], (devices, NB_DEV, NB_DEV))
    remote_ok = jnp.broadcast_to(valid[:, None, :], (devices, NB_DEV, N_COL * CAP))
    allowed = jnp.concatenate([local_ok, remote_ok], axis=2)
    remote_ids = jnp.arange(N_COL * CAP).astype(jnp.int32)
    forced_remote = remote_ids[None, :] % NB_DEV == block_ids[:, None]
    forced = jnp.concatenate([jnp.zeros((NB_DEV, NB_DEV), bool), forced_remote], axis=1)[None] & allowed
    ranked = jnp.where(forced, scores + (1 << 24), jnp.where(allowed, scores, -1 - entry_ids))
    picks = lax.top_k(ranked, NBR)[1].astype(jnp.int32)
    return (send_table, picks.reshape(devices * NB_DEV, NBR))


def draw_send_blocks(key, part):
    return graph_tables(key)[0]


def draw_tile_lists(key, part):
    return graph_tables(key)[1]


def weight_pair(key):
    base = jnp.clip(jax.random.normal(jax.random.fold_in(key, 21), (D, D), jnp.float32), -6.0, 6.0) / math.sqrt(D)
    other = jnp.clip(jax.random.normal(jax.random.fold_in(key, 22), (D, D), jnp.float32), -6.0, 6.0) / math.sqrt(D)
    return (base, other)


def draw_w_query(key, part):
    base, other = weight_pair(key)
    return base.astype(jnp.bfloat16)


def draw_w_key(key, part):
    base, other = weight_pair(key)
    return other.astype(jnp.bfloat16)


def draw_features(key, part):
    node_of_row = loader_table(key)
    noise_key = jax.random.fold_in(jax.random.fold_in(key, 41), 0)
    nodes = NODES_DEV * N_ROW * N_COL
    by_node = jnp.clip(jax.random.normal(noise_key, (nodes, D), jnp.float32), -6.0, 6.0)
    return by_node[node_of_row].astype(jnp.bfloat16)


def level_of(stream_key, dims, cuts, smallest, top_value):
    def one(axis_at, blocks):
        heights = jax.random.uniform(jax.random.fold_in(jax.random.fold_in(stream_key, 6), axis_at), (blocks,), jnp.float32, smallest / len(cuts), top_value / len(cuts))
        return jnp.repeat(jnp.exp(heights), dims[axis_at] // blocks).reshape((-1,) + (1,) * (len(dims) - axis_at - 1))

    loudness = one(*cuts[0])
    for cut in cuts[1:]:
        loudness = loudness * one(*cut)
    return loudness


def noise(rng, shape, spread, reach, shards=(), kind=jnp.bfloat16):
    array = jax.random.normal(rng, shape, jnp.float32) * spread
    if len(shards) > 0:
        array = level_of(rng, shape, shards, -0.22, 0.18) * array
    return jnp.clip(array, min=-reach, max=reach).astype(kind)


def setup_inputs(seed: int = 0) -> dict:
    key_of = jax.random.split(jax.random.key(seed), 10)
    features = draw_features(jax.random.fold_in(key_of[9], 71), 0)
    cotangent = noise(key_of[1], (NODES, D), 1.0, 6.0, ((0, 32),))
    loader = draw_loader(jax.random.fold_in(key_of[9], 71), 0)
    w_query = draw_w_query(jax.random.fold_in(key_of[9], 71), 0)
    w_key = draw_w_key(jax.random.fold_in(key_of[9], 71), 0)
    w_value = noise(key_of[5], (D, D), D ** -0.5, 0.1875)
    norm_gain = jnp.clip(1.0 + 0.15 * jax.random.normal(key_of[6], (D,), jnp.float32), 0.25, 1.75)
    send_blocks = draw_send_blocks(jax.random.fold_in(key_of[9], 71), 0)
    tile_lists = draw_tile_lists(jax.random.fold_in(key_of[9], 71), 0)
    return {"features": features, "cotangent": cotangent, "loader": loader, "w_query": w_query, "w_key": w_key, "w_value": w_value, "norm_gain": norm_gain, "send_blocks": send_blocks, "tile_lists": tile_lists}


def attend(queries, key_rows, value_rows, cot_rows, gain_row):
    count = queries.shape[0]
    q_heads = queries.astype(jnp.float32).reshape(count, BLOCK, HEADS, HEAD_DIM)
    k_heads = key_rows.astype(jnp.float32).reshape(count, -1, HEADS, HEAD_DIM)
    v_heads = value_rows.astype(jnp.float32).reshape(count, -1, HEADS, HEAD_DIM)
    score_scale = HEAD_DIM ** (-0.5)
    scores = jnp.einsum('bqhd,bkhd->bhqk', q_heads, k_heads) * score_scale
    row_max = lax.optimization_barrier(jnp.max(scores, axis=-1, keepdims=True))
    expo = jnp.exp(scores - row_max)
    prob_full = expo / lax.optimization_barrier(jnp.sum(expo, axis=-1, keepdims=True))
    prob_half = prob_full.astype(jnp.bfloat16)
    mixed_out = jnp.einsum('bhqk,bkhd->bqhd', prob_half.astype(jnp.float32), v_heads).reshape(count, BLOCK, D)
    inv_rms = lax.rsqrt(lax.optimization_barrier(jnp.mean(mixed_out * mixed_out, axis=-1, keepdims=True)) + 1e-06)
    normed = (mixed_out * inv_rms * gain_row).astype(jnp.bfloat16)
    grad_in = cot_rows.astype(jnp.float32) * gain_row
    inner = lax.optimization_barrier(jnp.mean(grad_in * mixed_out, axis=-1, keepdims=True))
    grad_mix = (inv_rms * (grad_in - mixed_out * inv_rms * inv_rms * inner)).astype(jnp.bfloat16)
    grad_heads = grad_mix.astype(jnp.float32).reshape(count, BLOCK, HEADS, HEAD_DIM)
    grad_prob = jnp.einsum('bqhd,bkhd->bhqk', grad_heads, v_heads)
    delta = lax.optimization_barrier(jnp.sum(prob_full * grad_prob, axis=-1, keepdims=True))
    grad_score = (prob_full * (grad_prob - delta) * score_scale).astype(jnp.bfloat16).astype(jnp.float32)
    grad_query = jnp.einsum('bhqk,bkhd->bqhd', grad_score, k_heads).reshape(count, BLOCK, D).astype(jnp.bfloat16)
    grad_key = jnp.einsum('bhqk,bqhd->bkhd', grad_score, q_heads).reshape(count, -1, D)
    grad_value = jnp.einsum('bhqk,bqhd->bkhd', prob_half.astype(jnp.float32), grad_heads).reshape(count, -1, D)
    return (normed, grad_query, grad_key, grad_value)

def reference(features, cotangent, loader, w_query, w_key, w_value, norm_gain, send_blocks, tile_lists):
    devices = N_ROW * N_COL
    owned_rows = jnp.zeros_like(features).at[loader].set(features)
    owned_cot = jnp.zeros_like(cotangent).at[loader].set(cotangent)
    queries = jnp.dot(owned_rows, w_query, preferred_element_type=jnp.float32).astype(jnp.bfloat16)
    key_all = jnp.dot(owned_rows, w_key, preferred_element_type=jnp.float32).astype(jnp.bfloat16)
    value_all = jnp.dot(owned_rows, w_value, preferred_element_type=jnp.float32).astype(jnp.bfloat16)
    kv_blocks = jnp.concatenate([key_all, value_all], axis=1).reshape(NBLOCKS, BLOCK, 2 * D)
    w_back = jnp.concatenate([w_key.T, w_value.T], axis=0)
    device_ids = jnp.arange(devices).astype(jnp.int32)
    row_ids = device_ids // N_COL
    col_ids = device_ids % N_COL
    local_entries = device_ids[:, None] * NB_DEV + jnp.arange(NB_DEV).astype(jnp.int32)[None, :]
    sources = row_ids[:, None] * N_COL + jnp.arange(N_COL).astype(jnp.int32)[None, :]
    sent_blocks = send_blocks[sources, col_ids[:, None]]
    remote_entries = sources[:, :, None] * NB_DEV + jnp.maximum(sent_blocks, 0)
    entry_blocks = jnp.concatenate([local_entries, remote_entries.reshape(devices, N_COL * CAP)], axis=1).astype(jnp.int32)
    own_column = jnp.broadcast_to(jnp.arange(NB_DEV).astype(jnp.int32)[None, :, None], (devices, NB_DEV, 1))
    read_entries = jnp.concatenate([own_column, tile_lists.reshape(devices, NB_DEV, NBR)], axis=2).astype(jnp.int32)
    slot_ids = jnp.arange(SLOTS).astype(jnp.int32)
    q_blocks = queries.reshape(devices, NB_DEV, BLOCK, D)
    cot_blocks = owned_cot.reshape(devices, NB_DEV, BLOCK, D)

    def per_device(totals, inputs):
        q_dev, cot_dev, entries, reads = inputs
        global_reads = entries[reads]
        selected = kv_blocks[global_reads].reshape(NB_DEV, (1 + NBR) * BLOCK, 2 * D)
        normed, grad_query, grad_key, grad_value = attend(q_dev, selected[:, :, :D], selected[:, :, D:], cot_dev, norm_gain)
        grad_tiles = jnp.concatenate([grad_key, grad_value], axis=-1).reshape(NB_DEV * (1 + NBR), BLOCK * 2 * D)
        one_hot = (reads.reshape(-1)[:, None] == slot_ids[None, :]).astype(jnp.float32)
        entry_sum = jnp.dot(one_hot.T, grad_tiles, precision=lax.Precision.HIGHEST)
        local_kv = entry_sum[:NB_DEV].reshape(NODES_DEV, 2 * D).astype(jnp.bfloat16)
        remote_kv = entry_sum[NB_DEV:].reshape(N_COL * CAP * BLOCK, 2 * D).astype(jnp.bfloat16)
        remote_proj = jnp.dot(remote_kv, w_back, preferred_element_type=jnp.float32).astype(jnp.bfloat16)
        totals = totals.at[entries[NB_DEV:]].add(remote_proj.astype(jnp.float32).reshape(N_COL * CAP, BLOCK, D))
        return (totals, (normed.reshape(NODES_DEV, D), grad_query.reshape(NODES_DEV, D), local_kv))
    start = jnp.zeros((NBLOCKS, BLOCK, D), jnp.float32)
    totals, (normed_all, grad_query_all, local_kv_all) = lax.scan(per_device, start, (q_blocks, cot_blocks, entry_blocks, read_entries))
    grad_query_rows = grad_query_all.reshape(NODES, D)
    grad_owned = jnp.dot(grad_query_rows, w_query.T, preferred_element_type=jnp.float32)
    grad_owned = grad_owned + jnp.dot(local_kv_all.reshape(NODES, 2 * D), w_back, preferred_element_type=jnp.float32)
    grad_owned = (grad_owned + totals.reshape(NODES, D)).astype(jnp.bfloat16)
    layer_owned = normed_all.reshape(NODES, D)
    return (layer_owned[loader], grad_owned[loader])
```

```python
import functools

import jax
import jax.numpy as jnp
from jax import lax
from jax.experimental import pallas as pl
from jax.experimental.pallas import tpu as pltpu
from jax.sharding import PartitionSpec as P

HEADS = 8
HEAD_DIM = 128
SCALE = HEAD_DIM ** (-0.5)
LANE = 128
VMEM_LIMIT = 60 * 1024 * 1024

NT = (((1,), (1,)), ((), ()))
TN = (((0,), (0,)), ((), ()))
bf16 = jnp.bfloat16
f32 = jnp.float32


def params(steps=1):
    return pltpu.CompilerParams(
        dimension_semantics=("arbitrary",) * steps, vmem_limit_bytes=VMEM_LIMIT
    )


def whole(shape):
    zeros = (0,) * len(shape)
    return pl.BlockSpec(shape, lambda *_: zeros, pipeline_mode=pl.Buffered(1))


def matmul(left, right):
    return jnp.dot(left, right, preferred_element_type=f32)


def iota(shape, axis):
    return lax.broadcasted_iota(jnp.int32, shape, axis)


def lane_rank(mask):
    rows, count = mask.shape
    before = (iota((LANE, LANE), 0) < iota((LANE, LANE), 1)).astype(f32).astype(bf16)
    carry = jnp.zeros((rows, 1), f32)
    pieces = []
    for at in range(0, count, LANE):
        part = mask[:, at : at + LANE]
        pieces.append(matmul(part.astype(bf16), before) + carry)
        carry = carry + jnp.sum(part, axis=1, keepdims=True)
    return jnp.concatenate(pieces, axis=1)


def send_slots(nodes, devices):
    rows_dev = nodes.shape[1]
    per_peer = rows_dev // devices
    owner = lax.shift_right_logical(nodes, rows_dev.bit_length() - 1)
    owners = iota((devices, rows_dev), 0)
    mask = (owner == owners).astype(f32)
    slot = mask * (lane_rank(mask) + (owners * per_peer).astype(f32))
    return jnp.sum(slot, axis=0, keepdims=True).astype(jnp.int32)


def one_hot(cond):
    return jnp.where(cond, 1.0, 0.0)


def send_kernel(self_ref, loader_ref, rows_ref, out_ref, slot_ref):
    step = pl.program_id(0)
    chunk = out_ref.shape[0]
    rows_dev = rows_ref.shape[0]

    @pl.when(step == 0)
    def _():
        nodes = loader_ref[pl.ds(self_ref[0], 1), :]
        slot_ref[...] = send_slots(nodes, loader_ref.shape[0])

    pick = one_hot(slot_ref[...] == iota((chunk, rows_dev), 0) + step * chunk)
    out_ref[...] = matmul(pick.astype(bf16), rows_ref[...]).astype(bf16)


def send_permute(self_id, loader, rows):
    rows_dev, width = rows.shape
    chunk = 256
    return pl.pallas_call(
        send_kernel,
        out_shape=jax.ShapeDtypeStruct((rows_dev, width), bf16),
        grid_spec=pltpu.PrefetchScalarGridSpec(
            num_scalar_prefetch=1,
            grid=(rows_dev // chunk,),
            in_specs=[whole(loader.shape), whole(rows.shape)],
            out_specs=pl.BlockSpec((chunk, width), lambda i, _: (i, 0)),
            scratch_shapes=[pltpu.VMEM((1, rows_dev), jnp.int32)],
        ),
        compiler_params=params(),
        name="send_permute",
    )(self_id, loader, rows)


def index_kernel(self_ref, loader_ref, to_node_ref, from_node_ref, to_row_ref, slot_ref, key_ref):
    step = pl.program_id(0)
    devices, rows_dev = loader_ref.shape
    per_peer = rows_dev // devices
    chunk = from_node_ref.shape[0]
    sources = chunk // per_peer
    me = self_ref[0]

    @pl.when(step == 0)
    def _():
        slot_ref[...] = send_slots(loader_ref[pl.ds(me, 1), :], devices)
        owner = lax.shift_right_logical(loader_ref[...], rows_dev.bit_length() - 1)
        mask = (owner == me).astype(f32)
        rank = lane_rank(mask).astype(jnp.int32)
        key_ref[...] = jnp.where(owner == me, rank, -1)

    pieces = []
    for t in range(sources):
        source = step * sources + t
        key = key_ref[pl.ds(source, 1), :]
        local = loader_ref[pl.ds(source, 1), :] - me * rows_dev
        hit = key == iota((per_peer, rows_dev), 0)
        pieces.append(jnp.sum(jnp.where(hit, local.astype(f32), 0.0), axis=1, keepdims=True))
    arriving = jnp.concatenate(pieces, axis=0).astype(jnp.int32)
    pick = one_hot(arriving == iota((chunk, rows_dev), 1))
    from_node_ref[...] = pick.astype(bf16)
    to_node_ref[...] = pick.T.astype(bf16)
    back = one_hot(slot_ref[...] == iota((chunk, rows_dev), 0) + step * chunk)
    to_row_ref[...] = back.T.astype(bf16)


def index_tables(self_id, loader, rows_dev):
    chunk = LANE
    square = jax.ShapeDtypeStruct((rows_dev, rows_dev), bf16)
    return pl.pallas_call(
        index_kernel,
        out_shape=(square, square, square),
        grid_spec=pltpu.PrefetchScalarGridSpec(
            num_scalar_prefetch=1,
            grid=(rows_dev // chunk,),
            in_specs=[whole(loader.shape)],
            out_specs=(
                pl.BlockSpec((rows_dev, chunk), lambda i, _: (0, i)),
                pl.BlockSpec((chunk, rows_dev), lambda i, _: (i, 0)),
                pl.BlockSpec((rows_dev, chunk), lambda i, _: (0, i)),
            ),
            scratch_shapes=[
                pltpu.VMEM((1, rows_dev), jnp.int32),
                pltpu.VMEM(loader.shape, jnp.int32),
            ],
        ),
        compiler_params=params(),
        name="index_tables",
    )(self_id, loader)


def permute_kernel(pick_ref, rows_ref, out_ref):
    out_ref[...] = matmul(pick_ref[...], rows_ref[...]).astype(bf16)


def permute(pick, rows):
    rows_dev, width = rows.shape
    chunk = 256
    return pl.pallas_call(
        permute_kernel,
        out_shape=jax.ShapeDtypeStruct((rows_dev, width), bf16),
        grid=(rows_dev // chunk,),
        in_specs=[pl.BlockSpec((chunk, rows_dev), lambda i: (i, 0)), whole(rows.shape)],
        out_specs=pl.BlockSpec((chunk, width), lambda i: (i, 0)),
        compiler_params=params(),
        name="permute",
    )(pick, rows)


def outbound_kernel(capacity, block, picks_ref, to_node_ref, rows_ref, *out_refs):
    for at, out_ref in enumerate(out_refs):
        for slot in range(capacity):
            start = pl.multiple_of(jnp.maximum(picks_ref[at * capacity + slot], 0) * block, block)
            picked = matmul(to_node_ref[pl.ds(start, block), :], rows_ref[...])
            out_ref[slot * block : (slot + 1) * block, :] = picked.astype(bf16)


def outbound_blocks(picks, to_node, rows, shifts, capacity, block):
    width = rows.shape[1]
    shape = (capacity * block, width)
    return pl.pallas_call(
        functools.partial(outbound_kernel, capacity, block),
        out_shape=[jax.ShapeDtypeStruct(shape, bf16)] * shifts,
        grid_spec=pltpu.PrefetchScalarGridSpec(
            num_scalar_prefetch=1,
            grid=(1,),
            in_specs=[whole(to_node.shape), whole(rows.shape)],
            out_specs=[whole(shape)] * shifts,
        ),
        compiler_params=params(),
        name="outbound",
    )(picks, to_node, rows)


def project_kernel(to_node_ref, rows_ref, wq_ref, wk_ref, wv_ref, q_ref, k_ref, v_ref):
    owned = matmul(to_node_ref[...], rows_ref[...]).astype(bf16)
    q_ref[...] = matmul(owned, wq_ref[...]).astype(bf16)
    k_ref[...] = matmul(owned, wk_ref[...]).astype(bf16)
    v_ref[...] = matmul(owned, wv_ref[...]).astype(bf16)


def project(to_node, rows, w_query, w_key, w_value, table_rows):
    rows_dev, width = rows.shape
    chunk = 256
    out_spec = pl.BlockSpec((chunk, width), lambda i: (i, 0))
    table = jax.ShapeDtypeStruct((table_rows, width), bf16)
    return pl.pallas_call(
        project_kernel,
        out_shape=(jax.ShapeDtypeStruct((rows_dev, width), bf16), table, table),
        grid=(rows_dev // chunk,),
        in_specs=[
            pl.BlockSpec((chunk, rows_dev), lambda i: (i, 0)),
            whole(rows.shape),
            whole(w_query.shape),
            whole(w_key.shape),
            whole(w_value.shape),
        ],
        out_specs=(out_spec, out_spec, out_spec),
        compiler_params=params(),
        name="project",
    )(to_node, rows, w_query, w_key, w_value)


def remote_kernel(rows_ref, wk_ref, wv_ref, k_in, v_in, k_ref, v_ref):
    k_ref[...] = matmul(rows_ref[...], wk_ref[...]).astype(bf16)
    v_ref[...] = matmul(rows_ref[...], wv_ref[...]).astype(bf16)


def remote_project(rows, w_key, w_value, k_table, v_table, first_row):
    chunk, width = rows.shape
    at = first_row // chunk
    out_spec = pl.BlockSpec((chunk, width), lambda i: (at, 0))
    any_spec = pl.BlockSpec(memory_space=pl.ANY)
    return pl.pallas_call(
        remote_kernel,
        out_shape=(
            jax.ShapeDtypeStruct(k_table.shape, bf16),
            jax.ShapeDtypeStruct(v_table.shape, bf16),
        ),
        grid=(1,),
        in_specs=[
            whole(rows.shape),
            whole(w_key.shape),
            whole(w_value.shape),
            any_spec,
            any_spec,
        ],
        out_specs=(out_spec, out_spec),
        input_output_aliases={3: 0, 4: 1},
        compiler_params=params(),
        name="remote_project",
    )(rows, w_key, w_value, k_table, v_table)


def block_starts(entries_ref, block, reads):
    at = pl.program_id(0) * reads
    return [pl.multiple_of(entries_ref[at + j] * block, block) for j in range(reads)]


def forward_kernel(
    reads,
    entries_ref,
    q_ref,
    k_ref,
    v_ref,
    gain_ref,
    from_node_ref,
    out_ref,
    mixed_ref,
    stats_ref,
    layer_ref,
):
    block, width = q_ref.shape
    step = pl.program_id(0)
    starts = block_starts(entries_ref, block, reads)
    lanes = iota((block, LANE), 1)
    stats = jnp.zeros((block, LANE), f32)
    for head in range(HEADS):
        cols = slice(head * HEAD_DIM, (head + 1) * HEAD_DIM)
        keys = jnp.concatenate([k_ref[pl.ds(at, block), cols] for at in starts], axis=0)
        vals = jnp.concatenate([v_ref[pl.ds(at, block), cols] for at in starts], axis=0)
        scores = lax.dot_general(q_ref[:, cols], keys, NT, preferred_element_type=f32) * SCALE
        top = jnp.max(scores, axis=1, keepdims=True)
        expo = jnp.exp(scores - top)
        inv = 1.0 / jnp.sum(expo, axis=1, keepdims=True)
        mixed_ref[:, cols] = matmul((expo * inv).astype(bf16), vals)
        stats = jnp.where(lanes == head, top, stats)
        stats = jnp.where(lanes == HEADS + head, inv, stats)
    mixed = mixed_ref[...]
    inv_rms = lax.rsqrt(jnp.mean(mixed * mixed, axis=1, keepdims=True) + 1e-06)
    stats_ref[...] = jnp.where(lanes == 2 * HEADS, inv_rms, stats)
    rows = pl.ds(pl.multiple_of(step * block, block), block)
    layer_ref[rows, :] = (mixed * inv_rms * gain_ref[...]).astype(bf16)

    @pl.when(step == pl.num_programs(0) - 1)
    def _():
        out_ref[...] = matmul(from_node_ref[...], layer_ref[...]).astype(bf16)


def forward(entries, queries, k_table, v_table, gain, from_node, block, reads):
    rows_dev, width = queries.shape
    return pl.pallas_call(
        functools.partial(forward_kernel, reads),
        out_shape=(
            jax.ShapeDtypeStruct((rows_dev, width), bf16),
            jax.ShapeDtypeStruct((rows_dev, width), f32),
            jax.ShapeDtypeStruct((rows_dev, LANE), f32),
        ),
        grid_spec=pltpu.PrefetchScalarGridSpec(
            num_scalar_prefetch=1,
            grid=(rows_dev // block,),
            in_specs=[
                pl.BlockSpec((block, width), lambda i, _: (i, 0)),
                whole(k_table.shape),
                whole(v_table.shape),
                whole(gain.shape),
                whole(from_node.shape),
            ],
            out_specs=(
                whole((rows_dev, width)),
                pl.BlockSpec((block, width), lambda i, _: (i, 0)),
                pl.BlockSpec((block, LANE), lambda i, _: (i, 0)),
            ),
            scratch_shapes=[pltpu.VMEM((rows_dev, width), bf16)],
        ),
        compiler_params=params(),
        name="forward",
    )(entries, queries, k_table, v_table, gain, from_node)


def backward_kernel(
    reads,
    entries_ref,
    to_node_ref,
    cot_ref,
    gain_ref,
    mixed_ref,
    stats_ref,
    q_ref,
    k_ref,
    v_ref,
    gq_ref,
    own_k_ref,
    own_v_ref,
    far_k_ref,
    far_v_ref,
    sum_k_ref,
    sum_v_ref,
):
    block, width = q_ref.shape
    step = pl.program_id(0)
    own = own_k_ref.shape[0]

    @pl.when(step == 0)
    def _():
        sum_k_ref[...] = jnp.zeros_like(sum_k_ref)
        sum_v_ref[...] = jnp.zeros_like(sum_v_ref)

    starts = block_starts(entries_ref, block, reads)
    stats = stats_ref[...]
    turned = stats.T
    inv_rms = stats[:, 2 * HEADS : 2 * HEADS + 1]
    mixed = mixed_ref[...]
    grad_in = matmul(to_node_ref[...], cot_ref[...]) * gain_ref[...]
    inner = jnp.mean(grad_in * mixed, axis=1, keepdims=True)
    grad_mix = (inv_rms * (grad_in - mixed * (inv_rms * inv_rms * inner))).astype(bf16)
    for head in range(HEADS):
        cols = slice(head * HEAD_DIM, (head + 1) * HEAD_DIM)
        keys = jnp.concatenate([k_ref[pl.ds(at, block), cols] for at in starts], axis=0)
        vals = jnp.concatenate([v_ref[pl.ds(at, block), cols] for at in starts], axis=0)
        queries = q_ref[:, cols]
        grads = grad_mix[:, cols]
        scores = lax.dot_general(keys, queries, NT, preferred_element_type=f32) * SCALE
        prob = jnp.exp(scores - turned[head : head + 1]) * turned[HEADS + head : HEADS + head + 1]
        grad_prob = lax.dot_general(vals, grads, NT, preferred_element_type=f32)
        delta = jnp.sum(prob * grad_prob, axis=0, keepdims=True)
        grad_score = (prob * (grad_prob - delta) * SCALE).astype(bf16)
        gq = lax.dot_general(grad_score, keys, TN, preferred_element_type=f32)
        gq_ref[:, cols] = gq.astype(bf16)
        key_term = matmul(grad_score, queries)
        value_term = matmul(prob.astype(bf16), grads)
        for j, at in enumerate(starts):
            part = slice(j * block, (j + 1) * block)
            sum_k_ref[pl.ds(at, block), cols] += key_term[part]
            sum_v_ref[pl.ds(at, block), cols] += value_term[part]

    @pl.when(step == pl.num_programs(0) - 1)
    def _():
        own_k_ref[...] = sum_k_ref[:own, :].astype(bf16)
        own_v_ref[...] = sum_v_ref[:own, :].astype(bf16)
        far_k_ref[...] = sum_k_ref[own:, :].astype(bf16)
        far_v_ref[...] = sum_v_ref[own:, :].astype(bf16)


def backward(
    entries, to_node, cot_rows, gain, mixed, stats, queries, k_table, v_table, block, reads
):
    rows_dev, width = queries.shape
    table_rows = k_table.shape[0]
    own = jax.ShapeDtypeStruct((rows_dev, width), bf16)
    far = jax.ShapeDtypeStruct((table_rows - rows_dev, width), bf16)
    row_spec = pl.BlockSpec((block, width), lambda i, _: (i, 0))
    return pl.pallas_call(
        functools.partial(backward_kernel, reads),
        out_shape=(own, own, own, far, far),
        grid_spec=pltpu.PrefetchScalarGridSpec(
            num_scalar_prefetch=1,
            grid=(rows_dev // block,),
            in_specs=[
                pl.BlockSpec((block, rows_dev), lambda i, _: (i, 0)),
                whole(cot_rows.shape),
                whole(gain.shape),
                row_spec,
                pl.BlockSpec((block, LANE), lambda i, _: (i, 0)),
                row_spec,
                whole(k_table.shape),
                whole(v_table.shape),
            ],
            out_specs=(
                row_spec,
                whole(own.shape),
                whole(own.shape),
                whole(far.shape),
                whole(far.shape),
            ),
            scratch_shapes=[
                pltpu.VMEM((table_rows, width), f32),
                pltpu.VMEM((table_rows, width), f32),
            ],
        ),
        compiler_params=params(),
        name="backward",
    )(entries, to_node, cot_rows, gain, mixed, stats, queries, k_table, v_table)


def far_kernel(k_ref, v_ref, wk_ref, wv_ref, *out_refs):
    chunk = out_refs[0].shape[0]
    for at, out_ref in enumerate(out_refs):
        rows = slice(at * chunk, (at + 1) * chunk)
        total = lax.dot_general(k_ref[rows, :], wk_ref[...], NT, preferred_element_type=f32)
        total += lax.dot_general(v_ref[rows, :], wv_ref[...], NT, preferred_element_type=f32)
        out_ref[...] = total.astype(bf16)


def far_project(far_k, far_v, w_key, w_value, shifts):
    rows, width = far_k.shape
    shape = (rows // shifts, width)
    return pl.pallas_call(
        far_kernel,
        out_shape=[jax.ShapeDtypeStruct(shape, bf16)] * shifts,
        grid=(1,),
        in_specs=[whole(far_k.shape), whole(far_v.shape), whole(w_key.shape), whole(w_value.shape)],
        out_specs=[whole(shape)] * shifts,
        compiler_params=params(),
        name="far_project",
    )(far_k, far_v, w_key, w_value)


def own_kernel(q_ref, k_ref, v_ref, wq_ref, wk_ref, wv_ref, out_ref):
    total = lax.dot_general(q_ref[...], wq_ref[...], NT, preferred_element_type=f32)
    total += lax.dot_general(k_ref[...], wk_ref[...], NT, preferred_element_type=f32)
    total += lax.dot_general(v_ref[...], wv_ref[...], NT, preferred_element_type=f32)
    out_ref[...] = total


def own_project(grad_q, own_k, own_v, w_query, w_key, w_value):
    rows_dev, width = grad_q.shape
    chunk = 256
    spec = pl.BlockSpec((chunk, width), lambda i: (i, 0))
    return pl.pallas_call(
        own_kernel,
        out_shape=jax.ShapeDtypeStruct((rows_dev, width), f32),
        grid=(rows_dev // chunk,),
        in_specs=[spec, spec, spec] + [whole(w_query.shape)] * 3,
        out_specs=spec,
        compiler_params=params(),
        name="own_project",
    )(grad_q, own_k, own_v, w_query, w_key, w_value)


def collect_kernel(capacity, block, picks_ref, own_ref, from_node_ref, *refs):
    returned, (out_ref, total_ref) = refs[:-2], refs[-2:]
    total_ref[...] = own_ref[...]
    for at, ref in enumerate(returned):
        for slot in range(capacity):
            pick = picks_ref[at * capacity + slot]

            @pl.when(pick >= 0)
            def _():
                rows = pl.ds(pl.multiple_of(pick * block, block), block)
                part = ref[slot * block : (slot + 1) * block, :]
                total_ref[rows, :] += part.astype(f32)

    out_ref[...] = matmul(from_node_ref[...], total_ref[...].astype(bf16)).astype(bf16)


def collect(picks, own, from_node, returned, capacity, block):
    rows_dev, width = own.shape
    return pl.pallas_call(
        functools.partial(collect_kernel, capacity, block),
        out_shape=jax.ShapeDtypeStruct((rows_dev, width), bf16),
        grid_spec=pltpu.PrefetchScalarGridSpec(
            num_scalar_prefetch=1,
            grid=(1,),
            in_specs=[whole(own.shape), whole(from_node.shape)]
            + [whole(part.shape) for part in returned],
            out_specs=whole((rows_dev, width)),
            scratch_shapes=[pltpu.VMEM((rows_dev, width), f32)],
        ),
        compiler_params=params(),
        name="collect",
    )(picks, own, from_node, *returned)


def body(
    features, cotangent, loader, w_query, w_key, w_value, norm_gain, send_blocks, tile_lists
):
    row_count = lax.axis_size("row")
    col_count = lax.axis_size("col")
    devices = row_count * col_count
    col = lax.axis_index("col")
    self_index = lax.axis_index("row") * col_count + col
    self_id = self_index.astype(jnp.int32).reshape(1)
    rows_dev, width = features.shape
    per_peer = rows_dev // devices
    block_count = tile_lists.shape[0]
    block = rows_dev // block_count
    capacity = send_blocks.shape[2]
    shifts = col_count - 1
    table_rows = rows_dev + shifts * capacity * block
    reads = 1 + tile_lists.shape[1]
    loader = loader.reshape(devices, rows_dev)
    gain = norm_gain.reshape(1, width)

    def exchange(rows):
        buffer = rows.reshape(devices, per_peer, width)
        out = lax.all_to_all(buffer, ("row", "col"), split_axis=0, concat_axis=0, tiled=True)
        return out.reshape(rows_dev, width)

    send_row = lax.dynamic_index_in_dim(send_blocks, self_index, 0, keepdims=False)
    peers = (col + 1 + jnp.arange(shifts, dtype=jnp.int32)) % col_count
    picks = send_row[peers].reshape(-1)
    source = (tile_lists - block_count) // capacity
    shift = (col - source) % col_count
    moved = block_count + (shift - 1) * capacity + (tile_lists - block_count) % capacity
    entries = jnp.where(tile_lists < block_count, tile_lists, moved)
    entries = jnp.concatenate(
        [jnp.arange(block_count, dtype=jnp.int32)[:, None], entries], axis=1
    ).reshape(-1)

    feature_rows = exchange(send_permute(self_id, loader, features))
    cot_out = send_permute(self_id, loader, cotangent)
    to_node, from_node, to_row = index_tables(self_id, loader, rows_dev)
    cot_rows = exchange(cot_out)

    outgoing = outbound_blocks(picks, to_node, feature_rows, shifts, capacity, block)
    queries, k_table, v_table = project(
        to_node, feature_rows, w_query, w_key, w_value, table_rows
    )
    for at in range(shifts):
        perm = [(c, (c + at + 1) % col_count) for c in range(col_count)]
        arrived = lax.ppermute(outgoing[at], "col", perm)
        first = rows_dev + at * capacity * block
        k_table, v_table = remote_project(arrived, w_key, w_value, k_table, v_table, first)

    layer_rows, mixed, stats = forward(
        entries, queries, k_table, v_table, gain, from_node, block, reads
    )
    layer_back = exchange(layer_rows)
    grad_q, own_k, own_v, far_k, far_v = backward(
        entries, to_node, cot_rows, gain, mixed, stats, queries, k_table, v_table, block, reads
    )
    far = far_project(far_k, far_v, w_key, w_value, shifts)
    returned = []
    for at in range(shifts):
        perm = [(c, (c - at - 1) % col_count) for c in range(col_count)]
        returned.append(lax.ppermute(far[at], "col", perm))
    own = own_project(grad_q, own_k, own_v, w_query, w_key, w_value)
    grad_back = exchange(collect(picks, own, from_node, returned, capacity, block))
    return (permute(to_row, layer_back), permute(to_row, grad_back))


def solution(mesh):
    split = P(("row", "col"), None)
    in_specs = (split, split, P(), P(), P(), P(), P(), P(), split)
    return jax.shard_map(
        body, mesh=mesh, in_specs=in_specs, out_specs=(split, split), check_vma=False
    )
```

```python
import functools
import math

import jax
import jax.numpy as jnp
from jax import lax
from jax.experimental import pallas as pl
from jax.experimental.pallas import tpu as pltpu
from jax.sharding import PartitionSpec as P

HEADS = 8
HEAD_DIM = 128
SCALE = HEAD_DIM ** (-0.5)
LANE = 128
EXPO = SCALE * math.log2(math.e)
MIB = 1024 * 1024
SUBLANES = 8
CHUNK = 64

NT = (((1,), (1,)), ((), ()))
TN = (((0,), (0,)), ((), ()))
bf16 = jnp.bfloat16
f32 = jnp.float32


def hbm(shape, dtype):
    return pltpu.HBM(shape, jnp.dtype(dtype))


def params(mib):
    return pltpu.CompilerParams(dimension_semantics=("arbitrary",), vmem_limit_bytes=mib * MIB)


def whole(shape):
    zeros = (0,) * len(shape)
    return pl.BlockSpec(shape, lambda *_: zeros, pipeline_mode=pl.Buffered(1))


def matmul(left, right):
    return jnp.dot(left, right, preferred_element_type=f32)


def iota(shape, axis):
    return lax.broadcasted_iota(jnp.int32, shape, axis)


def lane_rank(mask):
    rows, count = mask.shape
    before = (iota((LANE, LANE), 0) < iota((LANE, LANE), 1)).astype(f32).astype(bf16)
    carry = jnp.zeros((rows, 1), f32)
    pieces = []
    for at in range(0, count, LANE):
        part = mask[:, at : at + LANE]
        pieces.append(matmul(part.astype(bf16), before) + carry)
        carry = carry + jnp.sum(part, axis=1, keepdims=True)
    return jnp.concatenate(pieces, axis=1)


def send_slots(nodes, devices):
    rows_dev = nodes.shape[1]
    per_peer = rows_dev // devices
    owner = lax.shift_right_logical(nodes, rows_dev.bit_length() - 1)
    owners = iota((devices, rows_dev), 0)
    mask = (owner == owners).astype(f32)
    slot = mask * (lane_rank(mask) + (owners * per_peer).astype(f32))
    return jnp.sum(slot, axis=0, keepdims=True).astype(jnp.int32)


def one_hot(cond):
    return jnp.where(cond, 1.0, 0.0)


def send_kernel(self_ref, loader_ref, rows_ref, out_ref, slot_ref):
    step = pl.program_id(0)
    chunk = out_ref.shape[0]
    rows_dev = rows_ref.shape[0]

    @pl.when(step == 0)
    def _():
        nodes = loader_ref[pl.ds(self_ref[0], 1), :]
        slot_ref[...] = send_slots(nodes, loader_ref.shape[0])

    pick = one_hot(slot_ref[...] == iota((chunk, rows_dev), 0) + step * chunk)
    out_ref[...] = matmul(pick.astype(bf16), rows_ref[...]).astype(bf16)


def send_permute(self_id, loader, rows):
    rows_dev, width = rows.shape
    chunk = 256
    return pl.pallas_call(
        send_kernel,
        out_shape=hbm((rows_dev, width), bf16),
        grid_spec=pltpu.PrefetchScalarGridSpec(
            num_scalar_prefetch=1,
            grid=(rows_dev // chunk,),
            in_specs=[whole(loader.shape), whole(rows.shape)],
            out_specs=pl.BlockSpec((chunk, width), lambda i, _: (i, 0)),
            scratch_shapes=[pltpu.VMEM((1, rows_dev), jnp.int32)],
        ),
        compiler_params=params(10),
        name="send_permute",
    )(self_id, loader, rows)


def index_kernel(self_ref, loader_ref, to_node_ref, from_node_ref, to_row_ref, slot_ref, key_ref):
    step = pl.program_id(0)
    devices, rows_dev = loader_ref.shape
    per_peer = rows_dev // devices
    chunk = from_node_ref.shape[0]
    sources = chunk // per_peer
    me = self_ref[0]

    @pl.when(step == 0)
    def _():
        slot_ref[...] = send_slots(loader_ref[pl.ds(me, 1), :], devices)
        owner = lax.shift_right_logical(loader_ref[...], rows_dev.bit_length() - 1)
        mask = (owner == me).astype(f32)
        rank = lane_rank(mask).astype(jnp.int32)
        key_ref[...] = jnp.where(owner == me, rank, -1)

    pieces = []
    for t in range(sources):
        source = step * sources + t
        key = key_ref[pl.ds(source, 1), :]
        local = loader_ref[pl.ds(source, 1), :] - me * rows_dev
        hit = key == iota((per_peer, rows_dev), 0)
        pieces.append(jnp.sum(jnp.where(hit, local.astype(f32), 0.0), axis=1, keepdims=True))
    arriving = jnp.concatenate(pieces, axis=0).astype(jnp.int32)
    pick = one_hot(arriving == iota((chunk, rows_dev), 1))
    from_node_ref[...] = pick.astype(bf16)
    to_node_ref[...] = pick.T.astype(bf16)
    back = one_hot(slot_ref[...] == iota((chunk, rows_dev), 0) + step * chunk)
    to_row_ref[...] = back.T.astype(bf16)


def index_tables(self_id, loader, rows_dev):
    chunk = LANE
    square = hbm((rows_dev, rows_dev), bf16)
    return pl.pallas_call(
        index_kernel,
        out_shape=(square, square, square),
        grid_spec=pltpu.PrefetchScalarGridSpec(
            num_scalar_prefetch=1,
            grid=(rows_dev // chunk,),
            in_specs=[whole(loader.shape)],
            out_specs=(
                pl.BlockSpec((rows_dev, chunk), lambda i, _: (0, i)),
                pl.BlockSpec((chunk, rows_dev), lambda i, _: (i, 0)),
                pl.BlockSpec((rows_dev, chunk), lambda i, _: (0, i)),
            ),
            scratch_shapes=[
                pltpu.VMEM((1, rows_dev), jnp.int32),
                pltpu.VMEM(loader.shape, jnp.int32),
            ],
        ),
        compiler_params=params(10),
        name="index_tables",
    )(self_id, loader)


def permute_kernel(pick_ref, rows_ref, out_ref):
    out_ref[...] = matmul(pick_ref[...], rows_ref[...]).astype(bf16)


def permute(pick, rows):
    rows_dev, width = rows.shape
    chunk = 256
    return pl.pallas_call(
        permute_kernel,
        out_shape=hbm((rows_dev, width), bf16),
        grid=(rows_dev // chunk,),
        in_specs=[pl.BlockSpec((chunk, rows_dev), lambda i: (i, 0)), whole(rows.shape)],
        out_specs=pl.BlockSpec((chunk, width), lambda i: (i, 0)),
        compiler_params=params(8),
        name="permute",
    )(pick, rows)


def outbound_kernel(capacity, block, picks_ref, to_node_ref, rows_ref, *out_refs):
    for at, out_ref in enumerate(out_refs):
        for slot in range(capacity):
            start = pl.multiple_of(jnp.maximum(picks_ref[at * capacity + slot], 0) * block, block)
            picked = matmul(to_node_ref[pl.ds(start, block), :], rows_ref[...])
            out_ref[slot * block : (slot + 1) * block, :] = picked.astype(bf16)


def outbound_blocks(picks, to_node, rows, shifts, capacity, block):
    width = rows.shape[1]
    shape = (capacity * block, width)
    return pl.pallas_call(
        functools.partial(outbound_kernel, capacity, block),
        out_shape=[hbm(shape, bf16)] * shifts,
        grid_spec=pltpu.PrefetchScalarGridSpec(
            num_scalar_prefetch=1,
            grid=(1,),
            in_specs=[whole(to_node.shape), whole(rows.shape)],
            out_specs=[whole(shape)] * shifts,
        ),
        compiler_params=params(12),
        name="outbound",
    )(picks, to_node, rows)


def project_kernel(to_node_ref, rows_ref, wq_ref, wk_ref, wv_ref, q_ref, k_ref, v_ref):
    owned = matmul(to_node_ref[...], rows_ref[...]).astype(bf16)
    q_ref[...] = matmul(owned, wq_ref[...]).astype(bf16)
    k_ref[...] = matmul(owned, wk_ref[...]).astype(bf16)
    v_ref[...] = matmul(owned, wv_ref[...]).astype(bf16)


def project(to_node, rows, w_query, w_key, w_value, table_rows):
    rows_dev, width = rows.shape
    chunk = 256
    out_spec = pl.BlockSpec((chunk, width), lambda i: (i, 0))
    table = hbm((table_rows, width), bf16)
    return pl.pallas_call(
        project_kernel,
        out_shape=(hbm((rows_dev, width), bf16), table, table),
        grid=(rows_dev // chunk,),
        in_specs=[
            pl.BlockSpec((chunk, rows_dev), lambda i: (i, 0)),
            whole(rows.shape),
            whole(w_query.shape),
            whole(w_key.shape),
            whole(w_value.shape),
        ],
        out_specs=(out_spec, out_spec, out_spec),
        compiler_params=params(20),
        name="project",
    )(to_node, rows, w_query, w_key, w_value)


def remote_kernel(rows_ref, wk_ref, wv_ref, k_in, v_in, k_ref, v_ref):
    k_ref[...] = matmul(rows_ref[...], wk_ref[...]).astype(bf16)
    v_ref[...] = matmul(rows_ref[...], wv_ref[...]).astype(bf16)


def remote_project(rows, w_key, w_value, k_table, v_table, first_row):
    chunk, width = rows.shape
    at = first_row // chunk
    out_spec = pl.BlockSpec((chunk, width), lambda i: (at, 0))
    any_spec = pl.BlockSpec(memory_space=pl.ANY)
    return pl.pallas_call(
        remote_kernel,
        out_shape=(
            hbm(k_table.shape, bf16),
            hbm(v_table.shape, bf16),
        ),
        grid=(1,),
        in_specs=[
            whole(rows.shape),
            whole(w_key.shape),
            whole(w_value.shape),
            any_spec,
            any_spec,
        ],
        out_specs=(out_spec, out_spec),
        input_output_aliases={3: 0, 4: 1},
        compiler_params=params(12),
        name="remote_project",
    )(rows, w_key, w_value, k_table, v_table)


def split_dot(left, right):
    return lax.dot_general(left, right, NT, preferred_element_type=f32)


def fold(rows, op):
    total = rows[:SUBLANES]
    for at in range(SUBLANES, rows.shape[0], SUBLANES):
        total = op(total, rows[at : at + SUBLANES])
    return total


def block_starts(entries_ref, block, reads):
    at = pl.program_id(0) * reads
    return [pl.multiple_of(entries_ref[at + j] * block, block) for j in range(reads)]


def forward_kernel(
    reads,
    entries_ref,
    q_ref,
    k_ref,
    v_ref,
    gain_ref,
    from_node_ref,
    out_ref,
    mixed_ref,
    stats_ref,
    layer_ref,
    score_ref,
    prob_ref,
):
    block, width = q_ref.shape
    step = pl.program_id(0)
    keys = reads * block
    starts = block_starts(entries_ref, block, reads)
    for head in range(HEADS):
        cols = slice(head * HEAD_DIM, (head + 1) * HEAD_DIM)
        for j, at in enumerate(starts):
            part = slice(j * block, (j + 1) * block)
            score_ref[head, part, :] = split_dot(k_ref[pl.ds(at, block), cols], q_ref[:, cols])
    for head in range(HEADS):
        top = fold(score_ref[head, :CHUNK, :], jnp.maximum)
        for at in range(CHUNK, keys, CHUNK):
            top = jnp.maximum(top, fold(score_ref[head, at : at + CHUNK, :], jnp.maximum))
        top = jnp.max(top, axis=0, keepdims=True)
        total = jnp.zeros((SUBLANES, block), f32)
        for at in range(0, keys, CHUNK):
            expo = jnp.exp2((score_ref[head, at : at + CHUNK, :] - top) * EXPO)
            score_ref[head, at : at + CHUNK, :] = expo
            total = total + fold(expo, jnp.add)
        inv = 1.0 / jnp.sum(total, axis=0, keepdims=True)
        for at in range(0, keys, CHUNK):
            part = slice(at, at + CHUNK)
            prob_ref[head, part, :] = (score_ref[head, part, :] * inv).astype(bf16)
        stats_ref[2 * head : 2 * head + 1, :] = top
        stats_ref[2 * head + 1 : 2 * head + 2, :] = inv
    for head in range(HEADS):
        cols = slice(head * HEAD_DIM, (head + 1) * HEAD_DIM)
        vals = jnp.concatenate([v_ref[pl.ds(at, block), cols] for at in starts], axis=0)
        mixed_ref[:, cols] = lax.dot_general(
            prob_ref[head], vals, TN, preferred_element_type=f32
        )
    mixed = mixed_ref[...]
    inv_rms = lax.rsqrt(jnp.mean(mixed * mixed, axis=1, keepdims=True) + 1e-06)
    rows = pl.ds(pl.multiple_of(step * block, block), block)
    layer_ref[rows, :] = (mixed * inv_rms * gain_ref[...]).astype(bf16)

    @pl.when(step == pl.num_programs(0) - 1)
    def _():
        out_ref[...] = matmul(from_node_ref[...], layer_ref[...]).astype(bf16)


def forward(entries, queries, k_table, v_table, gain, from_node, block, reads):
    rows_dev, width = queries.shape
    return pl.pallas_call(
        functools.partial(forward_kernel, reads),
        out_shape=(
            hbm((rows_dev, width), bf16),
            hbm((rows_dev, width), f32),
            hbm((rows_dev // block * 2 * HEADS, block), f32),
        ),
        grid_spec=pltpu.PrefetchScalarGridSpec(
            num_scalar_prefetch=1,
            grid=(rows_dev // block,),
            in_specs=[
                pl.BlockSpec((block, width), lambda i, _: (i, 0)),
                whole(k_table.shape),
                whole(v_table.shape),
                whole(gain.shape),
                whole(from_node.shape),
            ],
            out_specs=(
                whole((rows_dev, width)),
                pl.BlockSpec((block, width), lambda i, _: (i, 0)),
                pl.BlockSpec((2 * HEADS, block), lambda i, _: (i, 0)),
            ),
            scratch_shapes=[
                pltpu.VMEM((rows_dev, width), bf16),
                pltpu.VMEM((HEADS, reads * block, block), f32),
                pltpu.VMEM((HEADS, reads * block, block), bf16),
            ],
        ),
        compiler_params=params(32),
        name="forward",
    )(entries, queries, k_table, v_table, gain, from_node)


def backward_kernel(
    reads,
    entries_ref,
    to_node_ref,
    cot_ref,
    gain_ref,
    mixed_ref,
    stats_ref,
    q_ref,
    k_ref,
    v_ref,
    gq_ref,
    own_k_ref,
    own_v_ref,
    far_k_ref,
    far_v_ref,
    sum_k_ref,
    sum_v_ref,
    prob_ref,
    grad_prob_ref,
    prob_half_ref,
    grad_score_ref,
    grad_mix_ref,
):
    block, width = q_ref.shape
    step = pl.program_id(0)
    own = own_k_ref.shape[0]
    keys = reads * block

    @pl.when(step == 0)
    def _():
        sum_k_ref[...] = jnp.zeros_like(sum_k_ref)
        sum_v_ref[...] = jnp.zeros_like(sum_v_ref)

    starts = block_starts(entries_ref, block, reads)
    mixed = mixed_ref[...]
    inv_rms = lax.rsqrt(jnp.mean(mixed * mixed, axis=1, keepdims=True) + 1e-06)
    grad_in = matmul(to_node_ref[...], cot_ref[...]) * gain_ref[...]
    inner = jnp.mean(grad_in * mixed, axis=1, keepdims=True)
    grad_mix = inv_rms * (grad_in - mixed * (inv_rms * inv_rms * inner))
    grad_mix_ref[...] = grad_mix.astype(bf16)
    for head in range(HEADS):
        cols = slice(head * HEAD_DIM, (head + 1) * HEAD_DIM)
        for j, at in enumerate(starts):
            part = slice(j * block, (j + 1) * block)
            rows = pl.ds(at, block)
            prob_ref[head, part, :] = split_dot(k_ref[rows, cols], q_ref[:, cols])
            grad_prob_ref[head, part, :] = split_dot(v_ref[rows, cols], grad_mix_ref[:, cols])
    for head in range(HEADS):
        top = stats_ref[2 * head : 2 * head + 1, :]
        inv = stats_ref[2 * head + 1 : 2 * head + 2, :]
        total = jnp.zeros((SUBLANES, block), f32)
        for at in range(0, keys, CHUNK):
            part = slice(at, at + CHUNK)
            prob = jnp.exp2((prob_ref[head, part, :] - top) * EXPO) * inv
            prob_ref[head, part, :] = prob
            prob_half_ref[head, part, :] = prob.astype(bf16)
            total = total + fold(prob * grad_prob_ref[head, part, :], jnp.add)
        delta = jnp.sum(total, axis=0, keepdims=True)
        for at in range(0, keys, CHUNK):
            part = slice(at, at + CHUNK)
            centred = (grad_prob_ref[head, part, :] - delta) * SCALE
            grad_score_ref[head, part, :] = (prob_ref[head, part, :] * centred).astype(bf16)
    for head in range(HEADS):
        cols = slice(head * HEAD_DIM, (head + 1) * HEAD_DIM)
        key_rows = jnp.concatenate([k_ref[pl.ds(at, block), cols] for at in starts], axis=0)
        gq = lax.dot_general(grad_score_ref[head], key_rows, TN, preferred_element_type=f32)
        gq_ref[:, cols] = gq.astype(bf16)
        for j, at in enumerate(starts):
            part = slice(j * block, (j + 1) * block)
            rows = pl.ds(at, block)
            sum_k_ref[rows, cols] += matmul(grad_score_ref[head, part, :], q_ref[:, cols])
            sum_v_ref[rows, cols] += matmul(prob_half_ref[head, part, :], grad_mix_ref[:, cols])

    @pl.when(step == pl.num_programs(0) - 1)
    def _():
        own_k_ref[...] = sum_k_ref[:own, :].astype(bf16)
        own_v_ref[...] = sum_v_ref[:own, :].astype(bf16)
        far_k_ref[...] = sum_k_ref[own:, :].astype(bf16)
        far_v_ref[...] = sum_v_ref[own:, :].astype(bf16)


def backward(
    entries, to_node, cot_rows, gain, mixed, stats, queries, k_table, v_table, block, reads
):
    rows_dev, width = queries.shape
    table_rows = k_table.shape[0]
    own = hbm((rows_dev, width), bf16)
    far = hbm((table_rows - rows_dev, width), bf16)
    row_spec = pl.BlockSpec((block, width), lambda i, _: (i, 0))
    return pl.pallas_call(
        functools.partial(backward_kernel, reads),
        out_shape=(own, own, own, far, far),
        grid_spec=pltpu.PrefetchScalarGridSpec(
            num_scalar_prefetch=1,
            grid=(rows_dev // block,),
            in_specs=[
                pl.BlockSpec((block, rows_dev), lambda i, _: (i, 0)),
                whole(cot_rows.shape),
                whole(gain.shape),
                row_spec,
                pl.BlockSpec((2 * HEADS, block), lambda i, _: (i, 0)),
                row_spec,
                whole(k_table.shape),
                whole(v_table.shape),
            ],
            out_specs=(
                row_spec,
                whole(own.shape),
                whole(own.shape),
                whole(far.shape),
                whole(far.shape),
            ),
            scratch_shapes=[
                pltpu.VMEM((table_rows, width), f32),
                pltpu.VMEM((table_rows, width), f32),
                pltpu.VMEM((HEADS, reads * block, block), f32),
                pltpu.VMEM((HEADS, reads * block, block), f32),
                pltpu.VMEM((HEADS, reads * block, block), bf16),
                pltpu.VMEM((HEADS, reads * block, block), bf16),
                pltpu.VMEM((block, width), bf16),
            ],
        ),
        compiler_params=params(60),
        name="backward",
    )(entries, to_node, cot_rows, gain, mixed, stats, queries, k_table, v_table)


def far_kernel(k_ref, v_ref, wk_ref, wv_ref, *out_refs):
    chunk = out_refs[0].shape[0]
    for at, out_ref in enumerate(out_refs):
        rows = slice(at * chunk, (at + 1) * chunk)
        total = lax.dot_general(k_ref[rows, :], wk_ref[...], NT, preferred_element_type=f32)
        total += lax.dot_general(v_ref[rows, :], wv_ref[...], NT, preferred_element_type=f32)
        out_ref[...] = total.astype(bf16)


def far_project(far_k, far_v, w_key, w_value, shifts):
    rows, width = far_k.shape
    shape = (rows // shifts, width)
    return pl.pallas_call(
        far_kernel,
        out_shape=[hbm(shape, bf16)] * shifts,
        grid=(1,),
        in_specs=[whole(far_k.shape), whole(far_v.shape), whole(w_key.shape), whole(w_value.shape)],
        out_specs=[whole(shape)] * shifts,
        compiler_params=params(14),
        name="far_project",
    )(far_k, far_v, w_key, w_value)


def own_kernel(q_ref, k_ref, v_ref, wq_ref, wk_ref, wv_ref, out_ref):
    total = lax.dot_general(q_ref[...], wq_ref[...], NT, preferred_element_type=f32)
    total += lax.dot_general(k_ref[...], wk_ref[...], NT, preferred_element_type=f32)
    total += lax.dot_general(v_ref[...], wv_ref[...], NT, preferred_element_type=f32)
    out_ref[...] = total


def own_project(grad_q, own_k, own_v, w_query, w_key, w_value):
    rows_dev, width = grad_q.shape
    chunk = 256
    spec = pl.BlockSpec((chunk, width), lambda i: (i, 0))
    return pl.pallas_call(
        own_kernel,
        out_shape=hbm((rows_dev, width), f32),
        grid=(rows_dev // chunk,),
        in_specs=[spec, spec, spec] + [whole(w_query.shape)] * 3,
        out_specs=spec,
        compiler_params=params(16),
        name="own_project",
    )(grad_q, own_k, own_v, w_query, w_key, w_value)


def collect_kernel(capacity, block, picks_ref, own_ref, from_node_ref, *refs):
    returned, (out_ref, total_ref) = refs[:-2], refs[-2:]
    total_ref[...] = own_ref[...]
    for at, ref in enumerate(returned):
        for slot in range(capacity):
            pick = picks_ref[at * capacity + slot]

            @pl.when(pick >= 0)
            def _():
                rows = pl.ds(pl.multiple_of(pick * block, block), block)
                part = ref[slot * block : (slot + 1) * block, :]
                total_ref[rows, :] += part.astype(f32)

    out_ref[...] = matmul(from_node_ref[...], total_ref[...].astype(bf16)).astype(bf16)


def collect(picks, own, from_node, returned, capacity, block):
    rows_dev, width = own.shape
    return pl.pallas_call(
        functools.partial(collect_kernel, capacity, block),
        out_shape=hbm((rows_dev, width), bf16),
        grid_spec=pltpu.PrefetchScalarGridSpec(
            num_scalar_prefetch=1,
            grid=(1,),
            in_specs=[whole(own.shape), whole(from_node.shape)]
            + [whole(part.shape) for part in returned],
            out_specs=whole((rows_dev, width)),
            scratch_shapes=[pltpu.VMEM((rows_dev, width), f32)],
        ),
        compiler_params=params(20),
        name="collect",
    )(picks, own, from_node, *returned)


def body(
    features, cotangent, loader, w_query, w_key, w_value, norm_gain, send_blocks, tile_lists
):
    row_count = lax.axis_size("row")
    col_count = lax.axis_size("col")
    devices = row_count * col_count
    col = lax.axis_index("col")
    self_index = lax.axis_index("row") * col_count + col
    self_id = self_index.astype(jnp.int32).reshape(1)
    rows_dev, width = features.shape
    per_peer = rows_dev // devices
    block_count = tile_lists.shape[0]
    block = rows_dev // block_count
    capacity = send_blocks.shape[2]
    shifts = col_count - 1
    table_rows = rows_dev + shifts * capacity * block
    reads = 1 + tile_lists.shape[1]
    loader = loader.reshape(devices, rows_dev)
    gain = norm_gain.reshape(1, width)

    def exchange(rows):
        buffer = rows.reshape(devices, per_peer, width)
        out = lax.all_to_all(buffer, ("row", "col"), split_axis=0, concat_axis=0, tiled=True)
        return out.reshape(rows_dev, width)

    send_row = lax.dynamic_index_in_dim(send_blocks, self_index, 0, keepdims=False)
    peers = (col + 1 + jnp.arange(shifts, dtype=jnp.int32)) % col_count
    picks = send_row[peers].reshape(-1)
    source = (tile_lists - block_count) // capacity
    shift = (col - source) % col_count
    moved = block_count + (shift - 1) * capacity + (tile_lists - block_count) % capacity
    entries = jnp.where(tile_lists < block_count, tile_lists, moved)
    entries = jnp.concatenate(
        [jnp.arange(block_count, dtype=jnp.int32)[:, None], entries], axis=1
    ).reshape(-1)

    feature_rows = exchange(send_permute(self_id, loader, features))
    cot_out = send_permute(self_id, loader, cotangent)
    to_node, from_node, to_row = index_tables(self_id, loader, rows_dev)
    feature_rows, cot_out, to_node, from_node, to_row, picks, entries = lax.optimization_barrier(
        (feature_rows, cot_out, to_node, from_node, to_row, picks, entries)
    )
    outgoing = outbound_blocks(picks, to_node, feature_rows, shifts, capacity, block)
    cot_out, outgoing = lax.optimization_barrier((cot_out, outgoing))
    cot_rows = exchange(cot_out)

    queries, k_table, v_table = project(
        to_node, feature_rows, w_query, w_key, w_value, table_rows
    )
    for at in range(shifts):
        perm = [(c, (c + at + 1) % col_count) for c in range(col_count)]
        arrived = lax.ppermute(outgoing[at], "col", perm)
        first = rows_dev + at * capacity * block
        k_table, v_table = remote_project(arrived, w_key, w_value, k_table, v_table, first)

    layer_rows, mixed, stats = forward(
        entries, queries, k_table, v_table, gain, from_node, block, reads
    )
    layer_back = exchange(layer_rows)
    grad_q, own_k, own_v, far_k, far_v = backward(
        entries, to_node, cot_rows, gain, mixed, stats, queries, k_table, v_table, block, reads
    )
    far = far_project(far_k, far_v, w_key, w_value, shifts)
    returned = []
    for at in range(shifts):
        perm = [(c, (c - at - 1) % col_count) for c in range(col_count)]
        returned.append(lax.ppermute(far[at], "col", perm))
    own = own_project(grad_q, own_k, own_v, w_query, w_key, w_value)
    grad_back = exchange(collect(picks, own, from_node, returned, capacity, block))
    return (permute(to_row, layer_back), permute(to_row, grad_back))


def solution(mesh):
    split = P(("row", "col"), None)
    in_specs = (split, split, P(), P(), P(), P(), P(), P(), split)
    return jax.shard_map(
        body, mesh=mesh, in_specs=in_specs, out_specs=(split, split), check_vma=False
    )
```

```python
import functools
import math

import jax
import jax.numpy as jnp
from jax import lax
from jax.experimental import pallas as pl
from jax.experimental.pallas import tpu as pltpu
from jax.sharding import PartitionSpec as P

HEADS = 8
HEAD_DIM = 128
SCALE = HEAD_DIM ** (-0.5)
LANE = 128
EXPO = SCALE * math.log2(math.e)
MIB = 1024 * 1024
SUBLANES = 8
CHUNK = 64

NT = (((1,), (1,)), ((), ()))
TN = (((0,), (0,)), ((), ()))
bf16 = jnp.bfloat16
f32 = jnp.float32


def hbm(shape, dtype):
    return pltpu.HBM(shape, jnp.dtype(dtype))


def pin(value):
    return pltpu.with_memory_space_constraint(value, pltpu.HBM)


def params(mib):
    return pltpu.CompilerParams(dimension_semantics=("arbitrary",), vmem_limit_bytes=mib * MIB)


def whole(shape):
    zeros = (0,) * len(shape)
    return pl.BlockSpec(shape, lambda *_: zeros, pipeline_mode=pl.Buffered(1))


def matmul(left, right):
    return jnp.dot(left, right, preferred_element_type=f32)


def iota(shape, axis):
    return lax.broadcasted_iota(jnp.int32, shape, axis)


def lane_rank(mask):
    rows, count = mask.shape
    before = (iota((LANE, LANE), 0) < iota((LANE, LANE), 1)).astype(f32).astype(bf16)
    carry = jnp.zeros((rows, 1), f32)
    pieces = []
    for at in range(0, count, LANE):
        part = mask[:, at : at + LANE]
        pieces.append(matmul(part.astype(bf16), before) + carry)
        carry = carry + jnp.sum(part, axis=1, keepdims=True)
    return jnp.concatenate(pieces, axis=1)


def send_slots(nodes, devices):
    rows_dev = nodes.shape[1]
    per_peer = rows_dev // devices
    owner = lax.shift_right_logical(nodes, rows_dev.bit_length() - 1)
    owners = iota((devices, rows_dev), 0)
    mask = (owner == owners).astype(f32)
    slot = mask * (lane_rank(mask) + (owners * per_peer).astype(f32))
    return jnp.sum(slot, axis=0, keepdims=True).astype(jnp.int32)


def one_hot(cond):
    return jnp.where(cond, 1.0, 0.0)


def send_kernel(self_ref, loader_ref, rows_ref, *refs):
    out_refs, slot_ref = refs[:-1], refs[-1]
    step = pl.program_id(0)
    chunk, piece = out_refs[0].shape
    rows_dev = rows_ref.shape[0]

    @pl.when(step == 0)
    def _():
        nodes = loader_ref[pl.ds(self_ref[0], 1), :]
        slot_ref[...] = send_slots(nodes, loader_ref.shape[0])

    pick = one_hot(slot_ref[...] == iota((chunk, rows_dev), 0) + step * chunk)
    moved = matmul(pick.astype(bf16), rows_ref[...]).astype(bf16)
    for at, out_ref in enumerate(out_refs):
        out_ref[...] = moved[:, at * piece : (at + 1) * piece]


def send_permute(self_id, loader, rows, pieces):
    rows_dev, width = rows.shape
    chunk = 256
    piece = width // pieces
    return pl.pallas_call(
        send_kernel,
        out_shape=[hbm((rows_dev, piece), bf16)] * pieces,
        grid_spec=pltpu.PrefetchScalarGridSpec(
            num_scalar_prefetch=1,
            grid=(rows_dev // chunk,),
            in_specs=[whole(loader.shape), whole(rows.shape)],
            out_specs=[pl.BlockSpec((chunk, piece), lambda i, _: (i, 0))] * pieces,
            scratch_shapes=[pltpu.VMEM((1, rows_dev), jnp.int32)],
        ),
        compiler_params=params(10),
        name="send_permute",
    )(self_id, loader, pin(rows))


def index_kernel(self_ref, loader_ref, to_node_ref, from_node_ref, to_row_ref, slot_ref, key_ref):
    step = pl.program_id(0)
    devices, rows_dev = loader_ref.shape
    per_peer = rows_dev // devices
    chunk = from_node_ref.shape[0]
    sources = chunk // per_peer
    me = self_ref[0]

    @pl.when(step == 0)
    def _():
        slot_ref[...] = send_slots(loader_ref[pl.ds(me, 1), :], devices)
        owner = lax.shift_right_logical(loader_ref[...], rows_dev.bit_length() - 1)
        mask = (owner == me).astype(f32)
        rank = lane_rank(mask).astype(jnp.int32)
        key_ref[...] = jnp.where(owner == me, rank, -1)

    pieces = []
    for t in range(sources):
        source = step * sources + t
        key = key_ref[pl.ds(source, 1), :]
        local = loader_ref[pl.ds(source, 1), :] - me * rows_dev
        hit = key == iota((per_peer, rows_dev), 0)
        pieces.append(jnp.sum(jnp.where(hit, local.astype(f32), 0.0), axis=1, keepdims=True))
    arriving = jnp.concatenate(pieces, axis=0).astype(jnp.int32)
    pick = one_hot(arriving == iota((chunk, rows_dev), 1))
    from_node_ref[...] = pick.astype(bf16)
    to_node_ref[...] = pick.T.astype(bf16)
    back = one_hot(slot_ref[...] == iota((chunk, rows_dev), 0) + step * chunk)
    to_row_ref[...] = back.T.astype(bf16)


def index_tables(self_id, loader, rows_dev):
    chunk = LANE
    square = hbm((rows_dev, rows_dev), bf16)
    return pl.pallas_call(
        index_kernel,
        out_shape=(square, square, square),
        grid_spec=pltpu.PrefetchScalarGridSpec(
            num_scalar_prefetch=1,
            grid=(rows_dev // chunk,),
            in_specs=[whole(loader.shape)],
            out_specs=(
                pl.BlockSpec((rows_dev, chunk), lambda i, _: (0, i)),
                pl.BlockSpec((chunk, rows_dev), lambda i, _: (i, 0)),
                pl.BlockSpec((rows_dev, chunk), lambda i, _: (0, i)),
            ),
            scratch_shapes=[
                pltpu.VMEM((1, rows_dev), jnp.int32),
                pltpu.VMEM(loader.shape, jnp.int32),
            ],
        ),
        compiler_params=params(10),
        name="index_tables",
    )(self_id, loader)


def permute_kernel(pick_ref, rows_ref, *refs):
    refs[-1][...] = matmul(pick_ref[...], rows_ref[...]).astype(bf16)


def permute(pick, pieces):
    rows_dev, piece = pieces[0].shape
    chunk = 256
    out = []
    for at, rows in enumerate(pieces):
        out = [
            pl.pallas_call(
                permute_kernel,
                out_shape=hbm((rows_dev, piece * len(pieces)), bf16),
                grid=(rows_dev // chunk,),
                in_specs=[pl.BlockSpec((chunk, rows_dev), lambda i: (i, 0)), whole(rows.shape)]
                + [pl.BlockSpec(memory_space=pl.ANY)] * len(out),
                out_specs=pl.BlockSpec((chunk, piece), lambda i, at=at: (i, at)),
                input_output_aliases={2: 0} if out else {},
                compiler_params=params(8),
                name="permute",
            )(pin(pick), pin(rows), *out)
        ]
    return out[0]


def outbound_kernel(capacity, block, picks_ref, to_node_ref, rows_ref, *out_refs):
    for at, out_ref in enumerate(out_refs):
        for slot in range(capacity):
            start = pl.multiple_of(jnp.maximum(picks_ref[at * capacity + slot], 0) * block, block)
            picked = matmul(to_node_ref[pl.ds(start, block), :], rows_ref[...])
            out_ref[slot * block : (slot + 1) * block, :] = picked.astype(bf16)


def outbound_blocks(picks, to_node, rows, shifts, capacity, block):
    width = rows.shape[1]
    shape = (capacity * block, width)
    return pl.pallas_call(
        functools.partial(outbound_kernel, capacity, block),
        out_shape=[hbm(shape, bf16)] * shifts,
        grid_spec=pltpu.PrefetchScalarGridSpec(
            num_scalar_prefetch=1,
            grid=(1,),
            in_specs=[whole(to_node.shape), whole(rows.shape)],
            out_specs=[whole(shape)] * shifts,
        ),
        compiler_params=params(12),
        name="outbound",
    )(picks, pin(to_node), pin(rows))


def project_kernel(to_node_ref, wq_ref, wk_ref, wv_ref, *refs):
    row_refs, (q_ref, k_ref, v_ref) = refs[:-3], refs[-3:]
    owned = [matmul(to_node_ref[...], ref[...]).astype(bf16) for ref in row_refs]
    owned = jnp.concatenate(owned, axis=1)
    q_ref[...] = matmul(owned, wq_ref[...]).astype(bf16)
    k_ref[...] = matmul(owned, wk_ref[...]).astype(bf16)
    v_ref[...] = matmul(owned, wv_ref[...]).astype(bf16)


def project(to_node, rows, w_query, w_key, w_value, table_rows):
    rows_dev = to_node.shape[0]
    width = w_query.shape[1]
    chunk = 256
    out_spec = pl.BlockSpec((chunk, width), lambda i: (i, 0))
    table = hbm((table_rows, width), bf16)
    return pl.pallas_call(
        project_kernel,
        out_shape=(hbm((rows_dev, width), bf16), table, table),
        grid=(rows_dev // chunk,),
        in_specs=[
            pl.BlockSpec((chunk, rows_dev), lambda i: (i, 0)),
            whole(w_query.shape),
            whole(w_key.shape),
            whole(w_value.shape),
        ]
        + [whole(piece.shape) for piece in rows],
        out_specs=(out_spec, out_spec, out_spec),
        compiler_params=params(20),
        name="project",
    )(pin(to_node), w_query, w_key, w_value, *map(pin, rows))


def remote_kernel(wk_ref, wv_ref, k_in, v_in, *refs):
    row_refs, (k_ref, v_ref) = refs[:-2], refs[-2:]
    rows = jnp.concatenate([ref[...] for ref in row_refs], axis=1)
    k_ref[...] = matmul(rows, wk_ref[...]).astype(bf16)
    v_ref[...] = matmul(rows, wv_ref[...]).astype(bf16)


def remote_project(rows, w_key, w_value, k_table, v_table, first_row):
    chunk = rows[0].shape[0]
    width = w_key.shape[1]
    at = first_row // chunk
    out_spec = pl.BlockSpec((chunk, width), lambda i: (at, 0))
    any_spec = pl.BlockSpec(memory_space=pl.ANY)
    table = hbm(k_table.shape, bf16)
    return pl.pallas_call(
        remote_kernel,
        out_shape=(table, table),
        grid=(1,),
        in_specs=[whole(w_key.shape), whole(w_value.shape), any_spec, any_spec]
        + [whole(piece.shape) for piece in rows],
        out_specs=(out_spec, out_spec),
        input_output_aliases={2: 0, 3: 1},
        compiler_params=params(12),
        name="remote_project",
    )(w_key, w_value, k_table, v_table, *rows)


def split_dot(left, right):
    return lax.dot_general(left, right, NT, preferred_element_type=f32)


def fold(rows, op):
    total = rows[:SUBLANES]
    for at in range(SUBLANES, rows.shape[0], SUBLANES):
        total = op(total, rows[at : at + SUBLANES])
    return total


def entry_specs(block, width, reads):
    return [
        pl.BlockSpec((block, width), lambda i, entries, j=j: (entries[i * reads + j], 0))
        for j in range(reads)
    ]


def entry_args(table, reads):
    return [pin(table)] * reads


def forward_kernel(
    reads,
    entries_ref,
    q_ref,
    gain_ref,
    from_node_ref,
    *refs,
):
    k_refs, v_refs = refs[:reads], refs[reads : 2 * reads]
    out_ref, mixed_ref, stats_ref, layer_ref, score_ref, prob_ref = refs[2 * reads :]
    block, width = q_ref.shape
    step = pl.program_id(0)
    keys = reads * block
    for head in range(HEADS):
        cols = slice(head * HEAD_DIM, (head + 1) * HEAD_DIM)
        for j, k_ref in enumerate(k_refs):
            part = slice(j * block, (j + 1) * block)
            score_ref[head, part, :] = split_dot(k_ref[:, cols], q_ref[:, cols])
    for head in range(HEADS):
        top = fold(score_ref[head, :CHUNK, :], jnp.maximum)
        for at in range(CHUNK, keys, CHUNK):
            top = jnp.maximum(top, fold(score_ref[head, at : at + CHUNK, :], jnp.maximum))
        top = jnp.max(top, axis=0, keepdims=True)
        total = jnp.zeros((SUBLANES, block), f32)
        for at in range(0, keys, CHUNK):
            expo = jnp.exp2((score_ref[head, at : at + CHUNK, :] - top) * EXPO)
            score_ref[head, at : at + CHUNK, :] = expo
            total = total + fold(expo, jnp.add)
        inv = 1.0 / jnp.sum(total, axis=0, keepdims=True)
        for at in range(0, keys, CHUNK):
            part = slice(at, at + CHUNK)
            prob_ref[head, part, :] = (score_ref[head, part, :] * inv).astype(bf16)
        stats_ref[2 * head : 2 * head + 1, :] = top
        stats_ref[2 * head + 1 : 2 * head + 2, :] = inv
    for head in range(HEADS):
        cols = slice(head * HEAD_DIM, (head + 1) * HEAD_DIM)
        vals = jnp.concatenate([ref[:, cols] for ref in v_refs], axis=0)
        mixed_ref[:, cols] = lax.dot_general(
            prob_ref[head], vals, TN, preferred_element_type=f32
        )
    mixed = mixed_ref[...]
    inv_rms = lax.rsqrt(jnp.mean(mixed * mixed, axis=1, keepdims=True) + 1e-06)
    rows = pl.ds(pl.multiple_of(step * block, block), block)
    layer_ref[rows, :] = (mixed * inv_rms * gain_ref[...]).astype(bf16)

    @pl.when(step == pl.num_programs(0) - 1)
    def _():
        out_ref[...] = matmul(from_node_ref[...], layer_ref[...]).astype(bf16)


def forward(entries, queries, k_table, v_table, gain, from_node, block, reads):
    rows_dev, width = queries.shape
    return pl.pallas_call(
        functools.partial(forward_kernel, reads),
        out_shape=(
            hbm((rows_dev, width), bf16),
            hbm((rows_dev, width), f32),
            hbm((rows_dev // block * 2 * HEADS, block), f32),
        ),
        grid_spec=pltpu.PrefetchScalarGridSpec(
            num_scalar_prefetch=1,
            grid=(rows_dev // block,),
            in_specs=[
                pl.BlockSpec((block, width), lambda i, _: (i, 0)),
                whole(gain.shape),
                whole(from_node.shape),
            ]
            + entry_specs(block, width, reads) * 2,
            out_specs=(
                whole((rows_dev, width)),
                pl.BlockSpec((block, width), lambda i, _: (i, 0)),
                pl.BlockSpec((2 * HEADS, block), lambda i, _: (i, 0)),
            ),
            scratch_shapes=[
                pltpu.VMEM((rows_dev, width), bf16),
                pltpu.VMEM((HEADS, reads * block, block), f32),
                pltpu.VMEM((HEADS, reads * block, block), bf16),
            ],
        ),
        compiler_params=params(32),
        name="forward",
    )(
        entries,
        pin(queries),
        gain,
        from_node,
        *entry_args(k_table, reads),
        *entry_args(v_table, reads),
    )


def backward_kernel(
    reads,
    entries_ref,
    to_node_ref,
    cot_ref,
    gain_ref,
    mixed_ref,
    stats_ref,
    q_ref,
    *refs,
):
    k_refs, v_refs = refs[:reads], refs[reads : 2 * reads]
    gq_ref, own_k_ref, own_v_ref, far_k_ref, far_v_ref = refs[2 * reads : 2 * reads + 5]
    sum_k_ref, sum_v_ref, prob_ref, grad_prob_ref = refs[2 * reads + 5 : 2 * reads + 9]
    prob_half_ref, grad_score_ref, grad_mix_ref = refs[2 * reads + 9 :]
    block, width = q_ref.shape
    step = pl.program_id(0)
    own = own_k_ref.shape[0]
    keys = reads * block

    @pl.when(step == 0)
    def _():
        sum_k_ref[...] = jnp.zeros_like(sum_k_ref)
        sum_v_ref[...] = jnp.zeros_like(sum_v_ref)

    entries = [entries_ref[step * reads + j] * block for j in range(reads)]
    starts = [pl.multiple_of(at, block) for at in entries]
    mixed = mixed_ref[...]
    inv_rms = lax.rsqrt(jnp.mean(mixed * mixed, axis=1, keepdims=True) + 1e-06)
    grad_in = matmul(to_node_ref[...], cot_ref[...]) * gain_ref[...]
    inner = jnp.mean(grad_in * mixed, axis=1, keepdims=True)
    grad_mix = inv_rms * (grad_in - mixed * (inv_rms * inv_rms * inner))
    grad_mix_ref[...] = grad_mix.astype(bf16)
    for head in range(HEADS):
        cols = slice(head * HEAD_DIM, (head + 1) * HEAD_DIM)
        for j, (k_ref, v_ref) in enumerate(zip(k_refs, v_refs)):
            part = slice(j * block, (j + 1) * block)
            prob_ref[head, part, :] = split_dot(k_ref[:, cols], q_ref[:, cols])
            grad_prob_ref[head, part, :] = split_dot(v_ref[:, cols], grad_mix_ref[:, cols])
    for head in range(HEADS):
        top = stats_ref[2 * head : 2 * head + 1, :]
        inv = stats_ref[2 * head + 1 : 2 * head + 2, :]
        total = jnp.zeros((SUBLANES, block), f32)
        for at in range(0, keys, CHUNK):
            part = slice(at, at + CHUNK)
            prob = jnp.exp2((prob_ref[head, part, :] - top) * EXPO) * inv
            prob_ref[head, part, :] = prob
            prob_half_ref[head, part, :] = prob.astype(bf16)
            total = total + fold(prob * grad_prob_ref[head, part, :], jnp.add)
        delta = jnp.sum(total, axis=0, keepdims=True)
        for at in range(0, keys, CHUNK):
            part = slice(at, at + CHUNK)
            centred = (grad_prob_ref[head, part, :] - delta) * SCALE
            grad_score_ref[head, part, :] = (prob_ref[head, part, :] * centred).astype(bf16)
    for head in range(HEADS):
        cols = slice(head * HEAD_DIM, (head + 1) * HEAD_DIM)
        key_rows = jnp.concatenate([ref[:, cols] for ref in k_refs], axis=0)
        gq = lax.dot_general(grad_score_ref[head], key_rows, TN, preferred_element_type=f32)
        gq_ref[:, cols] = gq.astype(bf16)
        for j, at in enumerate(starts):
            part = slice(j * block, (j + 1) * block)
            rows = pl.ds(at, block)
            sum_k_ref[rows, cols] += matmul(grad_score_ref[head, part, :], q_ref[:, cols])
            sum_v_ref[rows, cols] += matmul(prob_half_ref[head, part, :], grad_mix_ref[:, cols])

    @pl.when(step == pl.num_programs(0) - 1)
    def _():
        own_k_ref[...] = sum_k_ref[:own, :].astype(bf16)
        own_v_ref[...] = sum_v_ref[:own, :].astype(bf16)
        far_k_ref[...] = sum_k_ref[own:, :].astype(bf16)
        far_v_ref[...] = sum_v_ref[own:, :].astype(bf16)


def backward(
    entries, to_node, cot_rows, gain, mixed, stats, queries, k_table, v_table, block, reads
):
    rows_dev, width = queries.shape
    table_rows = k_table.shape[0]
    own = hbm((rows_dev, width), bf16)
    far = hbm((table_rows - rows_dev, width), bf16)
    grant = min(60, 16 + 12 * table_rows * width // MIB)
    row_spec = pl.BlockSpec((block, width), lambda i, _: (i, 0))
    return pl.pallas_call(
        functools.partial(backward_kernel, reads),
        out_shape=(own, own, own, far, far),
        grid_spec=pltpu.PrefetchScalarGridSpec(
            num_scalar_prefetch=1,
            grid=(rows_dev // block,),
            in_specs=[
                pl.BlockSpec((block, rows_dev), lambda i, _: (i, 0)),
                whole(cot_rows.shape),
                whole(gain.shape),
                row_spec,
                pl.BlockSpec((2 * HEADS, block), lambda i, _: (i, 0)),
                row_spec,
            ]
            + entry_specs(block, width, reads) * 2,
            out_specs=(
                row_spec,
                whole(own.shape),
                whole(own.shape),
                whole(far.shape),
                whole(far.shape),
            ),
            scratch_shapes=[
                pltpu.VMEM((table_rows, width), f32),
                pltpu.VMEM((table_rows, width), f32),
                pltpu.VMEM((HEADS, reads * block, block), f32),
                pltpu.VMEM((HEADS, reads * block, block), f32),
                pltpu.VMEM((HEADS, reads * block, block), bf16),
                pltpu.VMEM((HEADS, reads * block, block), bf16),
                pltpu.VMEM((block, width), bf16),
            ],
        ),
        compiler_params=params(grant),
        name="backward",
    )(
        entries,
        pin(to_node),
        pin(cot_rows),
        gain,
        pin(mixed),
        pin(stats),
        pin(queries),
        *entry_args(k_table, reads),
        *entry_args(v_table, reads),
    )


def far_kernel(k_ref, v_ref, wk_ref, wv_ref, *out_refs):
    chunk = out_refs[0].shape[0]
    for at, out_ref in enumerate(out_refs):
        rows = slice(at * chunk, (at + 1) * chunk)
        total = lax.dot_general(k_ref[rows, :], wk_ref[...], NT, preferred_element_type=f32)
        total += lax.dot_general(v_ref[rows, :], wv_ref[...], NT, preferred_element_type=f32)
        out_ref[...] = total.astype(bf16)


def far_project(far_k, far_v, w_key, w_value, shifts, piece, at):
    rows, width = far_k.shape
    shape = (rows // shifts, piece)
    w_spec = pl.BlockSpec((piece, width), lambda i: (at, 0), pipeline_mode=pl.Buffered(1))
    return pl.pallas_call(
        far_kernel,
        out_shape=[hbm(shape, bf16)] * shifts,
        grid=(1,),
        in_specs=[whole(far_k.shape), whole(far_v.shape), w_spec, w_spec],
        out_specs=[whole(shape)] * shifts,
        compiler_params=params(14),
        name="far_project",
    )(pin(far_k), pin(far_v), w_key, w_value)


def own_kernel(q_ref, k_ref, v_ref, wq_ref, wk_ref, wv_ref, out_ref):
    total = lax.dot_general(q_ref[...], wq_ref[...], NT, preferred_element_type=f32)
    total += lax.dot_general(k_ref[...], wk_ref[...], NT, preferred_element_type=f32)
    total += lax.dot_general(v_ref[...], wv_ref[...], NT, preferred_element_type=f32)
    out_ref[...] = total


def own_project(grad_q, own_k, own_v, w_query, w_key, w_value, piece, at):
    rows_dev, width = grad_q.shape
    chunk = 256
    spec = pl.BlockSpec((chunk, width), lambda i: (i, 0))
    w_spec = pl.BlockSpec((piece, width), lambda i: (at, 0), pipeline_mode=pl.Buffered(1))
    return pl.pallas_call(
        own_kernel,
        out_shape=jax.ShapeDtypeStruct((rows_dev, piece), f32),
        grid=(rows_dev // chunk,),
        in_specs=[spec, spec, spec, w_spec, w_spec, w_spec],
        out_specs=pl.BlockSpec((chunk, piece), lambda i: (i, 0)),
        compiler_params=params(16),
        name="own_project",
    )(pin(grad_q), pin(own_k), pin(own_v), w_query, w_key, w_value)


def collect_kernel(capacity, block, picks_ref, own_ref, from_node_ref, *refs):
    returned, (out_ref, total_ref) = refs[:-2], refs[-2:]
    total_ref[...] = own_ref[...]
    for at, ref in enumerate(returned):
        for slot in range(capacity):
            pick = picks_ref[at * capacity + slot]

            @pl.when(pick >= 0)
            def _():
                rows = pl.ds(pl.multiple_of(pick * block, block), block)
                part = ref[slot * block : (slot + 1) * block, :]
                total_ref[rows, :] += part.astype(f32)

    out_ref[...] = matmul(from_node_ref[...], total_ref[...].astype(bf16)).astype(bf16)


def collect(picks, own, from_node, returned, capacity, block):
    rows_dev, width = own.shape
    return pl.pallas_call(
        functools.partial(collect_kernel, capacity, block),
        out_shape=hbm((rows_dev, width), bf16),
        grid_spec=pltpu.PrefetchScalarGridSpec(
            num_scalar_prefetch=1,
            grid=(1,),
            in_specs=[whole(own.shape), whole(from_node.shape)]
            + [whole(part.shape) for part in returned],
            out_specs=whole((rows_dev, width)),
            scratch_shapes=[pltpu.VMEM((rows_dev, width), f32)],
        ),
        compiler_params=params(20),
        name="collect",
    )(picks, own, from_node, *returned)


def body(
    features, cotangent, loader, w_query, w_key, w_value, norm_gain, send_blocks, tile_lists
):
    row_count = lax.axis_size("row")
    col_count = lax.axis_size("col")
    devices = row_count * col_count
    col = lax.axis_index("col")
    self_index = lax.axis_index("row") * col_count + col
    self_id = self_index.astype(jnp.int32).reshape(1)
    rows_dev, width = features.shape
    per_peer = rows_dev // devices
    block_count = tile_lists.shape[0]
    block = rows_dev // block_count
    capacity = send_blocks.shape[2]
    shifts = col_count - 1
    table_rows = rows_dev + shifts * capacity * block
    reads = 1 + tile_lists.shape[1]
    loader = loader.reshape(devices, rows_dev)
    gain = norm_gain.reshape(1, width)

    pieces = 2
    piece = width // pieces

    def exchange(rows):
        buffer = rows.reshape(devices, per_peer, rows.shape[1])
        out = lax.all_to_all(buffer, ("row", "col"), split_axis=0, concat_axis=0, tiled=True)
        return out.reshape(rows.shape)

    send_row = lax.dynamic_index_in_dim(send_blocks, self_index, 0, keepdims=False)
    peers = (col + 1 + jnp.arange(shifts, dtype=jnp.int32)) % col_count
    picks = send_row[peers].reshape(-1)
    source = (tile_lists - block_count) // capacity
    shift = (col - source) % col_count
    moved = block_count + (shift - 1) * capacity + (tile_lists - block_count) % capacity
    entries = jnp.where(tile_lists < block_count, tile_lists, moved)
    entries = jnp.concatenate(
        [jnp.arange(block_count, dtype=jnp.int32)[:, None], entries], axis=1
    ).reshape(-1)

    first, *others = send_permute(self_id, loader, features, pieces)
    rows = exchange(first)
    to_node, from_node, to_row = index_tables(self_id, loader, rows_dev)
    rows, to_node, from_node, to_row, picks, entries, others = lax.optimization_barrier(
        (rows, to_node, from_node, to_row, picks, entries, others)
    )
    def forward_rows(outgoing):
        moved = []
        for at in range(shifts):
            perm = [(c, (c + at + 1) % col_count) for c in range(col_count)]
            moved.append(lax.ppermute(outgoing[at], "col", perm))
        return moved

    feature_rows = [rows]
    outgoing = outbound_blocks(picks, to_node, rows, shifts, capacity, block)
    arrived = [forward_rows(outgoing)]
    (cot_out,) = send_permute(self_id, loader, cotangent, 1)
    for other in others:
        rows = exchange(other)
        rows, cot_out, arrived = lax.optimization_barrier((rows, cot_out, arrived))
        feature_rows.append(rows)
        outgoing = outbound_blocks(picks, to_node, rows, shifts, capacity, block)
        cot_out, outgoing = lax.optimization_barrier((cot_out, outgoing))
        arrived.append(forward_rows(outgoing))
    cot_rows = exchange(cot_out)

    queries, k_table, v_table = project(
        to_node, feature_rows, w_query, w_key, w_value, table_rows
    )
    for at in range(shifts):
        parts = [moved[at] for moved in arrived]
        start = rows_dev + at * capacity * block
        k_table, v_table = remote_project(parts, w_key, w_value, k_table, v_table, start)

    layer_rows, mixed, stats = forward(
        entries, queries, k_table, v_table, gain, from_node, block, reads
    )
    layer_back = exchange(layer_rows)
    grad_q, own_k, own_v, far_k, far_v = backward(
        entries, to_node, cot_rows, gain, mixed, stats, queries, k_table, v_table, block, reads
    )
    returned = []
    far_all = [
        far_project(far_k, far_v, w_key, w_value, shifts, piece, part) for part in range(pieces)
    ]
    grad_q, far_all[1:] = lax.optimization_barrier((grad_q, far_all[1:]))
    for far in far_all:
        moved = []
        for at in range(shifts):
            perm = [(c, (c - at - 1) % col_count) for c in range(col_count)]
            moved.append(lax.ppermute(far[at], "col", perm))
        returned.append(moved)
    grad_back = []
    for part in range(pieces):
        own = own_project(grad_q, own_k, own_v, w_query, w_key, w_value, piece, part)
        grad_back.append(
            exchange(collect(picks, own, from_node, returned[part], capacity, block))
        )
    return (permute(to_row, [layer_back]), permute(to_row, grad_back))


def solution(mesh):
    split = P(("row", "col"), None)
    in_specs = (split, split, P(), P(), P(), P(), P(), P(), split)
    return jax.shard_map(
        body, mesh=mesh, in_specs=in_specs, out_specs=(split, split), check_vma=False
    )
```

```python
import functools
import math

import jax
import jax.numpy as jnp
from jax import lax
from jax.experimental import pallas as pl
from jax.experimental.pallas import tpu as pltpu
from jax.sharding import PartitionSpec as P

HEADS = 8
HEAD_DIM = 128
SCALE = HEAD_DIM ** (-0.5)
LANE = 128
EXPO = SCALE * math.log2(math.e)
MIB = 1024 * 1024
SUBLANES = 8
CHUNK = 64
UNIT = 256
LIGHT = pl.CostEstimate(flops=0, transcendentals=0, bytes_accessed=0)

NT = (((1,), (1,)), ((), ()))
TN = (((0,), (0,)), ((), ()))
bf16 = jnp.bfloat16
f32 = jnp.float32


def hbm(shape, dtype):
    return pltpu.HBM(shape, jnp.dtype(dtype))


def pin(value):
    return pltpu.with_memory_space_constraint(value, pltpu.HBM)


def params(mib, axes=1):
    return pltpu.CompilerParams(
        dimension_semantics=("arbitrary",) * axes, vmem_limit_bytes=mib * MIB
    )


def whole(shape):
    zeros = (0,) * len(shape)
    return pl.BlockSpec(shape, lambda *_: zeros, pipeline_mode=pl.Buffered(1))


def matmul(left, right):
    return jnp.dot(left, right, preferred_element_type=f32)


def iota(shape, axis):
    return lax.broadcasted_iota(jnp.int32, shape, axis)


def lane_rank(mask):
    rows, count = mask.shape
    before = (iota((LANE, LANE), 0) < iota((LANE, LANE), 1)).astype(f32).astype(bf16)
    carry = jnp.zeros((rows, 1), f32)
    pieces = []
    for at in range(0, count, LANE):
        part = mask[:, at : at + LANE]
        pieces.append(matmul(part.astype(bf16), before) + carry)
        carry = carry + jnp.sum(part, axis=1, keepdims=True)
    return jnp.concatenate(pieces, axis=1)


def send_slots(nodes, devices):
    rows_dev = nodes.shape[1]
    per_peer = rows_dev // devices
    owner = lax.shift_right_logical(nodes, rows_dev.bit_length() - 1)
    owners = iota((devices, rows_dev), 0)
    mask = (owner == owners).astype(f32)
    slot = mask * (lane_rank(mask) + (owners * per_peer).astype(f32))
    return jnp.sum(slot, axis=0, keepdims=True).astype(jnp.int32)


def one_hot(cond):
    return jnp.where(cond, 1.0, 0.0)


def send_kernel(self_ref, loader_ref, rows_ref, out_ref, slot_ref):
    step = pl.program_id(0)
    chunk = out_ref.shape[0]
    rows_dev = rows_ref.shape[0]

    @pl.when(step == 0)
    def _():
        nodes = loader_ref[pl.ds(self_ref[0], 1), :]
        slot_ref[...] = send_slots(nodes, loader_ref.shape[0])

    pick = one_hot(slot_ref[...] == iota((chunk, rows_dev), 0) + step * chunk)
    out_ref[...] = matmul(pick.astype(bf16), rows_ref[...]).astype(bf16)


def send_permute(self_id, loader, rows, pieces, at):
    rows_dev, width = rows.shape
    chunk = 256
    piece = width // pieces
    return pl.pallas_call(
        send_kernel,
        out_shape=hbm((rows_dev, piece), bf16),
        grid_spec=pltpu.PrefetchScalarGridSpec(
            num_scalar_prefetch=1,
            grid=(rows_dev // chunk,),
            in_specs=[
                whole(loader.shape),
                pl.BlockSpec(
                    (rows_dev, piece), lambda i, _: (0, at), pipeline_mode=pl.Buffered(1)
                ),
            ],
            out_specs=pl.BlockSpec((chunk, piece), lambda i, _: (i, 0)),
            scratch_shapes=[pltpu.VMEM((1, rows_dev), jnp.int32)],
        ),
        compiler_params=params(10),
        name="send_permute",
    )(self_id, loader, pin(rows))


def index_kernel(self_ref, loader_ref, to_node_ref, from_node_ref, to_row_ref, slot_ref, key_ref):
    step = pl.program_id(0)
    devices, rows_dev = loader_ref.shape
    per_peer = rows_dev // devices
    chunk = from_node_ref.shape[0]
    sources = chunk // per_peer
    me = self_ref[0]

    @pl.when(step == 0)
    def _():
        slot_ref[...] = send_slots(loader_ref[pl.ds(me, 1), :], devices)
        owner = lax.shift_right_logical(loader_ref[...], rows_dev.bit_length() - 1)
        mask = (owner == me).astype(f32)
        rank = lane_rank(mask).astype(jnp.int32)
        key_ref[...] = jnp.where(owner == me, rank, -1)

    pieces = []
    for t in range(sources):
        source = step * sources + t
        key = key_ref[pl.ds(source, 1), :]
        local = loader_ref[pl.ds(source, 1), :] - me * rows_dev
        hit = key == iota((per_peer, rows_dev), 0)
        pieces.append(jnp.sum(jnp.where(hit, local.astype(f32), 0.0), axis=1, keepdims=True))
    arriving = jnp.concatenate(pieces, axis=0).astype(jnp.int32)
    pick = one_hot(arriving == iota((chunk, rows_dev), 1))
    from_node_ref[...] = pick.astype(bf16)
    to_node_ref[...] = pick.T.astype(bf16)
    back = one_hot(slot_ref[...] == iota((chunk, rows_dev), 0) + step * chunk)
    to_row_ref[...] = back.T.astype(bf16)


def index_tables(self_id, loader, rows_dev):
    chunk = LANE
    square = hbm((rows_dev, rows_dev), bf16)
    return pl.pallas_call(
        index_kernel,
        out_shape=(square, square, square),
        grid_spec=pltpu.PrefetchScalarGridSpec(
            num_scalar_prefetch=1,
            grid=(rows_dev // chunk,),
            in_specs=[whole(loader.shape)],
            out_specs=(
                pl.BlockSpec((rows_dev, chunk), lambda i, _: (0, i)),
                pl.BlockSpec((chunk, rows_dev), lambda i, _: (i, 0)),
                pl.BlockSpec((rows_dev, chunk), lambda i, _: (0, i)),
            ),
            scratch_shapes=[
                pltpu.VMEM((1, rows_dev), jnp.int32),
                pltpu.VMEM(loader.shape, jnp.int32),
            ],
        ),
        compiler_params=params(10),
        name="index_tables",
    )(self_id, loader)


def permute_kernel(pick_ref, rows_ref, *refs):
    out_ref = refs[-1]
    chunk = out_ref.shape[0]
    at = pl.multiple_of(pl.program_id(1) * chunk, chunk)
    out_ref[...] = matmul(pick_ref[pl.ds(at, chunk), :], rows_ref[...]).astype(bf16)


def permute(pick, pieces):
    rows_dev = pick.shape[0]
    width = sum(rows.shape[1] for rows in pieces)
    chunk = 512
    out, low = [], 0
    for rows in pieces:
        first = low // UNIT
        out = [
            pl.pallas_call(
                permute_kernel,
                out_shape=hbm((rows_dev, width), bf16),
                grid=(rows.shape[1] // UNIT, rows_dev // chunk),
                in_specs=[
                    whole(pick.shape),
                    pl.BlockSpec((rows_dev, UNIT), lambda j, i: (0, j)),
                ]
                + [pl.BlockSpec(memory_space=pl.ANY)] * len(out),
                out_specs=pl.BlockSpec((chunk, UNIT), lambda j, i, first=first: (i, first + j)),
                input_output_aliases={2: 0} if out else {},
                compiler_params=params(10, 2),
                name="permute",
            )(pick, pin(rows), *out)
        ]
        low += rows.shape[1]
    return out[0]


def outbound_kernel(capacity, block, picks_ref, to_node_ref, rows_ref, *out_refs):
    for at, out_ref in enumerate(out_refs):
        for slot in range(capacity):
            start = pl.multiple_of(jnp.maximum(picks_ref[at * capacity + slot], 0) * block, block)
            picked = matmul(to_node_ref[pl.ds(start, block), :], rows_ref[...])
            out_ref[slot * block : (slot + 1) * block, :] = picked.astype(bf16)


def outbound_blocks(picks, to_node, rows, shifts, capacity, block):
    width = rows.shape[1]
    shape = (capacity * block, width)
    return pl.pallas_call(
        functools.partial(outbound_kernel, capacity, block),
        out_shape=[hbm(shape, bf16)] * shifts,
        grid_spec=pltpu.PrefetchScalarGridSpec(
            num_scalar_prefetch=1,
            grid=(1,),
            in_specs=[whole(to_node.shape), whole(rows.shape)],
            out_specs=[whole(shape)] * shifts,
        ),
        compiler_params=params(12),
        name="outbound",
    )(picks, pin(to_node), pin(rows))


def project_kernel(to_node_ref, wq_ref, wk_ref, wv_ref, *refs):
    row_refs, (q_ref, k_ref, v_ref) = refs[:-3], refs[-3:]
    owned = [matmul(to_node_ref[...], ref[...]).astype(bf16) for ref in row_refs]
    owned = jnp.concatenate(owned, axis=1)
    q_ref[...] = matmul(owned, wq_ref[...]).astype(bf16)
    k_ref[...] = matmul(owned, wk_ref[...]).astype(bf16)
    v_ref[...] = matmul(owned, wv_ref[...]).astype(bf16)


def project(to_node, rows, w_query, w_key, w_value, table_rows):
    rows_dev = to_node.shape[0]
    width = w_query.shape[1]
    chunk = 256
    out_spec = pl.BlockSpec((chunk, width), lambda i: (i, 0))
    table = hbm((table_rows, width), bf16)
    return pl.pallas_call(
        project_kernel,
        out_shape=(hbm((rows_dev, width), bf16), table, table),
        grid=(rows_dev // chunk,),
        in_specs=[
            pl.BlockSpec((chunk, rows_dev), lambda i: (i, 0)),
            whole(w_query.shape),
            whole(w_key.shape),
            whole(w_value.shape),
        ]
        + [whole(piece.shape) for piece in rows],
        out_specs=(out_spec, out_spec, out_spec),
        compiler_params=params(20),
        name="project",
    )(pin(to_node), w_query, w_key, w_value, *map(pin, rows))


def remote_kernel(wk_ref, wv_ref, k_in, v_in, *refs):
    row_refs, (k_ref, v_ref) = refs[:-2], refs[-2:]
    rows = jnp.concatenate([ref[...] for ref in row_refs], axis=1)
    k_ref[...] = matmul(rows, wk_ref[...]).astype(bf16)
    v_ref[...] = matmul(rows, wv_ref[...]).astype(bf16)


def remote_project(rows, w_key, w_value, k_table, v_table, first_row):
    chunk = rows[0].shape[0]
    width = w_key.shape[1]
    at = first_row // chunk
    out_spec = pl.BlockSpec((chunk, width), lambda i: (at, 0))
    any_spec = pl.BlockSpec(memory_space=pl.ANY)
    table = hbm(k_table.shape, bf16)
    return pl.pallas_call(
        remote_kernel,
        out_shape=(table, table),
        grid=(1,),
        in_specs=[whole(w_key.shape), whole(w_value.shape), any_spec, any_spec]
        + [whole(piece.shape) for piece in rows],
        out_specs=(out_spec, out_spec),
        input_output_aliases={2: 0, 3: 1},
        compiler_params=params(12),
        name="remote_project",
    )(w_key, w_value, k_table, v_table, *rows)


def split_dot(left, right):
    return lax.dot_general(left, right, NT, preferred_element_type=f32)


def fold(rows, op):
    total = rows[:SUBLANES]
    for at in range(SUBLANES, rows.shape[0], SUBLANES):
        total = op(total, rows[at : at + SUBLANES])
    return total


def entry_specs(block, width, reads):
    return [
        pl.BlockSpec((block, width), lambda i, entries, j=j: (entries[i * reads + j], 0))
        for j in range(reads)
    ]


def entry_args(table, reads):
    return [pin(table)] * reads


def forward_kernel(
    reads,
    entries_ref,
    q_ref,
    gain_ref,
    from_node_ref,
    *refs,
):
    k_refs, v_refs = refs[:reads], refs[reads : 2 * reads]
    out_ref, mixed_ref, stats_ref, layer_ref, score_ref, prob_ref = refs[2 * reads :]
    block, width = q_ref.shape
    step = pl.program_id(0)
    keys = reads * block
    for head in range(HEADS):
        cols = slice(head * HEAD_DIM, (head + 1) * HEAD_DIM)
        key_rows = jnp.concatenate([ref[:, cols] for ref in k_refs], axis=0)
        score_ref[head] = split_dot(key_rows, q_ref[:, cols])
    for head in range(HEADS):
        top = fold(score_ref[head, :CHUNK, :], jnp.maximum)
        for at in range(CHUNK, keys, CHUNK):
            top = jnp.maximum(top, fold(score_ref[head, at : at + CHUNK, :], jnp.maximum))
        top = jnp.max(top, axis=0, keepdims=True)
        total = jnp.zeros((SUBLANES, block), f32)
        for at in range(0, keys, CHUNK):
            expo = jnp.exp2((score_ref[head, at : at + CHUNK, :] - top) * EXPO)
            score_ref[head, at : at + CHUNK, :] = expo
            total = total + fold(expo, jnp.add)
        inv = 1.0 / jnp.sum(total, axis=0, keepdims=True)
        for at in range(0, keys, CHUNK):
            part = slice(at, at + CHUNK)
            prob_ref[head, part, :] = (score_ref[head, part, :] * inv).astype(bf16)
        stats_ref[2 * head : 2 * head + 1, :] = top
        stats_ref[2 * head + 1 : 2 * head + 2, :] = inv
    for head in range(HEADS):
        cols = slice(head * HEAD_DIM, (head + 1) * HEAD_DIM)
        vals = jnp.concatenate([ref[:, cols] for ref in v_refs], axis=0)
        mixed_ref[:, cols] = lax.dot_general(
            prob_ref[head], vals, TN, preferred_element_type=f32
        )
    mixed = mixed_ref[...]
    inv_rms = lax.rsqrt(jnp.mean(mixed * mixed, axis=1, keepdims=True) + 1e-06)
    rows = pl.ds(pl.multiple_of(step * block, block), block)
    layer_ref[rows, :] = (mixed * inv_rms * gain_ref[...]).astype(bf16)

    @pl.when(step == pl.num_programs(0) - 1)
    def _():
        out_ref[...] = matmul(from_node_ref[...], layer_ref[...]).astype(bf16)


def forward(entries, queries, k_table, v_table, gain, from_node, block, reads):
    rows_dev, width = queries.shape
    return pl.pallas_call(
        functools.partial(forward_kernel, reads),
        out_shape=(
            hbm((rows_dev, width), bf16),
            hbm((rows_dev, width), f32),
            hbm((rows_dev // block * 2 * HEADS, block), f32),
        ),
        grid_spec=pltpu.PrefetchScalarGridSpec(
            num_scalar_prefetch=1,
            grid=(rows_dev // block,),
            in_specs=[
                pl.BlockSpec((block, width), lambda i, _: (i, 0)),
                whole(gain.shape),
                whole(from_node.shape),
            ]
            + entry_specs(block, width, reads) * 2,
            out_specs=(
                whole((rows_dev, width)),
                pl.BlockSpec((block, width), lambda i, _: (i, 0)),
                pl.BlockSpec((2 * HEADS, block), lambda i, _: (i, 0)),
            ),
            scratch_shapes=[
                pltpu.VMEM((rows_dev, width), bf16),
                pltpu.VMEM((HEADS, reads * block, block), f32),
                pltpu.VMEM((HEADS, reads * block, block), bf16),
            ],
        ),
        compiler_params=params(32),
        name="forward",
    )(
        entries,
        pin(queries),
        gain,
        from_node,
        *entry_args(k_table, reads),
        *entry_args(v_table, reads),
    )


def backward_kernel(
    reads,
    shifts,
    entries_ref,
    to_node_ref,
    cot_ref,
    gain_ref,
    mixed_ref,
    stats_ref,
    q_ref,
    *refs,
):
    k_refs, v_refs = refs[:reads], refs[reads : 2 * reads]
    wk_hbm, wv_hbm, gq_ref, own_k_hbm, own_v_hbm = refs[2 * reads : 2 * reads + 5]
    far_refs = refs[2 * reads + 5 : -14]
    sum_k_ref, sum_v_ref, prob_ref, grad_prob_ref, prob_half_ref = refs[-14:-9]
    grad_score_ref, grad_mix_ref, own_k_ref, own_v_ref, wk_ref, wv_ref = refs[-9:-3]
    w_sem, own_k_sem, own_v_sem = refs[-3:]
    block, width = q_ref.shape
    step = pl.program_id(0)
    own = own_k_ref.shape[0]
    keys = reads * block
    load_wk = pltpu.make_async_copy(wk_hbm, wk_ref, w_sem.at[0])
    load_wv = pltpu.make_async_copy(wv_hbm, wv_ref, w_sem.at[1])
    save_k = pltpu.make_async_copy(own_k_ref, own_k_hbm, own_k_sem)
    save_v = pltpu.make_async_copy(own_v_ref, own_v_hbm, own_v_sem)

    @pl.when(step == 0)
    def _():
        sum_k_ref[...] = jnp.zeros_like(sum_k_ref)
        sum_v_ref[...] = jnp.zeros_like(sum_v_ref)
        load_wk.start()
        load_wv.start()

    entries = [entries_ref[step * reads + j] * block for j in range(reads)]
    starts = [pl.multiple_of(at, block) for at in entries]
    mixed = mixed_ref[...]
    inv_rms = lax.rsqrt(jnp.mean(mixed * mixed, axis=1, keepdims=True) + 1e-06)
    grad_in = matmul(to_node_ref[...], cot_ref[...]) * gain_ref[...]
    inner = jnp.mean(grad_in * mixed, axis=1, keepdims=True)
    grad_mix = inv_rms * (grad_in - mixed * (inv_rms * inv_rms * inner))
    grad_mix_ref[...] = grad_mix.astype(bf16)
    for head in range(HEADS):
        cols = slice(head * HEAD_DIM, (head + 1) * HEAD_DIM)
        key_rows = jnp.concatenate([ref[:, cols] for ref in k_refs], axis=0)
        val_rows = jnp.concatenate([ref[:, cols] for ref in v_refs], axis=0)
        prob_ref[head] = split_dot(key_rows, q_ref[:, cols])
        grad_prob_ref[head] = split_dot(val_rows, grad_mix_ref[:, cols])
    for head in range(HEADS):
        top = stats_ref[2 * head : 2 * head + 1, :]
        inv = stats_ref[2 * head + 1 : 2 * head + 2, :]
        total = jnp.zeros((SUBLANES, block), f32)
        for at in range(0, keys, CHUNK):
            part = slice(at, at + CHUNK)
            prob = jnp.exp2((prob_ref[head, part, :] - top) * EXPO) * inv
            prob_ref[head, part, :] = prob
            prob_half_ref[head, part, :] = prob.astype(bf16)
            total = total + fold(prob * grad_prob_ref[head, part, :], jnp.add)
        delta = jnp.sum(total, axis=0, keepdims=True)
        for at in range(0, keys, CHUNK):
            part = slice(at, at + CHUNK)
            centred = (grad_prob_ref[head, part, :] - delta) * SCALE
            grad_score_ref[head, part, :] = (prob_ref[head, part, :] * centred).astype(bf16)
    for head in range(HEADS):
        cols = slice(head * HEAD_DIM, (head + 1) * HEAD_DIM)
        key_rows = jnp.concatenate([ref[:, cols] for ref in k_refs], axis=0)
        gq = lax.dot_general(grad_score_ref[head], key_rows, TN, preferred_element_type=f32)
        gq_ref[:, cols] = gq.astype(bf16)
        key_term = matmul(grad_score_ref[head], q_ref[:, cols])
        value_term = matmul(prob_half_ref[head], grad_mix_ref[:, cols])
        for j, at in enumerate(starts):
            part = slice(j * block, (j + 1) * block)
            rows = pl.ds(at, block)
            sum_k_ref[rows, cols] += key_term[part]
            sum_v_ref[rows, cols] += value_term[part]

    @pl.when(step == pl.num_programs(0) - 1)
    def _():
        own_k_ref[...] = sum_k_ref[:own, :].astype(bf16)
        save_k.start()
        own_v_ref[...] = sum_v_ref[:own, :].astype(bf16)
        save_v.start()
        load_wk.wait()
        load_wv.wait()
        low = 0
        for piece in range(0, len(far_refs), shifts):
            chunk, wide = far_refs[piece].shape
            outs = slice(low, low + wide)
            for at in range(shifts):
                rows = slice(own + at * chunk, own + (at + 1) * chunk)
                total = split_dot(sum_k_ref[rows, :].astype(bf16), wk_ref[outs, :])
                total += split_dot(sum_v_ref[rows, :].astype(bf16), wv_ref[outs, :])
                far_refs[piece + at][...] = total.astype(bf16)
            low += wide
        save_k.wait()
        save_v.wait()


def backward(
    entries,
    to_node,
    cot_rows,
    gain,
    mixed,
    stats,
    queries,
    k_table,
    v_table,
    w_key,
    w_value,
    block,
    reads,
    shifts,
    splits,
):
    rows_dev, width = queries.shape
    table_rows = k_table.shape[0]
    own = hbm((rows_dev, width), bf16)
    far = [((table_rows - rows_dev) // shifts, wide) for wide in splits for _ in range(shifts)]
    grant = min(60, 24 + 10 * table_rows * width // MIB)
    row_spec = pl.BlockSpec((block, width), lambda i, _: (i, 0))
    any_spec = pl.BlockSpec(memory_space=pl.ANY)
    out = pl.pallas_call(
        functools.partial(backward_kernel, reads, shifts),
        out_shape=[own, own, own] + [hbm(shape, bf16) for shape in far],
        grid_spec=pltpu.PrefetchScalarGridSpec(
            num_scalar_prefetch=1,
            grid=(rows_dev // block,),
            in_specs=[
                pl.BlockSpec((block, rows_dev), lambda i, _: (i, 0)),
                whole(cot_rows.shape),
                whole(gain.shape),
                row_spec,
                pl.BlockSpec((2 * HEADS, block), lambda i, _: (i, 0)),
                row_spec,
            ]
            + entry_specs(block, width, reads) * 2
            + [any_spec, any_spec],
            out_specs=[row_spec, any_spec, any_spec] + [whole(shape) for shape in far],
            scratch_shapes=[
                pltpu.VMEM((table_rows, width), f32),
                pltpu.VMEM((table_rows, width), f32),
                pltpu.VMEM((HEADS, reads * block, block), f32),
                pltpu.VMEM((HEADS, reads * block, block), f32),
                pltpu.VMEM((HEADS, reads * block, block), bf16),
                pltpu.VMEM((HEADS, reads * block, block), bf16),
                pltpu.VMEM((block, width), bf16),
                pltpu.VMEM((rows_dev, width), bf16),
                pltpu.VMEM((rows_dev, width), bf16),
                pltpu.VMEM(w_key.shape, bf16),
                pltpu.VMEM(w_value.shape, bf16),
                pltpu.SemaphoreType.DMA((2,)),
                pltpu.SemaphoreType.DMA,
                pltpu.SemaphoreType.DMA,
            ],
        ),
        compiler_params=params(grant),
        name="backward",
    )(
        entries,
        pin(to_node),
        cot_rows,
        gain,
        pin(mixed),
        pin(stats),
        pin(queries),
        *entry_args(k_table, reads),
        *entry_args(v_table, reads),
        pin(w_key),
        pin(w_value),
    )
    pieces = [out[at : at + shifts] for at in range(3, len(out), shifts)]
    return out[0], out[1], out[2], pieces


def own_kernel(q_ref, k_ref, v_ref, wq_ref, wk_ref, wv_ref, *out_refs):
    total = split_dot(q_ref[...], wq_ref[...])
    total += split_dot(k_ref[...], wk_ref[...])
    total += split_dot(v_ref[...], wv_ref[...])
    low = 0
    for out_ref in out_refs:
        wide = out_ref.shape[1]
        out_ref[...] = total[:, low : low + wide]
        low += wide


def own_project(grad_q, own_k, own_v, w_query, w_key, w_value, splits):
    rows_dev, width = grad_q.shape
    chunk = 256
    spec = pl.BlockSpec((chunk, width), lambda i: (i, 0))
    return pl.pallas_call(
        own_kernel,
        out_shape=[jax.ShapeDtypeStruct((rows_dev, wide), f32) for wide in splits],
        grid=(rows_dev // chunk,),
        in_specs=[spec, spec, spec] + [whole(w_query.shape)] * 3,
        out_specs=[pl.BlockSpec((chunk, wide), lambda i: (i, 0)) for wide in splits],
        compiler_params=params(20),
        cost_estimate=LIGHT,
        name="own_project",
    )(pin(grad_q), pin(own_k), pin(own_v), w_query, w_key, w_value)


def collect_kernel(capacity, block, picks_ref, own_ref, from_node_ref, *refs):
    returned, (out_ref, total_ref) = refs[:-2], refs[-2:]
    total_ref[...] = own_ref[...]
    for at, ref in enumerate(returned):
        for slot in range(capacity):
            pick = picks_ref[at * capacity + slot]

            @pl.when(pick >= 0)
            def _():
                rows = pl.ds(pl.multiple_of(pick * block, block), block)
                part = ref[slot * block : (slot + 1) * block, :]
                total_ref[rows, :] += part.astype(f32)

    out_ref[...] = matmul(from_node_ref[...], total_ref[...].astype(bf16)).astype(bf16)


def collect(picks, own, from_node, returned, capacity, block):
    rows_dev, width = own.shape
    return pl.pallas_call(
        functools.partial(collect_kernel, capacity, block),
        out_shape=hbm((rows_dev, width), bf16),
        grid_spec=pltpu.PrefetchScalarGridSpec(
            num_scalar_prefetch=1,
            grid=(1,),
            in_specs=[whole(own.shape), whole(from_node.shape)]
            + [whole(part.shape) for part in returned],
            out_specs=whole((rows_dev, width)),
            scratch_shapes=[pltpu.VMEM((rows_dev, width), f32)],
        ),
        compiler_params=params(20),
        cost_estimate=LIGHT,
        name="collect",
    )(picks, own, from_node, *returned)


def body(
    features, cotangent, loader, w_query, w_key, w_value, norm_gain, send_blocks, tile_lists
):
    row_count = lax.axis_size("row")
    col_count = lax.axis_size("col")
    devices = row_count * col_count
    col = lax.axis_index("col")
    self_index = lax.axis_index("row") * col_count + col
    self_id = self_index.astype(jnp.int32).reshape(1)
    rows_dev, width = features.shape
    per_peer = rows_dev // devices
    block_count = tile_lists.shape[0]
    block = rows_dev // block_count
    capacity = send_blocks.shape[2]
    shifts = col_count - 1
    table_rows = rows_dev + shifts * capacity * block
    reads = 1 + tile_lists.shape[1]
    loader = loader.reshape(devices, rows_dev)
    gain = norm_gain.reshape(1, width)

    splits = (width // 2, width // 2)

    def exchange(rows):
        buffer = rows.reshape(devices, per_peer, rows.shape[1])
        out = lax.all_to_all(buffer, ("row", "col"), split_axis=0, concat_axis=0, tiled=True)
        return out.reshape(rows.shape)

    send_row = lax.dynamic_index_in_dim(send_blocks, self_index, 0, keepdims=False)
    peers = (col + 1 + jnp.arange(shifts, dtype=jnp.int32)) % col_count
    picks = send_row[peers].reshape(-1)
    source = (tile_lists - block_count) // capacity
    shift = (col - source) % col_count
    moved = block_count + (shift - 1) * capacity + (tile_lists - block_count) % capacity
    entries = jnp.where(tile_lists < block_count, tile_lists, moved)
    entries = jnp.concatenate(
        [jnp.arange(block_count, dtype=jnp.int32)[:, None], entries], axis=1
    ).reshape(-1)

    rows = exchange(send_permute(self_id, loader, features, 2, 0))
    others = [send_permute(self_id, loader, features, 2, 1)]
    to_node, from_node, to_row = index_tables(self_id, loader, rows_dev)
    rows, to_node, from_node, to_row, picks, entries, others = lax.optimization_barrier(
        (rows, to_node, from_node, to_row, picks, entries, others)
    )
    def forward_rows(outgoing):
        moved = []
        for at in range(shifts):
            perm = [(c, (c + at + 1) % col_count) for c in range(col_count)]
            moved.append(lax.ppermute(outgoing[at], "col", perm))
        return moved

    feature_rows = [rows]
    outgoing = outbound_blocks(picks, to_node, rows, shifts, capacity, block)
    arrived = [forward_rows(outgoing)]
    cot_out = send_permute(self_id, loader, cotangent, 1, 0)
    for other in others:
        rows = exchange(other)
        rows, cot_out, arrived = lax.optimization_barrier((rows, cot_out, arrived))
        feature_rows.append(rows)
        outgoing = outbound_blocks(picks, to_node, rows, shifts, capacity, block)
        cot_out, outgoing = lax.optimization_barrier((cot_out, outgoing))
        arrived.append(forward_rows(outgoing))
    cot_rows = exchange(cot_out)

    queries, k_table, v_table = project(
        to_node, feature_rows, w_query, w_key, w_value, table_rows
    )
    for at in range(shifts):
        parts = [moved[at] for moved in arrived]
        start = rows_dev + at * capacity * block
        k_table, v_table = remote_project(parts, w_key, w_value, k_table, v_table, start)

    layer_rows, mixed, stats = forward(
        entries, queries, k_table, v_table, gain, from_node, block, reads
    )
    layer_back = exchange(layer_rows)
    grad_q, own_k, own_v, far_all = backward(
        entries,
        to_node,
        cot_rows,
        gain,
        mixed,
        stats,
        queries,
        k_table,
        v_table,
        w_key,
        w_value,
        block,
        reads,
        shifts,
        splits,
    )
    returned = []
    for far in far_all:
        moved = []
        for at in range(shifts):
            perm = [(c, (c - at - 1) % col_count) for c in range(col_count)]
            moved.append(lax.ppermute(far[at], "col", perm))
        returned.append(moved)
    own_parts = own_project(grad_q, own_k, own_v, w_query, w_key, w_value, splits)
    grad_back = [
        exchange(collect(picks, own, from_node, moved, capacity, block))
        for own, moved in zip(own_parts, returned)
    ]
    return (permute(to_row, [layer_back]), permute(to_row, grad_back))


def solution(mesh):
    split = P(("row", "col"), None)
    in_specs = (split, split, P(), P(), P(), P(), P(), P(), split)
    return jax.shard_map(
        body, mesh=mesh, in_specs=in_specs, out_specs=(split, split), check_vma=False
    )
```

```python
import functools
import math

import jax
import jax.numpy as jnp
from jax import lax
from jax.experimental import pallas as pl
from jax.experimental.pallas import tpu as pltpu
from jax.sharding import PartitionSpec as P

HEADS = 8
HEAD_DIM = 128
SCALE = HEAD_DIM ** (-0.5)
LANE = 128
EXPO = SCALE * math.log2(math.e)
MIB = 1024 * 1024
SUBLANES = 8
CHUNK = 64
UNIT = 256
LIGHT = pl.CostEstimate(flops=0, transcendentals=0, bytes_accessed=0)

NT = (((1,), (1,)), ((), ()))
TN = (((0,), (0,)), ((), ()))
bf16 = jnp.bfloat16
f32 = jnp.float32


def hbm(shape, dtype):
    return pltpu.HBM(shape, jnp.dtype(dtype))


def pin(value):
    return pltpu.with_memory_space_constraint(value, pltpu.HBM)


def params(mib, axes=1):
    return pltpu.CompilerParams(
        dimension_semantics=("arbitrary",) * axes, vmem_limit_bytes=mib * MIB
    )


def whole(shape):
    zeros = (0,) * len(shape)
    return pl.BlockSpec(shape, lambda *_: zeros, pipeline_mode=pl.Buffered(1))


def matmul(left, right):
    return jnp.dot(left, right, preferred_element_type=f32)


def iota(shape, axis):
    return lax.broadcasted_iota(jnp.int32, shape, axis)


def lane_rank(mask):
    rows, count = mask.shape
    before = (iota((LANE, LANE), 0) < iota((LANE, LANE), 1)).astype(f32).astype(bf16)
    carry = jnp.zeros((rows, 1), f32)
    pieces = []
    for at in range(0, count, LANE):
        part = mask[:, at : at + LANE]
        pieces.append(matmul(part.astype(bf16), before) + carry)
        carry = carry + jnp.sum(part, axis=1, keepdims=True)
    return jnp.concatenate(pieces, axis=1)


def send_slots(nodes, devices):
    rows_dev = nodes.shape[1]
    per_peer = rows_dev // devices
    owner = lax.shift_right_logical(nodes, rows_dev.bit_length() - 1)
    owners = iota((devices, rows_dev), 0)
    mask = (owner == owners).astype(f32)
    slot = mask * (lane_rank(mask) + (owners * per_peer).astype(f32))
    return jnp.sum(slot, axis=0, keepdims=True).astype(jnp.int32)


def one_hot(cond):
    return jnp.where(cond, 1.0, 0.0)


def send_kernel(self_ref, loader_ref, rows_ref, out_ref, slot_ref):
    step = pl.program_id(0)
    chunk = out_ref.shape[0]
    rows_dev = rows_ref.shape[0]

    @pl.when(step == 0)
    def _():
        nodes = loader_ref[pl.ds(self_ref[0], 1), :]
        slot_ref[...] = send_slots(nodes, loader_ref.shape[0])

    pick = one_hot(slot_ref[...] == iota((chunk, rows_dev), 0) + step * chunk)
    out_ref[...] = matmul(pick.astype(bf16), rows_ref[...]).astype(bf16)


def send_permute(self_id, loader, rows, pieces, at):
    rows_dev, width = rows.shape
    chunk = 256
    piece = width // pieces
    return pl.pallas_call(
        send_kernel,
        out_shape=hbm((rows_dev, piece), bf16),
        grid_spec=pltpu.PrefetchScalarGridSpec(
            num_scalar_prefetch=1,
            grid=(rows_dev // chunk,),
            in_specs=[
                whole(loader.shape),
                pl.BlockSpec(
                    (rows_dev, piece), lambda i, _: (0, at), pipeline_mode=pl.Buffered(1)
                ),
            ],
            out_specs=pl.BlockSpec((chunk, piece), lambda i, _: (i, 0)),
            scratch_shapes=[pltpu.VMEM((1, rows_dev), jnp.int32)],
        ),
        compiler_params=params(10),
        name="send_permute",
    )(self_id, loader, pin(rows))


def index_kernel(self_ref, loader_ref, to_node_ref, from_node_ref, to_row_ref, slot_ref, key_ref):
    step = pl.program_id(0)
    devices, rows_dev = loader_ref.shape
    per_peer = rows_dev // devices
    chunk = from_node_ref.shape[0]
    sources = chunk // per_peer
    me = self_ref[0]

    @pl.when(step == 0)
    def _():
        slot_ref[...] = send_slots(loader_ref[pl.ds(me, 1), :], devices)
        owner = lax.shift_right_logical(loader_ref[...], rows_dev.bit_length() - 1)
        mask = (owner == me).astype(f32)
        rank = lane_rank(mask).astype(jnp.int32)
        key_ref[...] = jnp.where(owner == me, rank, -1)

    pieces = []
    for t in range(sources):
        source = step * sources + t
        key = key_ref[pl.ds(source, 1), :]
        local = loader_ref[pl.ds(source, 1), :] - me * rows_dev
        hit = key == iota((per_peer, rows_dev), 0)
        pieces.append(jnp.sum(jnp.where(hit, local.astype(f32), 0.0), axis=1, keepdims=True))
    arriving = jnp.concatenate(pieces, axis=0).astype(jnp.int32)
    pick = one_hot(arriving == iota((chunk, rows_dev), 1))
    from_node_ref[...] = pick.astype(bf16)
    to_node_ref[...] = pick.T.astype(bf16)
    back = one_hot(slot_ref[...] == iota((chunk, rows_dev), 0) + step * chunk)
    to_row_ref[...] = back.T.astype(bf16)


def index_tables(self_id, loader, rows_dev):
    chunk = LANE
    square = hbm((rows_dev, rows_dev), bf16)
    return pl.pallas_call(
        index_kernel,
        out_shape=(square, square, square),
        grid_spec=pltpu.PrefetchScalarGridSpec(
            num_scalar_prefetch=1,
            grid=(rows_dev // chunk,),
            in_specs=[whole(loader.shape)],
            out_specs=(
                pl.BlockSpec((rows_dev, chunk), lambda i, _: (0, i)),
                pl.BlockSpec((chunk, rows_dev), lambda i, _: (i, 0)),
                pl.BlockSpec((rows_dev, chunk), lambda i, _: (0, i)),
            ),
            scratch_shapes=[
                pltpu.VMEM((1, rows_dev), jnp.int32),
                pltpu.VMEM(loader.shape, jnp.int32),
            ],
        ),
        compiler_params=params(10),
        name="index_tables",
    )(self_id, loader)


def permute_kernel(pick_ref, rows_ref, *refs):
    out_ref = refs[-1]
    chunk = out_ref.shape[0]
    at = pl.multiple_of(pl.program_id(1) * chunk, chunk)
    out_ref[...] = matmul(pick_ref[pl.ds(at, chunk), :], rows_ref[...]).astype(bf16)


def permute(pick, pieces):
    rows_dev = pick.shape[0]
    width = sum(rows.shape[1] for rows in pieces)
    chunk = 512
    out, low = [], 0
    for rows in pieces:
        first = low // UNIT
        out = [
            pl.pallas_call(
                permute_kernel,
                out_shape=hbm((rows_dev, width), bf16),
                grid=(rows.shape[1] // UNIT, rows_dev // chunk),
                in_specs=[
                    whole(pick.shape),
                    pl.BlockSpec((rows_dev, UNIT), lambda j, i: (0, j)),
                ]
                + [pl.BlockSpec(memory_space=pl.ANY)] * len(out),
                out_specs=pl.BlockSpec((chunk, UNIT), lambda j, i, first=first: (i, first + j)),
                input_output_aliases={2: 0} if out else {},
                compiler_params=params(10, 2),
                name="permute",
            )(pick, pin(rows), *out)
        ]
        low += rows.shape[1]
    return out[0]


def outbound_kernel(picks_ref, rows_ref, *refs):
    pick_refs, out_refs = refs[: len(refs) // 2], refs[len(refs) // 2 :]
    for pick_ref, out_ref in zip(pick_refs, out_refs):
        out_ref[...] = matmul(pick_ref[...], rows_ref[...]).astype(bf16)


def outbound_blocks(picks, to_node, rows, shifts, capacity, block):
    rows_dev, width = rows.shape

    def pick_spec(shift):
        def index(slot, picks):
            return jnp.maximum(picks[shift * capacity + slot], 0), 0

        return pl.BlockSpec((block, rows_dev), index)

    return pl.pallas_call(
        outbound_kernel,
        out_shape=[hbm((capacity * block, width), bf16)] * len(shifts),
        grid_spec=pltpu.PrefetchScalarGridSpec(
            num_scalar_prefetch=1,
            grid=(capacity,),
            in_specs=[whole(rows.shape)] + [pick_spec(shift) for shift in shifts],
            out_specs=[pl.BlockSpec((block, width), lambda i, _: (i, 0))] * len(shifts),
        ),
        compiler_params=params(16),
        name="outbound",
    )(picks, pin(rows), *[pin(to_node)] * len(shifts))


def project_kernel(to_node_ref, wq_ref, wk_ref, wv_ref, *refs):
    row_refs, (q_ref, k_ref, v_ref) = refs[:-3], refs[-3:]
    owned = [matmul(to_node_ref[...], ref[...]).astype(bf16) for ref in row_refs]
    owned = jnp.concatenate(owned, axis=1)
    q_ref[...] = matmul(owned, wq_ref[...]).astype(bf16)
    k_ref[...] = matmul(owned, wk_ref[...]).astype(bf16)
    v_ref[...] = matmul(owned, wv_ref[...]).astype(bf16)


def project(to_node, rows, w_query, w_key, w_value, table_rows):
    rows_dev = to_node.shape[0]
    width = w_query.shape[1]
    chunk = 256
    out_spec = pl.BlockSpec((chunk, width), lambda i: (i, 0))
    table = hbm((table_rows, width), bf16)
    return pl.pallas_call(
        project_kernel,
        out_shape=(hbm((rows_dev, width), bf16), table, table),
        grid=(rows_dev // chunk,),
        in_specs=[
            pl.BlockSpec((chunk, rows_dev), lambda i: (i, 0)),
            whole(w_query.shape),
            whole(w_key.shape),
            whole(w_value.shape),
        ]
        + [whole(piece.shape) for piece in rows],
        out_specs=(out_spec, out_spec, out_spec),
        compiler_params=params(20),
        name="project",
    )(pin(to_node), w_query, w_key, w_value, *map(pin, rows))


def remote_kernel(wk_ref, wv_ref, k_in, v_in, *refs):
    row_refs, (k_ref, v_ref) = refs[:-2], refs[-2:]
    rows = jnp.concatenate([ref[...] for ref in row_refs], axis=1)
    k_ref[...] = matmul(rows, wk_ref[...]).astype(bf16)
    v_ref[...] = matmul(rows, wv_ref[...]).astype(bf16)


def remote_project(rows, w_key, w_value, k_table, v_table, first_row):
    chunk = rows[0].shape[0]
    width = w_key.shape[1]
    at = first_row // chunk
    out_spec = pl.BlockSpec((chunk, width), lambda i: (at, 0))
    any_spec = pl.BlockSpec(memory_space=pl.ANY)
    table = hbm(k_table.shape, bf16)
    return pl.pallas_call(
        remote_kernel,
        out_shape=(table, table),
        grid=(1,),
        in_specs=[whole(w_key.shape), whole(w_value.shape), any_spec, any_spec]
        + [whole(piece.shape) for piece in rows],
        out_specs=(out_spec, out_spec),
        input_output_aliases={2: 0, 3: 1},
        compiler_params=params(12),
        name="remote_project",
    )(w_key, w_value, k_table, v_table, *rows)


def split_dot(left, right):
    return lax.dot_general(left, right, NT, preferred_element_type=f32)


def fold(rows, op):
    total = rows[:SUBLANES]
    for at in range(SUBLANES, rows.shape[0], SUBLANES):
        total = op(total, rows[at : at + SUBLANES])
    return total


def entry_specs(block, width, reads):
    return [
        pl.BlockSpec((block, width), lambda i, entries, j=j: (entries[i * reads + j], 0))
        for j in range(reads)
    ]


def entry_args(table, reads):
    return [pin(table)] * reads


def forward_kernel(
    reads,
    entries_ref,
    q_ref,
    gain_ref,
    from_node_ref,
    *refs,
):
    k_refs, v_refs = refs[:reads], refs[reads : 2 * reads]
    out_hbm, mixed_ref, stats_ref, layer_ref, score_ref, prob_ref = refs[2 * reads : -2]
    out_ref, out_sem = refs[-2:]
    block, width = q_ref.shape
    step = pl.program_id(0)
    keys = reads * block
    for head in range(HEADS):
        cols = slice(head * HEAD_DIM, (head + 1) * HEAD_DIM)
        key_rows = jnp.concatenate([ref[:, cols] for ref in k_refs], axis=0)
        score_ref[head] = split_dot(key_rows, q_ref[:, cols])
    for head in range(HEADS):
        top = fold(score_ref[head, :CHUNK, :], jnp.maximum)
        for at in range(CHUNK, keys, CHUNK):
            top = jnp.maximum(top, fold(score_ref[head, at : at + CHUNK, :], jnp.maximum))
        top = jnp.max(top, axis=0, keepdims=True)
        total = jnp.zeros((SUBLANES, block), f32)
        for at in range(0, keys, CHUNK):
            expo = jnp.exp2((score_ref[head, at : at + CHUNK, :] - top) * EXPO)
            score_ref[head, at : at + CHUNK, :] = expo
            total = total + fold(expo, jnp.add)
        inv = 1.0 / jnp.sum(total, axis=0, keepdims=True)
        for at in range(0, keys, CHUNK):
            part = slice(at, at + CHUNK)
            prob_ref[head, part, :] = (score_ref[head, part, :] * inv).astype(bf16)
        stats_ref[2 * head : 2 * head + 1, :] = top
        stats_ref[2 * head + 1 : 2 * head + 2, :] = inv
    for head in range(HEADS):
        cols = slice(head * HEAD_DIM, (head + 1) * HEAD_DIM)
        vals = jnp.concatenate([ref[:, cols] for ref in v_refs], axis=0)
        mixed_ref[:, cols] = lax.dot_general(
            prob_ref[head], vals, TN, preferred_element_type=f32
        )
    mixed = mixed_ref[...]
    inv_rms = lax.rsqrt(jnp.mean(mixed * mixed, axis=1, keepdims=True) + 1e-06)
    rows = pl.ds(pl.multiple_of(step * block, block), block)
    layer_ref[rows, :] = (mixed * inv_rms * gain_ref[...]).astype(bf16)

    @pl.when(step == pl.num_programs(0) - 1)
    def _():
        chunk = 2 * block
        saves = []
        for at in range(0, out_ref.shape[0], chunk):
            part = slice(at, at + chunk)
            out_ref[part, :] = matmul(from_node_ref[part, :], layer_ref[...]).astype(bf16)
            saves.append(
                pltpu.make_async_copy(
                    out_ref.at[part, :], out_hbm.at[part, :], out_sem.at[at // chunk]
                )
            )
            saves[-1].start()
        for save in saves:
            save.wait()


def forward(entries, queries, k_table, v_table, gain, from_node, block, reads):
    rows_dev, width = queries.shape
    return pl.pallas_call(
        functools.partial(forward_kernel, reads),
        out_shape=(
            hbm((rows_dev, width), bf16),
            hbm((rows_dev, width), f32),
            hbm((rows_dev // block * 2 * HEADS, block), f32),
        ),
        grid_spec=pltpu.PrefetchScalarGridSpec(
            num_scalar_prefetch=1,
            grid=(rows_dev // block,),
            in_specs=[
                pl.BlockSpec((block, width), lambda i, _: (i, 0)),
                whole(gain.shape),
                whole(from_node.shape),
            ]
            + entry_specs(block, width, reads) * 2,
            out_specs=(
                pl.BlockSpec(memory_space=pl.ANY),
                pl.BlockSpec((block, width), lambda i, _: (i, 0)),
                pl.BlockSpec((2 * HEADS, block), lambda i, _: (i, 0)),
            ),
            scratch_shapes=[
                pltpu.VMEM((rows_dev, width), bf16),
                pltpu.VMEM((HEADS, reads * block, block), f32),
                pltpu.VMEM((HEADS, reads * block, block), bf16),
                pltpu.VMEM((rows_dev, width), bf16),
                pltpu.SemaphoreType.DMA((rows_dev // (2 * block),)),
            ],
        ),
        compiler_params=params(32),
        name="forward",
    )(
        entries,
        pin(queries),
        gain,
        from_node,
        *entry_args(k_table, reads),
        *entry_args(v_table, reads),
    )


def backward_kernel(
    reads,
    shifts,
    entries_ref,
    to_node_ref,
    cot_ref,
    gain_ref,
    mixed_ref,
    stats_ref,
    q_ref,
    *refs,
):
    k_refs, v_refs = refs[:reads], refs[reads : 2 * reads]
    wk_hbm, wv_hbm, gq_ref, own_k_hbm, own_v_hbm = refs[2 * reads : 2 * reads + 5]
    far_refs = refs[2 * reads + 5 : -14]
    sum_k_ref, sum_v_ref, prob_ref, grad_prob_ref, prob_half_ref = refs[-14:-9]
    grad_score_ref, grad_mix_ref, own_k_ref, own_v_ref, wk_ref, wv_ref = refs[-9:-3]
    w_sem, own_k_sem, own_v_sem = refs[-3:]
    block, width = q_ref.shape
    step = pl.program_id(0)
    own = own_k_ref.shape[0]
    keys = reads * block
    load_wk = pltpu.make_async_copy(wk_hbm, wk_ref, w_sem.at[0])
    load_wv = pltpu.make_async_copy(wv_hbm, wv_ref, w_sem.at[1])
    save_k = pltpu.make_async_copy(own_k_ref, own_k_hbm, own_k_sem)
    save_v = pltpu.make_async_copy(own_v_ref, own_v_hbm, own_v_sem)

    @pl.when(step == 0)
    def _():
        sum_k_ref[...] = jnp.zeros_like(sum_k_ref)
        sum_v_ref[...] = jnp.zeros_like(sum_v_ref)
        load_wk.start()
        load_wv.start()

    entries = [entries_ref[step * reads + j] * block for j in range(reads)]
    starts = [pl.multiple_of(at, block) for at in entries]
    mixed = mixed_ref[...]
    inv_rms = lax.rsqrt(jnp.mean(mixed * mixed, axis=1, keepdims=True) + 1e-06)
    grad_in = matmul(to_node_ref[...], cot_ref[...]) * gain_ref[...]
    inner = jnp.mean(grad_in * mixed, axis=1, keepdims=True)
    grad_mix = inv_rms * (grad_in - mixed * (inv_rms * inv_rms * inner))
    grad_mix_ref[...] = grad_mix.astype(bf16)
    for head in range(HEADS):
        cols = slice(head * HEAD_DIM, (head + 1) * HEAD_DIM)
        key_rows = jnp.concatenate([ref[:, cols] for ref in k_refs], axis=0)
        val_rows = jnp.concatenate([ref[:, cols] for ref in v_refs], axis=0)
        prob_ref[head] = split_dot(key_rows, q_ref[:, cols])
        grad_prob_ref[head] = split_dot(val_rows, grad_mix_ref[:, cols])
    for head in range(HEADS):
        top = stats_ref[2 * head : 2 * head + 1, :]
        inv = stats_ref[2 * head + 1 : 2 * head + 2, :]
        total = jnp.zeros((SUBLANES, block), f32)
        for at in range(0, keys, CHUNK):
            part = slice(at, at + CHUNK)
            prob = jnp.exp2((prob_ref[head, part, :] - top) * EXPO) * inv
            prob_ref[head, part, :] = prob
            prob_half_ref[head, part, :] = prob.astype(bf16)
            total = total + fold(prob * grad_prob_ref[head, part, :], jnp.add)
        delta = jnp.sum(total, axis=0, keepdims=True)
        for at in range(0, keys, CHUNK):
            part = slice(at, at + CHUNK)
            centred = (grad_prob_ref[head, part, :] - delta) * SCALE
            grad_score_ref[head, part, :] = (prob_ref[head, part, :] * centred).astype(bf16)
    for head in range(HEADS):
        cols = slice(head * HEAD_DIM, (head + 1) * HEAD_DIM)
        key_rows = jnp.concatenate([ref[:, cols] for ref in k_refs], axis=0)
        gq = lax.dot_general(grad_score_ref[head], key_rows, TN, preferred_element_type=f32)
        gq_ref[:, cols] = gq.astype(bf16)
        key_term = matmul(grad_score_ref[head], q_ref[:, cols])
        value_term = matmul(prob_half_ref[head], grad_mix_ref[:, cols])
        for j, at in enumerate(starts):
            part = slice(j * block, (j + 1) * block)
            rows = pl.ds(at, block)
            sum_k_ref[rows, cols] += key_term[part]
            sum_v_ref[rows, cols] += value_term[part]

    @pl.when(step == pl.num_programs(0) - 1)
    def _():
        own_k_ref[...] = sum_k_ref[:own, :].astype(bf16)
        save_k.start()
        own_v_ref[...] = sum_v_ref[:own, :].astype(bf16)
        save_v.start()
        load_wk.wait()
        load_wv.wait()
        low = 0
        for piece in range(0, len(far_refs), shifts):
            chunk, wide = far_refs[piece].shape
            outs = slice(low, low + wide)
            for at in range(shifts):
                rows = slice(own + at * chunk, own + (at + 1) * chunk)
                total = split_dot(sum_k_ref[rows, :].astype(bf16), wk_ref[outs, :])
                total += split_dot(sum_v_ref[rows, :].astype(bf16), wv_ref[outs, :])
                far_refs[piece + at][...] = total.astype(bf16)
            low += wide
        save_k.wait()
        save_v.wait()


def backward(
    entries,
    to_node,
    cot_rows,
    gain,
    mixed,
    stats,
    queries,
    k_table,
    v_table,
    w_key,
    w_value,
    block,
    reads,
    shifts,
    splits,
):
    rows_dev, width = queries.shape
    table_rows = k_table.shape[0]
    own = hbm((rows_dev, width), bf16)
    far = [((table_rows - rows_dev) // shifts, wide) for wide in splits for _ in range(shifts)]
    grant = min(60, 24 + 10 * table_rows * width // MIB)
    row_spec = pl.BlockSpec((block, width), lambda i, _: (i, 0))
    any_spec = pl.BlockSpec(memory_space=pl.ANY)
    out = pl.pallas_call(
        functools.partial(backward_kernel, reads, shifts),
        out_shape=[own, own, own] + [hbm(shape, bf16) for shape in far],
        grid_spec=pltpu.PrefetchScalarGridSpec(
            num_scalar_prefetch=1,
            grid=(rows_dev // block,),
            in_specs=[
                pl.BlockSpec((block, rows_dev), lambda i, _: (i, 0)),
                whole(cot_rows.shape),
                whole(gain.shape),
                row_spec,
                pl.BlockSpec((2 * HEADS, block), lambda i, _: (i, 0)),
                row_spec,
            ]
            + entry_specs(block, width, reads) * 2
            + [any_spec, any_spec],
            out_specs=[row_spec, any_spec, any_spec] + [whole(shape) for shape in far],
            scratch_shapes=[
                pltpu.VMEM((table_rows, width), f32),
                pltpu.VMEM((table_rows, width), f32),
                pltpu.VMEM((HEADS, reads * block, block), f32),
                pltpu.VMEM((HEADS, reads * block, block), f32),
                pltpu.VMEM((HEADS, reads * block, block), bf16),
                pltpu.VMEM((HEADS, reads * block, block), bf16),
                pltpu.VMEM((block, width), bf16),
                pltpu.VMEM((rows_dev, width), bf16),
                pltpu.VMEM((rows_dev, width), bf16),
                pltpu.VMEM(w_key.shape, bf16),
                pltpu.VMEM(w_value.shape, bf16),
                pltpu.SemaphoreType.DMA((2,)),
                pltpu.SemaphoreType.DMA,
                pltpu.SemaphoreType.DMA,
            ],
        ),
        compiler_params=params(grant),
        name="backward",
    )(
        entries,
        pin(to_node),
        cot_rows,
        gain,
        pin(mixed),
        pin(stats),
        pin(queries),
        *entry_args(k_table, reads),
        *entry_args(v_table, reads),
        pin(w_key),
        pin(w_value),
    )
    pieces = [out[at : at + shifts] for at in range(3, len(out), shifts)]
    return out[0], out[1], out[2], pieces


def own_kernel(q_ref, k_ref, v_ref, wq_ref, wk_ref, wv_ref, *out_refs):
    total = split_dot(q_ref[...], wq_ref[...])
    total += split_dot(k_ref[...], wk_ref[...])
    total += split_dot(v_ref[...], wv_ref[...])
    low = 0
    for out_ref in out_refs:
        wide = out_ref.shape[1]
        out_ref[...] = total[:, low : low + wide]
        low += wide


def own_project(grad_q, own_k, own_v, w_query, w_key, w_value, splits):
    rows_dev, width = grad_q.shape
    chunk = 256
    spec = pl.BlockSpec((chunk, width), lambda i: (i, 0))
    return pl.pallas_call(
        own_kernel,
        out_shape=[jax.ShapeDtypeStruct((rows_dev, wide), f32) for wide in splits],
        grid=(rows_dev // chunk,),
        in_specs=[spec, spec, spec] + [whole(w_query.shape)] * 3,
        out_specs=[pl.BlockSpec((chunk, wide), lambda i: (i, 0)) for wide in splits],
        compiler_params=params(20),
        cost_estimate=LIGHT,
        name="own_project",
    )(pin(grad_q), pin(own_k), pin(own_v), w_query, w_key, w_value)


def collect_kernel(capacity, block, picks_ref, own_ref, from_node_ref, *refs):
    returned, (out_ref, total_ref) = refs[:-2], refs[-2:]
    total_ref[...] = own_ref[...]
    for at, ref in enumerate(returned):
        for slot in range(capacity):
            pick = picks_ref[at * capacity + slot]

            @pl.when(pick >= 0)
            def _():
                rows = pl.ds(pl.multiple_of(pick * block, block), block)
                part = ref[slot * block : (slot + 1) * block, :]
                total_ref[rows, :] += part.astype(f32)

    out_ref[...] = matmul(from_node_ref[...], total_ref[...].astype(bf16)).astype(bf16)


def collect(picks, own, from_node, returned, capacity, block):
    rows_dev, width = own.shape
    return pl.pallas_call(
        functools.partial(collect_kernel, capacity, block),
        out_shape=hbm((rows_dev, width), bf16),
        grid_spec=pltpu.PrefetchScalarGridSpec(
            num_scalar_prefetch=1,
            grid=(1,),
            in_specs=[whole(own.shape), whole(from_node.shape)]
            + [whole(part.shape) for part in returned],
            out_specs=whole((rows_dev, width)),
            scratch_shapes=[pltpu.VMEM((rows_dev, width), f32)],
        ),
        compiler_params=params(20),
        cost_estimate=LIGHT,
        name="collect",
    )(picks, own, from_node, *returned)


def body(
    features, cotangent, loader, w_query, w_key, w_value, norm_gain, send_blocks, tile_lists
):
    row_count = lax.axis_size("row")
    col_count = lax.axis_size("col")
    devices = row_count * col_count
    col = lax.axis_index("col")
    self_index = lax.axis_index("row") * col_count + col
    self_id = self_index.astype(jnp.int32).reshape(1)
    rows_dev, width = features.shape
    per_peer = rows_dev // devices
    block_count = tile_lists.shape[0]
    block = rows_dev // block_count
    capacity = send_blocks.shape[2]
    shifts = col_count - 1
    table_rows = rows_dev + shifts * capacity * block
    reads = 1 + tile_lists.shape[1]
    loader = loader.reshape(devices, rows_dev)
    gain = norm_gain.reshape(1, width)

    splits = (width // 2, width // 2)

    def exchange(rows):
        buffer = rows.reshape(devices, per_peer, rows.shape[1])
        out = lax.all_to_all(buffer, ("row", "col"), split_axis=0, concat_axis=0, tiled=True)
        return out.reshape(rows.shape)

    send_row = lax.dynamic_index_in_dim(send_blocks, self_index, 0, keepdims=False)
    peers = (col + 1 + jnp.arange(shifts, dtype=jnp.int32)) % col_count
    picks = send_row[peers].reshape(-1)
    source = (tile_lists - block_count) // capacity
    shift = (col - source) % col_count
    moved = block_count + (shift - 1) * capacity + (tile_lists - block_count) % capacity
    entries = jnp.where(tile_lists < block_count, tile_lists, moved)
    entries = jnp.concatenate(
        [jnp.arange(block_count, dtype=jnp.int32)[:, None], entries], axis=1
    ).reshape(-1)

    rows = exchange(send_permute(self_id, loader, features, 2, 0))
    others = [send_permute(self_id, loader, features, 2, 1)]
    to_node, from_node, to_row = index_tables(self_id, loader, rows_dev)
    rows, to_node, from_node, to_row, picks, entries, others = lax.optimization_barrier(
        (rows, to_node, from_node, to_row, picks, entries, others)
    )
    def forward_rows(outgoing, at):
        perm = [(c, (c + at + 1) % col_count) for c in range(col_count)]
        return lax.ppermute(outgoing, "col", perm)

    every = list(range(shifts))
    feature_rows = [rows]
    outgoing = outbound_blocks(picks, to_node, rows, every, capacity, block)
    arrived = [[forward_rows(outgoing[at], at) for at in every]]
    cot_out = send_permute(self_id, loader, cotangent, 1, 0)
    for other in others:
        rows = exchange(other)
        rows, cot_out, arrived = lax.optimization_barrier((rows, cot_out, arrived))
        feature_rows.append(rows)
        outgoing = outbound_blocks(picks, to_node, rows, every, capacity, block)
        cot_out, outgoing = lax.optimization_barrier((cot_out, outgoing))
        arrived.append([forward_rows(outgoing[at], at) for at in every])
    cot_rows = exchange(cot_out)

    queries, k_table, v_table = project(
        to_node, feature_rows, w_query, w_key, w_value, table_rows
    )
    for at in range(shifts):
        parts = [moved[at] for moved in arrived]
        start = rows_dev + at * capacity * block
        k_table, v_table = remote_project(parts, w_key, w_value, k_table, v_table, start)

    layer_rows, mixed, stats = forward(
        entries, queries, k_table, v_table, gain, from_node, block, reads
    )
    layer_back = exchange(layer_rows)
    grad_q, own_k, own_v, far_all = backward(
        entries,
        to_node,
        cot_rows,
        gain,
        mixed,
        stats,
        queries,
        k_table,
        v_table,
        w_key,
        w_value,
        block,
        reads,
        shifts,
        splits,
    )
    returned = []
    for far in far_all:
        moved = []
        for at in range(shifts):
            perm = [(c, (c - at - 1) % col_count) for c in range(col_count)]
            moved.append(lax.ppermute(far[at], "col", perm))
        returned.append(moved)
    own_parts = own_project(grad_q, own_k, own_v, w_query, w_key, w_value, splits)
    grad_back = [
        exchange(collect(picks, own, from_node, moved, capacity, block))
        for own, moved in zip(own_parts, returned)
    ]
    return (permute(to_row, [layer_back]), permute(to_row, grad_back))


def solution(mesh):
    split = P(("row", "col"), None)
    in_specs = (split, split, P(), P(), P(), P(), P(), P(), split)
    return jax.shard_map(
        body, mesh=mesh, in_specs=in_specs, out_specs=(split, split), check_vma=False
    )
```

```python
import functools
import math

import jax
import jax.numpy as jnp
from jax import lax
from jax.experimental import pallas as pl
from jax.experimental.pallas import tpu as pltpu
from jax.sharding import PartitionSpec as P

HEADS = 8
HEAD_DIM = 128
SCALE = HEAD_DIM ** (-0.5)
LANE = 128
EXPO = SCALE * math.log2(math.e)
MIB = 1024 * 1024
SUBLANES = 8
CHUNK = 64
UNIT = 256
LIGHT = pl.CostEstimate(flops=0, transcendentals=0, bytes_accessed=0)

NT = (((1,), (1,)), ((), ()))
TN = (((0,), (0,)), ((), ()))
bf16 = jnp.bfloat16
f32 = jnp.float32


def hbm(shape, dtype):
    return pltpu.HBM(shape, jnp.dtype(dtype))


def pin(value):
    return pltpu.with_memory_space_constraint(value, pltpu.HBM)


def params(mib, axes=1):
    return pltpu.CompilerParams(
        dimension_semantics=("arbitrary",) * axes, vmem_limit_bytes=mib * MIB
    )


def whole(shape):
    zeros = (0,) * len(shape)
    return pl.BlockSpec(shape, lambda *_: zeros, pipeline_mode=pl.Buffered(1))


def matmul(left, right):
    return jnp.dot(left, right, preferred_element_type=f32)


def iota(shape, axis):
    return lax.broadcasted_iota(jnp.int32, shape, axis)


def lane_rank(mask):
    rows, count = mask.shape
    before = (iota((LANE, LANE), 0) < iota((LANE, LANE), 1)).astype(f32).astype(bf16)
    carry = jnp.zeros((rows, 1), f32)
    pieces = []
    for at in range(0, count, LANE):
        part = mask[:, at : at + LANE]
        pieces.append(matmul(part.astype(bf16), before) + carry)
        carry = carry + jnp.sum(part, axis=1, keepdims=True)
    return jnp.concatenate(pieces, axis=1)


def send_slots(nodes, devices):
    rows_dev = nodes.shape[1]
    per_peer = rows_dev // devices
    owner = lax.shift_right_logical(nodes, rows_dev.bit_length() - 1)
    owners = iota((devices, rows_dev), 0)
    mask = (owner == owners).astype(f32)
    slot = mask * (lane_rank(mask) + (owners * per_peer).astype(f32))
    return jnp.sum(slot, axis=0, keepdims=True).astype(jnp.int32)


def one_hot(cond):
    return jnp.where(cond, 1.0, 0.0)


def send_kernel(self_ref, loader_ref, rows_ref, out_ref, slot_ref):
    step = pl.program_id(0)
    chunk = out_ref.shape[0]
    rows_dev = rows_ref.shape[0]

    @pl.when(step == 0)
    def _():
        nodes = loader_ref[pl.ds(self_ref[0], 1), :]
        slot_ref[...] = send_slots(nodes, loader_ref.shape[0])

    pick = one_hot(slot_ref[...] == iota((chunk, rows_dev), 0) + step * chunk)
    out_ref[...] = matmul(pick.astype(bf16), rows_ref[...]).astype(bf16)


def send_permute(self_id, loader, rows, pieces, at):
    rows_dev, width = rows.shape
    chunk = 256
    piece = width // pieces
    return pl.pallas_call(
        send_kernel,
        out_shape=hbm((rows_dev, piece), bf16),
        grid_spec=pltpu.PrefetchScalarGridSpec(
            num_scalar_prefetch=1,
            grid=(rows_dev // chunk,),
            in_specs=[
                whole(loader.shape),
                pl.BlockSpec(
                    (rows_dev, piece), lambda i, _: (0, at), pipeline_mode=pl.Buffered(1)
                ),
            ],
            out_specs=pl.BlockSpec((chunk, piece), lambda i, _: (i, 0)),
            scratch_shapes=[pltpu.VMEM((1, rows_dev), jnp.int32)],
        ),
        compiler_params=params(10),
        name="send_permute",
    )(self_id, loader, pin(rows))


def index_kernel(self_ref, loader_ref, to_node_ref, from_node_ref, to_row_ref, slot_ref, key_ref):
    step = pl.program_id(0)
    devices, rows_dev = loader_ref.shape
    per_peer = rows_dev // devices
    chunk = from_node_ref.shape[0]
    sources = chunk // per_peer
    me = self_ref[0]

    @pl.when(step == 0)
    def _():
        slot_ref[...] = send_slots(loader_ref[pl.ds(me, 1), :], devices)
        owner = lax.shift_right_logical(loader_ref[...], rows_dev.bit_length() - 1)
        mask = (owner == me).astype(f32)
        rank = lane_rank(mask).astype(jnp.int32)
        key_ref[...] = jnp.where(owner == me, rank, -1)

    pieces = []
    for t in range(sources):
        source = step * sources + t
        key = key_ref[pl.ds(source, 1), :]
        local = loader_ref[pl.ds(source, 1), :] - me * rows_dev
        hit = key == iota((per_peer, rows_dev), 0)
        pieces.append(jnp.sum(jnp.where(hit, local.astype(f32), 0.0), axis=1, keepdims=True))
    arriving = jnp.concatenate(pieces, axis=0).astype(jnp.int32)
    pick = one_hot(arriving == iota((chunk, rows_dev), 1))
    from_node_ref[...] = pick.astype(bf16)
    to_node_ref[...] = pick.T.astype(bf16)
    back = one_hot(slot_ref[...] == iota((chunk, rows_dev), 0) + step * chunk)
    to_row_ref[...] = back.T.astype(bf16)


def index_tables(self_id, loader, rows_dev):
    chunk = LANE
    square = hbm((rows_dev, rows_dev), bf16)
    return pl.pallas_call(
        index_kernel,
        out_shape=(square, square, square),
        grid_spec=pltpu.PrefetchScalarGridSpec(
            num_scalar_prefetch=1,
            grid=(rows_dev // chunk,),
            in_specs=[whole(loader.shape)],
            out_specs=(
                pl.BlockSpec((rows_dev, chunk), lambda i, _: (0, i)),
                pl.BlockSpec((chunk, rows_dev), lambda i, _: (i, 0)),
                pl.BlockSpec((rows_dev, chunk), lambda i, _: (0, i)),
            ),
            scratch_shapes=[
                pltpu.VMEM((1, rows_dev), jnp.int32),
                pltpu.VMEM(loader.shape, jnp.int32),
            ],
        ),
        compiler_params=params(10),
        name="index_tables",
    )(self_id, loader)


def permute_kernel(pick_ref, rows_ref, *refs):
    out_ref = refs[-1]
    chunk = out_ref.shape[0]
    at = pl.multiple_of(pl.program_id(1) * chunk, chunk)
    out_ref[...] = matmul(pick_ref[pl.ds(at, chunk), :], rows_ref[...]).astype(bf16)


def permute(pick, pieces):
    rows_dev = pick.shape[0]
    width = sum(rows.shape[1] for rows in pieces)
    chunk = 512
    out, low = [], 0
    for rows in pieces:
        first = low // UNIT
        out = [
            pl.pallas_call(
                permute_kernel,
                out_shape=hbm((rows_dev, width), bf16),
                grid=(rows.shape[1] // UNIT, rows_dev // chunk),
                in_specs=[
                    whole(pick.shape),
                    pl.BlockSpec((rows_dev, UNIT), lambda j, i: (0, j)),
                ]
                + [pl.BlockSpec(memory_space=pl.ANY)] * len(out),
                out_specs=pl.BlockSpec((chunk, UNIT), lambda j, i, first=first: (i, first + j)),
                input_output_aliases={2: 0} if out else {},
                compiler_params=params(10, 2),
                name="permute",
            )(pick, pin(rows), *out)
        ]
        low += rows.shape[1]
    return out[0]


def outbound_kernel(picks_ref, rows_ref, *refs):
    pick_refs, out_refs = refs[: len(refs) // 2], refs[len(refs) // 2 :]
    for pick_ref, out_ref in zip(pick_refs, out_refs):
        out_ref[...] = matmul(pick_ref[...], rows_ref[...]).astype(bf16)


def outbound_blocks(picks, to_node, rows, shifts, capacity, block):
    rows_dev, width = rows.shape

    def pick_spec(shift):
        def index(slot, picks):
            return jnp.maximum(picks[shift * capacity + slot], 0), 0

        return pl.BlockSpec((block, rows_dev), index)

    return pl.pallas_call(
        outbound_kernel,
        out_shape=[hbm((capacity * block, width), bf16)] * len(shifts),
        grid_spec=pltpu.PrefetchScalarGridSpec(
            num_scalar_prefetch=1,
            grid=(capacity,),
            in_specs=[whole(rows.shape)] + [pick_spec(shift) for shift in shifts],
            out_specs=[pl.BlockSpec((block, width), lambda i, _: (i, 0))] * len(shifts),
        ),
        compiler_params=params(16),
        name="outbound",
    )(picks, pin(rows), *[pin(to_node)] * len(shifts))


def project_kernel(to_node_ref, wq_ref, wk_ref, wv_ref, *refs):
    row_refs, (q_ref, k_ref, v_ref) = refs[:-3], refs[-3:]
    owned = [matmul(to_node_ref[...], ref[...]).astype(bf16) for ref in row_refs]
    owned = jnp.concatenate(owned, axis=1)
    q_ref[...] = matmul(owned, wq_ref[...]).astype(bf16)
    k_ref[...] = matmul(owned, wk_ref[...]).astype(bf16)
    v_ref[...] = matmul(owned, wv_ref[...]).astype(bf16)


def project(to_node, rows, w_query, w_key, w_value, table_rows):
    rows_dev = to_node.shape[0]
    width = w_query.shape[1]
    chunk = 256
    out_spec = pl.BlockSpec((chunk, width), lambda i: (i, 0))
    table = hbm((table_rows, width), bf16)
    return pl.pallas_call(
        project_kernel,
        out_shape=(hbm((rows_dev, width), bf16), table, table),
        grid=(rows_dev // chunk,),
        in_specs=[
            pl.BlockSpec((chunk, rows_dev), lambda i: (i, 0)),
            whole(w_query.shape),
            whole(w_key.shape),
            whole(w_value.shape),
        ]
        + [whole(piece.shape) for piece in rows],
        out_specs=(out_spec, out_spec, out_spec),
        compiler_params=params(20),
        name="project",
    )(pin(to_node), w_query, w_key, w_value, *map(pin, rows))


def remote_kernel(wk_ref, wv_ref, k_in, v_in, *refs):
    row_refs, (k_ref, v_ref) = refs[:-2], refs[-2:]
    rows = jnp.concatenate([ref[...] for ref in row_refs], axis=1)
    k_ref[...] = matmul(rows, wk_ref[...]).astype(bf16)
    v_ref[...] = matmul(rows, wv_ref[...]).astype(bf16)


def remote_project(rows, w_key, w_value, k_table, v_table, first_row):
    chunk = rows[0].shape[0]
    width = w_key.shape[1]
    at = first_row // chunk
    out_spec = pl.BlockSpec((chunk, width), lambda i: (at, 0))
    any_spec = pl.BlockSpec(memory_space=pl.ANY)
    table = hbm(k_table.shape, bf16)
    return pl.pallas_call(
        remote_kernel,
        out_shape=(table, table),
        grid=(1,),
        in_specs=[whole(w_key.shape), whole(w_value.shape), any_spec, any_spec]
        + [whole(piece.shape) for piece in rows],
        out_specs=(out_spec, out_spec),
        input_output_aliases={2: 0, 3: 1},
        compiler_params=params(12),
        name="remote_project",
    )(w_key, w_value, k_table, v_table, *rows)


def split_dot(left, right):
    return lax.dot_general(left, right, NT, preferred_element_type=f32)


def fold(rows, op):
    total = rows[:SUBLANES]
    for at in range(SUBLANES, rows.shape[0], SUBLANES):
        total = op(total, rows[at : at + SUBLANES])
    return total


def entry_specs(block, width, reads):
    return [
        pl.BlockSpec((block, width), lambda i, entries, j=j: (entries[i * reads + j], 0))
        for j in range(reads)
    ]


def entry_args(table, reads):
    return [pin(table)] * reads


def forward_kernel(
    reads,
    entries_ref,
    q_ref,
    gain_ref,
    from_node_ref,
    *refs,
):
    k_refs, v_refs = refs[:reads], refs[reads : 2 * reads]
    out_hbm, mixed_ref, stats_ref, layer_ref, score_ref, prob_ref = refs[2 * reads : -2]
    out_ref, out_sem = refs[-2:]
    block, width = q_ref.shape
    step = pl.program_id(0)
    keys = reads * block
    for head in range(HEADS):
        cols = slice(head * HEAD_DIM, (head + 1) * HEAD_DIM)
        key_rows = jnp.concatenate([ref[:, cols] for ref in k_refs], axis=0)
        score_ref[head] = split_dot(key_rows, q_ref[:, cols])
    for head in range(HEADS):
        top = fold(score_ref[head, :CHUNK, :], jnp.maximum)
        for at in range(CHUNK, keys, CHUNK):
            top = jnp.maximum(top, fold(score_ref[head, at : at + CHUNK, :], jnp.maximum))
        top = jnp.max(top, axis=0, keepdims=True)
        total = jnp.zeros((SUBLANES, block), f32)
        for at in range(0, keys, CHUNK):
            expo = jnp.exp2((score_ref[head, at : at + CHUNK, :] - top) * EXPO)
            score_ref[head, at : at + CHUNK, :] = expo
            total = total + fold(expo, jnp.add)
        inv = 1.0 / jnp.sum(total, axis=0, keepdims=True)
        for at in range(0, keys, CHUNK):
            part = slice(at, at + CHUNK)
            prob_ref[head, part, :] = (score_ref[head, part, :] * inv).astype(bf16)
        stats_ref[2 * head : 2 * head + 1, :] = top
        stats_ref[2 * head + 1 : 2 * head + 2, :] = inv
    for head in range(HEADS):
        cols = slice(head * HEAD_DIM, (head + 1) * HEAD_DIM)
        vals = jnp.concatenate([ref[:, cols] for ref in v_refs], axis=0)
        mixed_ref[:, cols] = lax.dot_general(
            prob_ref[head], vals, TN, preferred_element_type=f32
        )
    mixed = mixed_ref[...]
    inv_rms = lax.rsqrt(jnp.mean(mixed * mixed, axis=1, keepdims=True) + 1e-06)
    rows = pl.ds(pl.multiple_of(step * block, block), block)
    layer_ref[rows, :] = (mixed * inv_rms * gain_ref[...]).astype(bf16)

    @pl.when(step == pl.num_programs(0) - 1)
    def _():
        chunk = 2 * block
        saves = []
        for at in range(0, out_ref.shape[0], chunk):
            part = slice(at, at + chunk)
            out_ref[part, :] = matmul(from_node_ref[part, :], layer_ref[...]).astype(bf16)
            saves.append(
                pltpu.make_async_copy(
                    out_ref.at[part, :], out_hbm.at[part, :], out_sem.at[at // chunk]
                )
            )
            saves[-1].start()
        for save in saves:
            save.wait()


def forward(entries, queries, k_table, v_table, gain, from_node, block, reads):
    rows_dev, width = queries.shape
    return pl.pallas_call(
        functools.partial(forward_kernel, reads),
        out_shape=(
            hbm((rows_dev, width), bf16),
            hbm((rows_dev, width), f32),
            hbm((rows_dev // block * 2 * HEADS, block), f32),
        ),
        grid_spec=pltpu.PrefetchScalarGridSpec(
            num_scalar_prefetch=1,
            grid=(rows_dev // block,),
            in_specs=[
                pl.BlockSpec((block, width), lambda i, _: (i, 0)),
                whole(gain.shape),
                whole(from_node.shape),
            ]
            + entry_specs(block, width, reads) * 2,
            out_specs=(
                pl.BlockSpec(memory_space=pl.ANY),
                pl.BlockSpec((block, width), lambda i, _: (i, 0)),
                pl.BlockSpec((2 * HEADS, block), lambda i, _: (i, 0)),
            ),
            scratch_shapes=[
                pltpu.VMEM((rows_dev, width), bf16),
                pltpu.VMEM((HEADS, reads * block, block), f32),
                pltpu.VMEM((HEADS, reads * block, block), bf16),
                pltpu.VMEM((rows_dev, width), bf16),
                pltpu.SemaphoreType.DMA((rows_dev // (2 * block),)),
            ],
        ),
        compiler_params=params(32),
        name="forward",
    )(
        entries,
        pin(queries),
        gain,
        from_node,
        *entry_args(k_table, reads),
        *entry_args(v_table, reads),
    )


def backward_kernel(
    reads,
    shifts,
    entries_ref,
    to_node_ref,
    cot_ref,
    gain_ref,
    mixed_ref,
    stats_ref,
    q_ref,
    *refs,
):
    k_refs, v_refs = refs[:reads], refs[reads : 2 * reads]
    wk_hbm, wv_hbm, gq_ref, own_k_hbm, own_v_hbm = refs[2 * reads : 2 * reads + 5]
    far_refs = refs[2 * reads + 5 : -14]
    sum_k_ref, sum_v_ref, prob_ref, grad_prob_ref, prob_half_ref = refs[-14:-9]
    grad_score_ref, grad_mix_ref, own_k_ref, own_v_ref, wk_ref, wv_ref = refs[-9:-3]
    w_sem, own_k_sem, own_v_sem = refs[-3:]
    block, width = q_ref.shape
    step = pl.program_id(0)
    own = own_k_ref.shape[0]
    keys = reads * block
    load_wk = pltpu.make_async_copy(wk_hbm, wk_ref, w_sem.at[0])
    load_wv = pltpu.make_async_copy(wv_hbm, wv_ref, w_sem.at[1])
    save_k = pltpu.make_async_copy(own_k_ref, own_k_hbm, own_k_sem)
    save_v = pltpu.make_async_copy(own_v_ref, own_v_hbm, own_v_sem)

    @pl.when(step == 0)
    def _():
        sum_k_ref[...] = jnp.zeros_like(sum_k_ref)
        sum_v_ref[...] = jnp.zeros_like(sum_v_ref)
        load_wk.start()
        load_wv.start()

    entries = [entries_ref[step * reads + j] * block for j in range(reads)]
    starts = [pl.multiple_of(at, block) for at in entries]
    mixed = mixed_ref[...]
    inv_rms = lax.rsqrt(jnp.mean(mixed * mixed, axis=1, keepdims=True) + 1e-06)
    grad_in = matmul(to_node_ref[...], cot_ref[...]) * gain_ref[...]
    inner = jnp.mean(grad_in * mixed, axis=1, keepdims=True)
    grad_mix = inv_rms * (grad_in - mixed * (inv_rms * inv_rms * inner))
    grad_mix_ref[...] = grad_mix.astype(bf16)
    for head in range(HEADS):
        cols = slice(head * HEAD_DIM, (head + 1) * HEAD_DIM)
        key_rows = jnp.concatenate([ref[:, cols] for ref in k_refs], axis=0)
        val_rows = jnp.concatenate([ref[:, cols] for ref in v_refs], axis=0)
        prob_ref[head] = split_dot(key_rows, q_ref[:, cols])
        grad_prob_ref[head] = split_dot(val_rows, grad_mix_ref[:, cols])
    for head in range(HEADS):
        top = stats_ref[2 * head : 2 * head + 1, :]
        inv = stats_ref[2 * head + 1 : 2 * head + 2, :]
        total = jnp.zeros((SUBLANES, block), f32)
        for at in range(0, keys, CHUNK):
            part = slice(at, at + CHUNK)
            prob = jnp.exp2((prob_ref[head, part, :] - top) * EXPO) * inv
            prob_ref[head, part, :] = prob
            prob_half_ref[head, part, :] = prob.astype(bf16)
            total = total + fold(prob * grad_prob_ref[head, part, :], jnp.add)
        delta = jnp.sum(total, axis=0, keepdims=True)
        for at in range(0, keys, CHUNK):
            part = slice(at, at + CHUNK)
            centred = (grad_prob_ref[head, part, :] - delta) * SCALE
            grad_score_ref[head, part, :] = (prob_ref[head, part, :] * centred).astype(bf16)
    for head in range(HEADS):
        cols = slice(head * HEAD_DIM, (head + 1) * HEAD_DIM)
        key_rows = jnp.concatenate([ref[:, cols] for ref in k_refs], axis=0)
        gq = lax.dot_general(grad_score_ref[head], key_rows, TN, preferred_element_type=f32)
        gq_ref[:, cols] = gq.astype(bf16)
        key_term = matmul(grad_score_ref[head], q_ref[:, cols])
        value_term = matmul(prob_half_ref[head], grad_mix_ref[:, cols])
        for j, at in enumerate(starts):
            part = slice(j * block, (j + 1) * block)
            rows = pl.ds(at, block)
            sum_k_ref[rows, cols] += key_term[part]
            sum_v_ref[rows, cols] += value_term[part]

    @pl.when(step == pl.num_programs(0) - 1)
    def _():
        own_k_ref[...] = sum_k_ref[:own, :].astype(bf16)
        save_k.start()
        own_v_ref[...] = sum_v_ref[:own, :].astype(bf16)
        save_v.start()
        load_wk.wait()
        load_wv.wait()
        low = 0
        for piece in range(0, len(far_refs), shifts):
            chunk, wide = far_refs[piece].shape
            outs = slice(low, low + wide)
            for at in range(shifts):
                rows = slice(own + at * chunk, own + (at + 1) * chunk)
                total = split_dot(sum_k_ref[rows, :].astype(bf16), wk_ref[outs, :])
                total += split_dot(sum_v_ref[rows, :].astype(bf16), wv_ref[outs, :])
                far_refs[piece + at][...] = total.astype(bf16)
            low += wide
        save_k.wait()
        save_v.wait()


def backward(
    entries,
    to_node,
    cot_rows,
    gain,
    mixed,
    stats,
    queries,
    k_table,
    v_table,
    w_key,
    w_value,
    block,
    reads,
    shifts,
    splits,
):
    rows_dev, width = queries.shape
    table_rows = k_table.shape[0]
    own = hbm((rows_dev, width), bf16)
    far = [((table_rows - rows_dev) // shifts, wide) for wide in splits for _ in range(shifts)]
    grant = min(60, 24 + 10 * table_rows * width // MIB)
    row_spec = pl.BlockSpec((block, width), lambda i, _: (i, 0))
    any_spec = pl.BlockSpec(memory_space=pl.ANY)
    out = pl.pallas_call(
        functools.partial(backward_kernel, reads, shifts),
        out_shape=[own, own, own] + [hbm(shape, bf16) for shape in far],
        grid_spec=pltpu.PrefetchScalarGridSpec(
            num_scalar_prefetch=1,
            grid=(rows_dev // block,),
            in_specs=[
                pl.BlockSpec((block, rows_dev), lambda i, _: (i, 0)),
                whole(cot_rows.shape),
                whole(gain.shape),
                row_spec,
                pl.BlockSpec((2 * HEADS, block), lambda i, _: (i, 0)),
                row_spec,
            ]
            + entry_specs(block, width, reads) * 2
            + [any_spec, any_spec],
            out_specs=[row_spec, any_spec, any_spec] + [whole(shape) for shape in far],
            scratch_shapes=[
                pltpu.VMEM((table_rows, width), f32),
                pltpu.VMEM((table_rows, width), f32),
                pltpu.VMEM((HEADS, reads * block, block), f32),
                pltpu.VMEM((HEADS, reads * block, block), f32),
                pltpu.VMEM((HEADS, reads * block, block), bf16),
                pltpu.VMEM((HEADS, reads * block, block), bf16),
                pltpu.VMEM((block, width), bf16),
                pltpu.VMEM((rows_dev, width), bf16),
                pltpu.VMEM((rows_dev, width), bf16),
                pltpu.VMEM(w_key.shape, bf16),
                pltpu.VMEM(w_value.shape, bf16),
                pltpu.SemaphoreType.DMA((2,)),
                pltpu.SemaphoreType.DMA,
                pltpu.SemaphoreType.DMA,
            ],
        ),
        compiler_params=params(grant),
        name="backward",
    )(
        entries,
        pin(to_node),
        cot_rows,
        gain,
        pin(mixed),
        pin(stats),
        pin(queries),
        *entry_args(k_table, reads),
        *entry_args(v_table, reads),
        pin(w_key),
        pin(w_value),
    )
    pieces = [out[at : at + shifts] for at in range(3, len(out), shifts)]
    return out[0], out[1], out[2], pieces


def own_kernel(q_ref, k_ref, v_ref, wq_ref, wk_ref, wv_ref, out_ref):
    total = split_dot(q_ref[...], wq_ref[...])
    total += split_dot(k_ref[...], wk_ref[...])
    total += split_dot(v_ref[...], wv_ref[...])
    out_ref[...] = total


def own_project(grad_q, own_k, own_v, w_query, w_key, w_value, wide, at):
    rows_dev, width = grad_q.shape
    chunk = 256
    spec = pl.BlockSpec((chunk, width), lambda i: (i, 0))
    w_spec = pl.BlockSpec((wide, width), lambda i: (at, 0), pipeline_mode=pl.Buffered(1))
    return pl.pallas_call(
        own_kernel,
        out_shape=pltpu.VMEM((rows_dev, wide), jnp.dtype(f32)),
        grid=(rows_dev // chunk,),
        in_specs=[spec, spec, spec, w_spec, w_spec, w_spec],
        out_specs=pl.BlockSpec((chunk, wide), lambda i: (i, 0)),
        compiler_params=params(16),
        cost_estimate=LIGHT,
        name="own_project",
    )(pin(grad_q), pin(own_k), pin(own_v), w_query, w_key, w_value)


def collect_kernel(capacity, block, picks_ref, own_ref, from_node_ref, *refs):
    returned, (out_ref, total_ref) = refs[:-2], refs[-2:]
    total_ref[...] = own_ref[...]
    for at, ref in enumerate(returned):
        for slot in range(capacity):
            pick = picks_ref[at * capacity + slot]

            @pl.when(pick >= 0)
            def _():
                rows = pl.ds(pl.multiple_of(pick * block, block), block)
                part = ref[slot * block : (slot + 1) * block, :]
                total_ref[rows, :] += part.astype(f32)

    out_ref[...] = matmul(from_node_ref[...], total_ref[...].astype(bf16)).astype(bf16)


def collect(picks, own, from_node, returned, capacity, block):
    rows_dev, width = own.shape
    return pl.pallas_call(
        functools.partial(collect_kernel, capacity, block),
        out_shape=hbm((rows_dev, width), bf16),
        grid_spec=pltpu.PrefetchScalarGridSpec(
            num_scalar_prefetch=1,
            grid=(1,),
            in_specs=[whole(own.shape), whole(from_node.shape)]
            + [whole(part.shape) for part in returned],
            out_specs=whole((rows_dev, width)),
            scratch_shapes=[pltpu.VMEM((rows_dev, width), f32)],
        ),
        compiler_params=params(14),
        cost_estimate=LIGHT,
        name="collect",
    )(picks, own, from_node, *returned)


def body(
    features, cotangent, loader, w_query, w_key, w_value, norm_gain, send_blocks, tile_lists
):
    row_count = lax.axis_size("row")
    col_count = lax.axis_size("col")
    devices = row_count * col_count
    col = lax.axis_index("col")
    self_index = lax.axis_index("row") * col_count + col
    self_id = self_index.astype(jnp.int32).reshape(1)
    rows_dev, width = features.shape
    per_peer = rows_dev // devices
    block_count = tile_lists.shape[0]
    block = rows_dev // block_count
    capacity = send_blocks.shape[2]
    shifts = col_count - 1
    table_rows = rows_dev + shifts * capacity * block
    reads = 1 + tile_lists.shape[1]
    loader = loader.reshape(devices, rows_dev)
    gain = norm_gain.reshape(1, width)

    splits = (width // 2, width // 2)

    def exchange(rows):
        buffer = rows.reshape(devices, per_peer, rows.shape[1])
        out = lax.all_to_all(buffer, ("row", "col"), split_axis=0, concat_axis=0, tiled=True)
        return out.reshape(rows.shape)

    send_row = lax.dynamic_index_in_dim(send_blocks, self_index, 0, keepdims=False)
    peers = (col + 1 + jnp.arange(shifts, dtype=jnp.int32)) % col_count
    picks = send_row[peers].reshape(-1)
    source = (tile_lists - block_count) // capacity
    shift = (col - source) % col_count
    moved = block_count + (shift - 1) * capacity + (tile_lists - block_count) % capacity
    entries = jnp.where(tile_lists < block_count, tile_lists, moved)
    entries = jnp.concatenate(
        [jnp.arange(block_count, dtype=jnp.int32)[:, None], entries], axis=1
    ).reshape(-1)

    rows = exchange(send_permute(self_id, loader, features, 2, 0))
    others = [send_permute(self_id, loader, features, 2, 1)]
    to_node, from_node, to_row = index_tables(self_id, loader, rows_dev)
    rows, to_node, from_node, to_row, picks, entries, others = lax.optimization_barrier(
        (rows, to_node, from_node, to_row, picks, entries, others)
    )
    def forward_rows(outgoing, at):
        perm = [(c, (c + at + 1) % col_count) for c in range(col_count)]
        return lax.ppermute(outgoing, "col", perm)

    every = list(range(shifts))
    feature_rows = [rows]
    outgoing = outbound_blocks(picks, to_node, rows, every, capacity, block)
    arrived = [[forward_rows(outgoing[at], at) for at in every]]
    cot_out = send_permute(self_id, loader, cotangent, 1, 0)
    for other in others:
        rows = exchange(other)
        rows, cot_out, arrived = lax.optimization_barrier((rows, cot_out, arrived))
        feature_rows.append(rows)
        outgoing = outbound_blocks(picks, to_node, rows, every, capacity, block)
        cot_out, outgoing = lax.optimization_barrier((cot_out, outgoing))
        arrived.append([forward_rows(outgoing[at], at) for at in every])
    cot_rows = exchange(cot_out)

    queries, k_table, v_table = project(
        to_node, feature_rows, w_query, w_key, w_value, table_rows
    )
    for at in sorted(every, key=lambda at: min(at + 1, shifts - at)):
        parts = [moved[at] for moved in arrived]
        start = rows_dev + at * capacity * block
        k_table, v_table = remote_project(parts, w_key, w_value, k_table, v_table, start)

    layer_rows, mixed, stats = forward(
        entries, queries, k_table, v_table, gain, from_node, block, reads
    )
    layer_back = exchange(layer_rows)
    grad_q, own_k, own_v, far_all = backward(
        entries,
        to_node,
        cot_rows,
        gain,
        mixed,
        stats,
        queries,
        k_table,
        v_table,
        w_key,
        w_value,
        block,
        reads,
        shifts,
        splits,
    )
    returned = []
    for far in far_all:
        moved = []
        for at in range(shifts):
            perm = [(c, (c - at - 1) % col_count) for c in range(col_count)]
            moved.append(lax.ppermute(far[at], "col", perm))
        returned.append(moved)
    grad_back = []
    for at, (wide, moved) in enumerate(zip(splits, returned)):
        own = own_project(grad_q, own_k, own_v, w_query, w_key, w_value, wide, at)
        grad_back.append(exchange(collect(picks, own, from_node, moved, capacity, block)))
    return (permute(to_row, [layer_back]), permute(to_row, grad_back))


def solution(mesh):
    split = P(("row", "col"), None)
    in_specs = (split, split, P(), P(), P(), P(), P(), P(), split)
    return jax.shard_map(
        body, mesh=mesh, in_specs=in_specs, out_specs=(split, split), check_vma=False
    )
```

```python
import functools
import math

import jax
import jax.numpy as jnp
from jax import lax
from jax.experimental import pallas as pl
from jax.experimental.pallas import tpu as pltpu
from jax.sharding import PartitionSpec as P

HEADS = 8
HEAD_DIM = 128
SCALE = HEAD_DIM ** (-0.5)
LANE = 128
EXPO = SCALE * math.log2(math.e)
MIB = 1024 * 1024
SUBLANES = 8
CHUNK = 64
UNIT = 512
LIGHT = pl.CostEstimate(flops=0, transcendentals=0, bytes_accessed=0)

NT = (((1,), (1,)), ((), ()))
TN = (((0,), (0,)), ((), ()))
bf16 = jnp.bfloat16
f32 = jnp.float32


def hbm(shape, dtype):
    return pltpu.HBM(shape, jnp.dtype(dtype))


def pin(value):
    return pltpu.with_memory_space_constraint(value, pltpu.HBM)


def params(mib, axes=1):
    return pltpu.CompilerParams(
        dimension_semantics=("arbitrary",) * axes, vmem_limit_bytes=mib * MIB
    )


def whole(shape):
    zeros = (0,) * len(shape)
    return pl.BlockSpec(shape, lambda *_: zeros, pipeline_mode=pl.Buffered(1))


def matmul(left, right):
    return jnp.dot(left, right, preferred_element_type=f32)


def iota(shape, axis):
    return lax.broadcasted_iota(jnp.int32, shape, axis)


def lane_rank(mask):
    rows, count = mask.shape
    before = (iota((LANE, LANE), 0) < iota((LANE, LANE), 1)).astype(f32).astype(bf16)
    carry = jnp.zeros((rows, 1), f32)
    pieces = []
    for at in range(0, count, LANE):
        part = mask[:, at : at + LANE]
        pieces.append(matmul(part.astype(bf16), before) + carry)
        carry = carry + jnp.sum(part, axis=1, keepdims=True)
    return jnp.concatenate(pieces, axis=1)


def send_slots(nodes, devices):
    rows_dev = nodes.shape[1]
    per_peer = rows_dev // devices
    owner = lax.shift_right_logical(nodes, rows_dev.bit_length() - 1)
    owners = iota((devices, rows_dev), 0)
    mask = (owner == owners).astype(f32)
    slot = mask * (lane_rank(mask) + (owners * per_peer).astype(f32))
    return jnp.sum(slot, axis=0, keepdims=True).astype(jnp.int32)


def one_hot(cond):
    return jnp.where(cond, 1.0, 0.0)


def send_kernel(self_ref, loader_ref, rows_ref, out_ref, slot_ref):
    step = pl.program_id(0)
    chunk = out_ref.shape[0]
    rows_dev = rows_ref.shape[0]

    @pl.when(step == 0)
    def _():
        nodes = loader_ref[pl.ds(self_ref[0], 1), :]
        slot_ref[...] = send_slots(nodes, loader_ref.shape[0])

    pick = one_hot(slot_ref[...] == iota((chunk, rows_dev), 0) + step * chunk)
    out_ref[...] = matmul(pick.astype(bf16), rows_ref[...]).astype(bf16)


def send_permute(self_id, loader, rows, pieces, at):
    rows_dev, width = rows.shape
    chunk = 256
    piece = width // pieces
    return pl.pallas_call(
        send_kernel,
        out_shape=hbm((rows_dev, piece), bf16),
        grid_spec=pltpu.PrefetchScalarGridSpec(
            num_scalar_prefetch=1,
            grid=(rows_dev // chunk,),
            in_specs=[
                whole(loader.shape),
                pl.BlockSpec(
                    (rows_dev, piece), lambda i, _: (0, at), pipeline_mode=pl.Buffered(1)
                ),
            ],
            out_specs=pl.BlockSpec((chunk, piece), lambda i, _: (i, 0)),
            scratch_shapes=[pltpu.VMEM((1, rows_dev), jnp.int32)],
        ),
        compiler_params=params(10),
        name="send_permute",
    )(self_id, loader, pin(rows))


def index_kernel(self_ref, loader_ref, to_node_ref, from_node_ref, to_row_ref, slot_ref, key_ref):
    step = pl.program_id(0)
    devices, rows_dev = loader_ref.shape
    per_peer = rows_dev // devices
    chunk = from_node_ref.shape[0]
    sources = chunk // per_peer
    me = self_ref[0]

    @pl.when(step == 0)
    def _():
        slot_ref[...] = send_slots(loader_ref[pl.ds(me, 1), :], devices)
        owner = lax.shift_right_logical(loader_ref[...], rows_dev.bit_length() - 1)
        mask = (owner == me).astype(f32)
        rank = lane_rank(mask).astype(jnp.int32)
        key_ref[...] = jnp.where(owner == me, rank, -1)

    pieces = []
    for t in range(sources):
        source = step * sources + t
        key = key_ref[pl.ds(source, 1), :]
        local = loader_ref[pl.ds(source, 1), :] - me * rows_dev
        hit = key == iota((per_peer, rows_dev), 0)
        pieces.append(jnp.sum(jnp.where(hit, local.astype(f32), 0.0), axis=1, keepdims=True))
    arriving = jnp.concatenate(pieces, axis=0).astype(jnp.int32)
    pick = one_hot(arriving == iota((chunk, rows_dev), 1))
    from_node_ref[...] = pick.astype(bf16)
    to_node_ref[...] = pick.T.astype(bf16)
    back = one_hot(slot_ref[...] == iota((chunk, rows_dev), 0) + step * chunk)
    to_row_ref[...] = back.T.astype(bf16)


def index_tables(self_id, loader, rows_dev):
    chunk = LANE
    square = hbm((rows_dev, rows_dev), bf16)
    return pl.pallas_call(
        index_kernel,
        out_shape=(square, square, square),
        grid_spec=pltpu.PrefetchScalarGridSpec(
            num_scalar_prefetch=1,
            grid=(rows_dev // chunk,),
            in_specs=[whole(loader.shape)],
            out_specs=(
                pl.BlockSpec((rows_dev, chunk), lambda i, _: (0, i)),
                pl.BlockSpec((chunk, rows_dev), lambda i, _: (i, 0)),
                pl.BlockSpec((rows_dev, chunk), lambda i, _: (0, i)),
            ),
            scratch_shapes=[
                pltpu.VMEM((1, rows_dev), jnp.int32),
                pltpu.VMEM(loader.shape, jnp.int32),
            ],
        ),
        compiler_params=params(10),
        name="index_tables",
    )(self_id, loader)


def permute_kernel(pick_ref, rows_ref, *refs):
    out_ref = refs[-1]
    chunk = out_ref.shape[0]
    at = pl.multiple_of(pl.program_id(1) * chunk, chunk)
    out_ref[...] = matmul(pick_ref[pl.ds(at, chunk), :], rows_ref[...]).astype(bf16)


def permute(pick, pieces):
    rows_dev = pick.shape[0]
    width = sum(rows.shape[1] for rows in pieces)
    chunk = 256
    out, low = [], 0
    for rows in pieces:
        first = low // UNIT
        out = [
            pl.pallas_call(
                permute_kernel,
                out_shape=hbm((rows_dev, width), bf16),
                grid=(rows.shape[1] // UNIT, rows_dev // chunk),
                in_specs=[
                    whole(pick.shape),
                    pl.BlockSpec((rows_dev, UNIT), lambda j, i: (0, j)),
                ]
                + [pl.BlockSpec(memory_space=pl.ANY)] * len(out),
                out_specs=pl.BlockSpec((chunk, UNIT), lambda j, i, first=first: (i, first + j)),
                input_output_aliases={2: 0} if out else {},
                compiler_params=params(10, 2),
                name="permute",
            )(pick, pin(rows), *out)
        ]
        low += rows.shape[1]
    return out[0]


def outbound_kernel(picks_ref, rows_ref, *refs):
    pick_refs, out_refs = refs[: len(refs) // 2], refs[len(refs) // 2 :]
    for pick_ref, out_ref in zip(pick_refs, out_refs):
        out_ref[...] = matmul(pick_ref[...], rows_ref[...]).astype(bf16)


def outbound_blocks(picks, to_node, rows, shifts, capacity, block):
    rows_dev, width = rows.shape

    def pick_spec(shift):
        def index(slot, picks):
            return jnp.maximum(picks[shift * capacity + slot], 0), 0

        return pl.BlockSpec((block, rows_dev), index)

    return pl.pallas_call(
        outbound_kernel,
        out_shape=[hbm((capacity * block, width), bf16)] * len(shifts),
        grid_spec=pltpu.PrefetchScalarGridSpec(
            num_scalar_prefetch=1,
            grid=(capacity,),
            in_specs=[whole(rows.shape)] + [pick_spec(shift) for shift in shifts],
            out_specs=[pl.BlockSpec((block, width), lambda i, _: (i, 0))] * len(shifts),
        ),
        compiler_params=params(16),
        name="outbound",
    )(picks, pin(rows), *[pin(to_node)] * len(shifts))


def project_kernel(to_node_ref, wq_ref, wk_ref, wv_ref, *refs):
    row_refs, (q_ref, k_ref, v_ref) = refs[:-3], refs[-3:]
    owned = [matmul(to_node_ref[...], ref[...]).astype(bf16) for ref in row_refs]
    owned = jnp.concatenate(owned, axis=1)
    q_ref[...] = matmul(owned, wq_ref[...]).astype(bf16)
    k_ref[...] = matmul(owned, wk_ref[...]).astype(bf16)
    v_ref[...] = matmul(owned, wv_ref[...]).astype(bf16)


def project(to_node, rows, w_query, w_key, w_value, table_rows):
    rows_dev = to_node.shape[0]
    width = w_query.shape[1]
    chunk = 256
    out_spec = pl.BlockSpec((chunk, width), lambda i: (i, 0))
    table = hbm((table_rows, width), bf16)
    return pl.pallas_call(
        project_kernel,
        out_shape=(hbm((rows_dev, width), bf16), table, table),
        grid=(rows_dev // chunk,),
        in_specs=[
            pl.BlockSpec((chunk, rows_dev), lambda i: (i, 0)),
            whole(w_query.shape),
            whole(w_key.shape),
            whole(w_value.shape),
        ]
        + [whole(piece.shape) for piece in rows],
        out_specs=(out_spec, out_spec, out_spec),
        compiler_params=params(20),
        name="project",
    )(pin(to_node), w_query, w_key, w_value, *map(pin, rows))


def remote_kernel(wk_ref, wv_ref, k_in, v_in, *refs):
    row_refs, (k_ref, v_ref) = refs[:-2], refs[-2:]
    rows = jnp.concatenate([ref[...] for ref in row_refs], axis=1)
    k_ref[...] = matmul(rows, wk_ref[...]).astype(bf16)
    v_ref[...] = matmul(rows, wv_ref[...]).astype(bf16)


def remote_project(rows, w_key, w_value, k_table, v_table, first_row):
    chunk = rows[0].shape[0]
    width = w_key.shape[1]
    at = first_row // chunk
    out_spec = pl.BlockSpec((chunk, width), lambda i: (at, 0))
    any_spec = pl.BlockSpec(memory_space=pl.ANY)
    table = hbm(k_table.shape, bf16)
    return pl.pallas_call(
        remote_kernel,
        out_shape=(table, table),
        grid=(1,),
        in_specs=[whole(w_key.shape), whole(w_value.shape), any_spec, any_spec]
        + [whole(piece.shape) for piece in rows],
        out_specs=(out_spec, out_spec),
        input_output_aliases={2: 0, 3: 1},
        compiler_params=params(12),
        name="remote_project",
    )(w_key, w_value, k_table, v_table, *rows)


def split_dot(left, right):
    return lax.dot_general(left, right, NT, preferred_element_type=f32)


def fold(rows, op):
    total = rows[:SUBLANES]
    for at in range(SUBLANES, rows.shape[0], SUBLANES):
        total = op(total, rows[at : at + SUBLANES])
    return total


def entry_specs(block, width, reads):
    return [
        pl.BlockSpec((block, width), lambda i, entries, j=j: (entries[i * reads + j], 0))
        for j in range(reads)
    ]


def entry_args(table, reads):
    return [pin(table)] * reads


def forward_kernel(
    reads,
    entries_ref,
    q_ref,
    gain_ref,
    from_node_ref,
    *refs,
):
    k_refs, v_refs = refs[:reads], refs[reads : 2 * reads]
    out_hbm, mixed_ref, stats_ref, layer_ref, score_ref, prob_ref = refs[2 * reads : -2]
    out_ref, out_sem = refs[-2:]
    block, width = q_ref.shape
    step = pl.program_id(0)
    keys = reads * block
    for head in range(HEADS):
        cols = slice(head * HEAD_DIM, (head + 1) * HEAD_DIM)
        key_rows = jnp.concatenate([ref[:, cols] for ref in k_refs], axis=0)
        score_ref[head] = split_dot(key_rows, q_ref[:, cols])
    for head in range(HEADS):
        top = fold(score_ref[head, :CHUNK, :], jnp.maximum)
        for at in range(CHUNK, keys, CHUNK):
            top = jnp.maximum(top, fold(score_ref[head, at : at + CHUNK, :], jnp.maximum))
        top = jnp.max(top, axis=0, keepdims=True)
        total = jnp.zeros((SUBLANES, block), f32)
        for at in range(0, keys, CHUNK):
            expo = jnp.exp2((score_ref[head, at : at + CHUNK, :] - top) * EXPO)
            score_ref[head, at : at + CHUNK, :] = expo
            total = total + fold(expo, jnp.add)
        inv = 1.0 / jnp.sum(total, axis=0, keepdims=True)
        for at in range(0, keys, CHUNK):
            part = slice(at, at + CHUNK)
            prob_ref[head, part, :] = (score_ref[head, part, :] * inv).astype(bf16)
        stats_ref[2 * head : 2 * head + 1, :] = top
        stats_ref[2 * head + 1 : 2 * head + 2, :] = inv
    for head in range(HEADS):
        cols = slice(head * HEAD_DIM, (head + 1) * HEAD_DIM)
        vals = jnp.concatenate([ref[:, cols] for ref in v_refs], axis=0)
        mixed_ref[:, cols] = lax.dot_general(
            prob_ref[head], vals, TN, preferred_element_type=f32
        )
    mixed = mixed_ref[...]
    inv_rms = lax.rsqrt(jnp.mean(mixed * mixed, axis=1, keepdims=True) + 1e-06)
    rows = pl.ds(pl.multiple_of(step * block, block), block)
    layer_ref[rows, :] = (mixed * inv_rms * gain_ref[...]).astype(bf16)

    @pl.when(step == pl.num_programs(0) - 1)
    def _():
        chunk = 2 * block
        saves = []
        for at in range(0, out_ref.shape[0], chunk):
            part = slice(at, at + chunk)
            out_ref[part, :] = matmul(from_node_ref[part, :], layer_ref[...]).astype(bf16)
            saves.append(
                pltpu.make_async_copy(
                    out_ref.at[part, :], out_hbm.at[part, :], out_sem.at[at // chunk]
                )
            )
            saves[-1].start()
        for save in saves:
            save.wait()


def forward(entries, queries, k_table, v_table, gain, from_node, block, reads):
    rows_dev, width = queries.shape
    return pl.pallas_call(
        functools.partial(forward_kernel, reads),
        out_shape=(
            hbm((rows_dev, width), bf16),
            hbm((rows_dev, width), f32),
            hbm((rows_dev // block * 2 * HEADS, block), f32),
        ),
        grid_spec=pltpu.PrefetchScalarGridSpec(
            num_scalar_prefetch=1,
            grid=(rows_dev // block,),
            in_specs=[
                pl.BlockSpec((block, width), lambda i, _: (i, 0)),
                whole(gain.shape),
                whole(from_node.shape),
            ]
            + entry_specs(block, width, reads) * 2,
            out_specs=(
                pl.BlockSpec(memory_space=pl.ANY),
                pl.BlockSpec((block, width), lambda i, _: (i, 0)),
                pl.BlockSpec((2 * HEADS, block), lambda i, _: (i, 0)),
            ),
            scratch_shapes=[
                pltpu.VMEM((rows_dev, width), bf16),
                pltpu.VMEM((HEADS, reads * block, block), f32),
                pltpu.VMEM((HEADS, reads * block, block), bf16),
                pltpu.VMEM((rows_dev, width), bf16),
                pltpu.SemaphoreType.DMA((rows_dev // (2 * block),)),
            ],
        ),
        compiler_params=params(32),
        name="forward",
    )(
        entries,
        pin(queries),
        gain,
        from_node,
        *entry_args(k_table, reads),
        *entry_args(v_table, reads),
    )


def backward_kernel(
    reads,
    shifts,
    entries_ref,
    to_node_ref,
    cot_ref,
    gain_ref,
    mixed_ref,
    stats_ref,
    q_ref,
    *refs,
):
    k_refs, v_refs = refs[:reads], refs[reads : 2 * reads]
    wk_hbm, wv_hbm, gq_ref, own_k_hbm, own_v_hbm = refs[2 * reads : 2 * reads + 5]
    far_refs = refs[2 * reads + 5 : -14]
    sum_k_ref, sum_v_ref, prob_ref, grad_prob_ref, prob_half_ref = refs[-14:-9]
    grad_score_ref, grad_mix_ref, own_k_ref, own_v_ref, wk_ref, wv_ref = refs[-9:-3]
    w_sem, own_k_sem, own_v_sem = refs[-3:]
    block, width = q_ref.shape
    step = pl.program_id(0)
    own = own_k_ref.shape[0]
    keys = reads * block
    load_wk = pltpu.make_async_copy(wk_hbm, wk_ref, w_sem.at[0])
    load_wv = pltpu.make_async_copy(wv_hbm, wv_ref, w_sem.at[1])
    save_k = pltpu.make_async_copy(own_k_ref, own_k_hbm, own_k_sem)
    save_v = pltpu.make_async_copy(own_v_ref, own_v_hbm, own_v_sem)

    @pl.when(step == 0)
    def _():
        sum_k_ref[...] = jnp.zeros_like(sum_k_ref)
        sum_v_ref[...] = jnp.zeros_like(sum_v_ref)
        load_wk.start()
        load_wv.start()

    entries = [entries_ref[step * reads + j] * block for j in range(reads)]
    starts = [pl.multiple_of(at, block) for at in entries]
    mixed = mixed_ref[...]
    inv_rms = lax.rsqrt(jnp.mean(mixed * mixed, axis=1, keepdims=True) + 1e-06)
    grad_in = matmul(to_node_ref[...], cot_ref[...]) * gain_ref[...]
    inner = jnp.mean(grad_in * mixed, axis=1, keepdims=True)
    grad_mix = inv_rms * (grad_in - mixed * (inv_rms * inv_rms * inner))
    grad_mix_ref[...] = grad_mix.astype(bf16)
    for head in range(HEADS):
        cols = slice(head * HEAD_DIM, (head + 1) * HEAD_DIM)
        key_rows = jnp.concatenate([ref[:, cols] for ref in k_refs], axis=0)
        val_rows = jnp.concatenate([ref[:, cols] for ref in v_refs], axis=0)
        prob_ref[head] = split_dot(key_rows, q_ref[:, cols])
        grad_prob_ref[head] = split_dot(val_rows, grad_mix_ref[:, cols])
    for head in range(HEADS):
        top = stats_ref[2 * head : 2 * head + 1, :]
        inv = stats_ref[2 * head + 1 : 2 * head + 2, :]
        total = jnp.zeros((SUBLANES, block), f32)
        for at in range(0, keys, CHUNK):
            part = slice(at, at + CHUNK)
            prob = jnp.exp2((prob_ref[head, part, :] - top) * EXPO) * inv
            prob_ref[head, part, :] = prob
            prob_half_ref[head, part, :] = prob.astype(bf16)
            total = total + fold(prob * grad_prob_ref[head, part, :], jnp.add)
        delta = jnp.sum(total, axis=0, keepdims=True)
        for at in range(0, keys, CHUNK):
            part = slice(at, at + CHUNK)
            centred = (grad_prob_ref[head, part, :] - delta) * SCALE
            grad_score_ref[head, part, :] = (prob_ref[head, part, :] * centred).astype(bf16)
    for head in range(HEADS):
        cols = slice(head * HEAD_DIM, (head + 1) * HEAD_DIM)
        key_rows = jnp.concatenate([ref[:, cols] for ref in k_refs], axis=0)
        gq = lax.dot_general(grad_score_ref[head], key_rows, TN, preferred_element_type=f32)
        gq_ref[:, cols] = gq.astype(bf16)
        key_term = matmul(grad_score_ref[head], q_ref[:, cols])
        value_term = matmul(prob_half_ref[head], grad_mix_ref[:, cols])
        for j, at in enumerate(starts):
            part = slice(j * block, (j + 1) * block)
            rows = pl.ds(at, block)
            sum_k_ref[rows, cols] += key_term[part]
            sum_v_ref[rows, cols] += value_term[part]

    @pl.when(step == pl.num_programs(0) - 1)
    def _():
        own_k_ref[...] = sum_k_ref[:own, :].astype(bf16)
        save_k.start()
        own_v_ref[...] = sum_v_ref[:own, :].astype(bf16)
        save_v.start()
        load_wk.wait()
        load_wv.wait()
        low = 0
        for piece in range(0, len(far_refs), shifts):
            chunk, wide = far_refs[piece].shape
            outs = slice(low, low + wide)
            for at in range(shifts):
                rows = slice(own + at * chunk, own + (at + 1) * chunk)
                total = split_dot(sum_k_ref[rows, :].astype(bf16), wk_ref[outs, :])
                total += split_dot(sum_v_ref[rows, :].astype(bf16), wv_ref[outs, :])
                far_refs[piece + at][...] = total.astype(bf16)
            low += wide
        save_k.wait()
        save_v.wait()


def backward(
    entries,
    to_node,
    cot_rows,
    gain,
    mixed,
    stats,
    queries,
    k_table,
    v_table,
    w_key,
    w_value,
    block,
    reads,
    shifts,
    splits,
):
    rows_dev, width = queries.shape
    table_rows = k_table.shape[0]
    own = hbm((rows_dev, width), bf16)
    far = [((table_rows - rows_dev) // shifts, wide) for wide in splits for _ in range(shifts)]
    grant = min(60, 24 + 10 * table_rows * width // MIB)
    row_spec = pl.BlockSpec((block, width), lambda i, _: (i, 0))
    any_spec = pl.BlockSpec(memory_space=pl.ANY)
    out = pl.pallas_call(
        functools.partial(backward_kernel, reads, shifts),
        out_shape=[own, own, own] + [hbm(shape, bf16) for shape in far],
        grid_spec=pltpu.PrefetchScalarGridSpec(
            num_scalar_prefetch=1,
            grid=(rows_dev // block,),
            in_specs=[
                pl.BlockSpec((block, rows_dev), lambda i, _: (i, 0)),
                whole(cot_rows.shape),
                whole(gain.shape),
                row_spec,
                pl.BlockSpec((2 * HEADS, block), lambda i, _: (i, 0)),
                row_spec,
            ]
            + entry_specs(block, width, reads) * 2
            + [any_spec, any_spec],
            out_specs=[row_spec, any_spec, any_spec] + [whole(shape) for shape in far],
            scratch_shapes=[
                pltpu.VMEM((table_rows, width), f32),
                pltpu.VMEM((table_rows, width), f32),
                pltpu.VMEM((HEADS, reads * block, block), f32),
                pltpu.VMEM((HEADS, reads * block, block), f32),
                pltpu.VMEM((HEADS, reads * block, block), bf16),
                pltpu.VMEM((HEADS, reads * block, block), bf16),
                pltpu.VMEM((block, width), bf16),
                pltpu.VMEM((rows_dev, width), bf16),
                pltpu.VMEM((rows_dev, width), bf16),
                pltpu.VMEM(w_key.shape, bf16),
                pltpu.VMEM(w_value.shape, bf16),
                pltpu.SemaphoreType.DMA((2,)),
                pltpu.SemaphoreType.DMA,
                pltpu.SemaphoreType.DMA,
            ],
        ),
        compiler_params=params(grant),
        name="backward",
    )(
        entries,
        pin(to_node),
        cot_rows,
        gain,
        pin(mixed),
        pin(stats),
        pin(queries),
        *entry_args(k_table, reads),
        *entry_args(v_table, reads),
        pin(w_key),
        pin(w_value),
    )
    pieces = [out[at : at + shifts] for at in range(3, len(out), shifts)]
    return out[0], out[1], out[2], pieces


def own_kernel(q_ref, k_ref, v_ref, wq_ref, wk_ref, wv_ref, out_ref):
    total = split_dot(q_ref[...], wq_ref[...])
    total += split_dot(k_ref[...], wk_ref[...])
    total += split_dot(v_ref[...], wv_ref[...])
    out_ref[...] = total


def own_project(grad_q, own_k, own_v, w_query, w_key, w_value, wide, at):
    rows_dev, width = grad_q.shape
    chunk = 256
    spec = pl.BlockSpec((chunk, width), lambda i: (i, 0))
    w_spec = pl.BlockSpec((wide, width), lambda i: (at, 0), pipeline_mode=pl.Buffered(1))
    return pl.pallas_call(
        own_kernel,
        out_shape=pltpu.VMEM((rows_dev, wide), jnp.dtype(f32)),
        grid=(rows_dev // chunk,),
        in_specs=[spec, spec, spec, w_spec, w_spec, w_spec],
        out_specs=pl.BlockSpec((chunk, wide), lambda i: (i, 0)),
        compiler_params=params(16),
        cost_estimate=LIGHT,
        name="own_project",
    )(pin(grad_q), pin(own_k), pin(own_v), w_query, w_key, w_value)


def collect_kernel(capacity, block, picks_ref, own_ref, from_node_ref, *refs):
    returned, (out_ref, total_ref) = refs[:-2], refs[-2:]
    total_ref[...] = own_ref[...]
    for at, ref in enumerate(returned):
        for slot in range(capacity):
            pick = picks_ref[at * capacity + slot]

            @pl.when(pick >= 0)
            def _():
                rows = pl.ds(pl.multiple_of(pick * block, block), block)
                part = ref[slot * block : (slot + 1) * block, :]
                total_ref[rows, :] += part.astype(f32)

    out_ref[...] = matmul(from_node_ref[...], total_ref[...].astype(bf16)).astype(bf16)


def collect(picks, own, from_node, returned, capacity, block):
    rows_dev, width = own.shape
    return pl.pallas_call(
        functools.partial(collect_kernel, capacity, block),
        out_shape=hbm((rows_dev, width), bf16),
        grid_spec=pltpu.PrefetchScalarGridSpec(
            num_scalar_prefetch=1,
            grid=(1,),
            in_specs=[whole(own.shape), whole(from_node.shape)]
            + [whole(part.shape) for part in returned],
            out_specs=whole((rows_dev, width)),
            scratch_shapes=[pltpu.VMEM((rows_dev, width), f32)],
        ),
        compiler_params=params(14),
        cost_estimate=LIGHT,
        name="collect",
    )(picks, own, from_node, *returned)


def body(
    features, cotangent, loader, w_query, w_key, w_value, norm_gain, send_blocks, tile_lists
):
    row_count = lax.axis_size("row")
    col_count = lax.axis_size("col")
    devices = row_count * col_count
    col = lax.axis_index("col")
    self_index = lax.axis_index("row") * col_count + col
    self_id = self_index.astype(jnp.int32).reshape(1)
    rows_dev, width = features.shape
    per_peer = rows_dev // devices
    block_count = tile_lists.shape[0]
    block = rows_dev // block_count
    capacity = send_blocks.shape[2]
    shifts = col_count - 1
    table_rows = rows_dev + shifts * capacity * block
    reads = 1 + tile_lists.shape[1]
    loader = loader.reshape(devices, rows_dev)
    gain = norm_gain.reshape(1, width)

    splits = (width // 2, width // 2)

    def exchange(rows):
        buffer = rows.reshape(devices, per_peer, rows.shape[1])
        out = lax.all_to_all(buffer, ("row", "col"), split_axis=0, concat_axis=0, tiled=True)
        return out.reshape(rows.shape)

    send_row = lax.dynamic_index_in_dim(send_blocks, self_index, 0, keepdims=False)
    peers = (col + 1 + jnp.arange(shifts, dtype=jnp.int32)) % col_count
    picks = send_row[peers].reshape(-1)
    source = (tile_lists - block_count) // capacity
    shift = (col - source) % col_count
    moved = block_count + (shift - 1) * capacity + (tile_lists - block_count) % capacity
    entries = jnp.where(tile_lists < block_count, tile_lists, moved)
    entries = jnp.concatenate(
        [jnp.arange(block_count, dtype=jnp.int32)[:, None], entries], axis=1
    ).reshape(-1)

    rows = exchange(send_permute(self_id, loader, features, 2, 0))
    others = [send_permute(self_id, loader, features, 2, 1)]
    to_node, from_node, to_row = index_tables(self_id, loader, rows_dev)
    rows, to_node, from_node, to_row, picks, entries, others = lax.optimization_barrier(
        (rows, to_node, from_node, to_row, picks, entries, others)
    )
    def forward_rows(outgoing, at):
        perm = [(c, (c + at + 1) % col_count) for c in range(col_count)]
        return lax.ppermute(outgoing, "col", perm)

    every = list(range(shifts))
    feature_rows = [rows]
    outgoing = outbound_blocks(picks, to_node, rows, every, capacity, block)
    arrived = [[forward_rows(outgoing[at], at) for at in every]]
    cot_out = send_permute(self_id, loader, cotangent, 1, 0)
    for other in others:
        rows = exchange(other)
        rows, cot_out, arrived = lax.optimization_barrier((rows, cot_out, arrived))
        feature_rows.append(rows)
        outgoing = outbound_blocks(picks, to_node, rows, every, capacity, block)
        arrived.append([forward_rows(outgoing[at], at) for at in every])
    cot_rows = exchange(cot_out)

    queries, k_table, v_table = project(
        to_node, feature_rows, w_query, w_key, w_value, table_rows
    )
    for at in sorted(every, key=lambda at: min(at + 1, shifts - at)):
        parts = [moved[at] for moved in arrived]
        start = rows_dev + at * capacity * block
        k_table, v_table = remote_project(parts, w_key, w_value, k_table, v_table, start)

    layer_rows, mixed, stats = forward(
        entries, queries, k_table, v_table, gain, from_node, block, reads
    )
    layer_back = exchange(layer_rows)
    grad_q, own_k, own_v, far_all = backward(
        entries,
        to_node,
        cot_rows,
        gain,
        mixed,
        stats,
        queries,
        k_table,
        v_table,
        w_key,
        w_value,
        block,
        reads,
        shifts,
        splits,
    )
    returned = []
    for far in far_all:
        moved = []
        for at in range(shifts):
            perm = [(c, (c - at - 1) % col_count) for c in range(col_count)]
            moved.append(lax.ppermute(far[at], "col", perm))
        returned.append(moved)
    grad_back = []
    for at, (wide, moved) in enumerate(zip(splits, returned)):
        own = own_project(grad_q, own_k, own_v, w_query, w_key, w_value, wide, at)
        grad_back.append(exchange(collect(picks, own, from_node, moved, capacity, block)))
    return (permute(to_row, [layer_back]), permute(to_row, grad_back))


def solution(mesh):
    split = P(("row", "col"), None)
    in_specs = (split, split, P(), P(), P(), P(), P(), P(), split)
    return jax.shard_map(
        body, mesh=mesh, in_specs=in_specs, out_specs=(split, split), check_vma=False
    )
```

```python
import functools
import math

import jax
import jax.numpy as jnp
from jax import lax
from jax.experimental import pallas as pl
from jax.experimental.pallas import tpu as pltpu
from jax.sharding import PartitionSpec as P

HEADS = 8
HEAD_DIM = 128
SCALE = HEAD_DIM ** (-0.5)
LANE = 128
EXPO = SCALE * math.log2(math.e)
MIB = 1024 * 1024
SUBLANES = 8
CHUNK = 64
UNIT = 512
LIGHT = pl.CostEstimate(flops=0, transcendentals=0, bytes_accessed=0)

NT = (((1,), (1,)), ((), ()))
TN = (((0,), (0,)), ((), ()))
bf16 = jnp.bfloat16
f32 = jnp.float32


def hbm(shape, dtype):
    return pltpu.HBM(shape, jnp.dtype(dtype))


def pin(value):
    return pltpu.with_memory_space_constraint(value, pltpu.HBM)


def params(mib, axes=1):
    return pltpu.CompilerParams(
        dimension_semantics=("arbitrary",) * axes, vmem_limit_bytes=mib * MIB
    )


def whole(shape):
    zeros = (0,) * len(shape)
    return pl.BlockSpec(shape, lambda *_: zeros, pipeline_mode=pl.Buffered(1))


def matmul(left, right):
    return jnp.dot(left, right, preferred_element_type=f32)


def iota(shape, axis):
    return lax.broadcasted_iota(jnp.int32, shape, axis)


def lane_rank(mask):
    rows, count = mask.shape
    before = (iota((LANE, LANE), 0) < iota((LANE, LANE), 1)).astype(f32).astype(bf16)
    carry = jnp.zeros((rows, 1), f32)
    pieces = []
    for at in range(0, count, LANE):
        part = mask[:, at : at + LANE]
        pieces.append(matmul(part.astype(bf16), before) + carry)
        carry = carry + jnp.sum(part, axis=1, keepdims=True)
    return jnp.concatenate(pieces, axis=1)


def send_slots(nodes, devices):
    rows_dev = nodes.shape[1]
    per_peer = rows_dev // devices
    owner = lax.shift_right_logical(nodes, rows_dev.bit_length() - 1)
    owners = iota((devices, rows_dev), 0)
    mask = (owner == owners).astype(f32)
    slot = mask * (lane_rank(mask) + (owners * per_peer).astype(f32))
    return jnp.sum(slot, axis=0, keepdims=True).astype(jnp.int32)


def one_hot(cond):
    return jnp.where(cond, 1.0, 0.0)


def send_kernel(self_ref, loader_ref, rows_ref, out_ref, slot_ref):
    step = pl.program_id(0)
    chunk = out_ref.shape[0]
    rows_dev = rows_ref.shape[0]

    @pl.when(step == 0)
    def _():
        nodes = loader_ref[pl.ds(self_ref[0], 1), :]
        slot_ref[...] = send_slots(nodes, loader_ref.shape[0])

    pick = one_hot(slot_ref[...] == iota((chunk, rows_dev), 0) + step * chunk)
    out_ref[...] = matmul(pick.astype(bf16), rows_ref[...]).astype(bf16)


def send_permute(self_id, loader, rows, pieces, at):
    rows_dev, width = rows.shape
    chunk = 256
    piece = width // pieces
    return pl.pallas_call(
        send_kernel,
        out_shape=hbm((rows_dev, piece), bf16),
        grid_spec=pltpu.PrefetchScalarGridSpec(
            num_scalar_prefetch=1,
            grid=(rows_dev // chunk,),
            in_specs=[
                whole(loader.shape),
                pl.BlockSpec(
                    (rows_dev, piece), lambda i, _: (0, at), pipeline_mode=pl.Buffered(1)
                ),
            ],
            out_specs=pl.BlockSpec((chunk, piece), lambda i, _: (i, 0)),
            scratch_shapes=[pltpu.VMEM((1, rows_dev), jnp.int32)],
        ),
        compiler_params=params(10),
        name="send_permute",
    )(self_id, loader, pin(rows))


def index_kernel(self_ref, loader_ref, to_node_ref, from_node_ref, to_row_ref, slot_ref, key_ref):
    step = pl.program_id(0)
    devices, rows_dev = loader_ref.shape
    per_peer = rows_dev // devices
    chunk = from_node_ref.shape[0]
    sources = chunk // per_peer
    me = self_ref[0]

    @pl.when(step == 0)
    def _():
        slot_ref[...] = send_slots(loader_ref[pl.ds(me, 1), :], devices)
        owner = lax.shift_right_logical(loader_ref[...], rows_dev.bit_length() - 1)
        mask = (owner == me).astype(f32)
        rank = lane_rank(mask).astype(jnp.int32)
        key_ref[...] = jnp.where(owner == me, rank, -1)

    pieces = []
    for t in range(sources):
        source = step * sources + t
        key = key_ref[pl.ds(source, 1), :]
        local = loader_ref[pl.ds(source, 1), :] - me * rows_dev
        hit = key == iota((per_peer, rows_dev), 0)
        pieces.append(jnp.sum(jnp.where(hit, local.astype(f32), 0.0), axis=1, keepdims=True))
    arriving = jnp.concatenate(pieces, axis=0).astype(jnp.int32)
    pick = one_hot(arriving == iota((chunk, rows_dev), 1))
    from_node_ref[...] = pick.astype(bf16)
    to_node_ref[...] = pick.T.astype(bf16)
    back = one_hot(slot_ref[...] == iota((chunk, rows_dev), 0) + step * chunk)
    to_row_ref[...] = back.T.astype(bf16)


def index_tables(self_id, loader, rows_dev):
    chunk = LANE
    square = hbm((rows_dev, rows_dev), bf16)
    return pl.pallas_call(
        index_kernel,
        out_shape=(square, square, square),
        grid_spec=pltpu.PrefetchScalarGridSpec(
            num_scalar_prefetch=1,
            grid=(rows_dev // chunk,),
            in_specs=[whole(loader.shape)],
            out_specs=(
                pl.BlockSpec((rows_dev, chunk), lambda i, _: (0, i)),
                pl.BlockSpec((chunk, rows_dev), lambda i, _: (i, 0)),
                pl.BlockSpec((rows_dev, chunk), lambda i, _: (0, i)),
            ),
            scratch_shapes=[
                pltpu.VMEM((1, rows_dev), jnp.int32),
                pltpu.VMEM(loader.shape, jnp.int32),
            ],
        ),
        compiler_params=params(10),
        name="index_tables",
    )(self_id, loader)


def permute_kernel(pick_ref, rows_ref, *refs):
    out_ref = refs[-1]
    chunk = out_ref.shape[0]
    at = pl.multiple_of(pl.program_id(1) * chunk, chunk)
    out_ref[...] = matmul(pick_ref[pl.ds(at, chunk), :], rows_ref[...]).astype(bf16)


def permute(pick, pieces):
    rows_dev = pick.shape[0]
    width = sum(rows.shape[1] for rows in pieces)
    chunk = 256
    out, low = [], 0
    for rows in pieces:
        first = low // UNIT
        out = [
            pl.pallas_call(
                permute_kernel,
                out_shape=hbm((rows_dev, width), bf16),
                grid=(rows.shape[1] // UNIT, rows_dev // chunk),
                in_specs=[
                    whole(pick.shape),
                    pl.BlockSpec((rows_dev, UNIT), lambda j, i: (0, j)),
                ]
                + [pl.BlockSpec(memory_space=pl.ANY)] * len(out),
                out_specs=pl.BlockSpec((chunk, UNIT), lambda j, i, first=first: (i, first + j)),
                input_output_aliases={2: 0} if out else {},
                compiler_params=params(10, 2),
                name="permute",
            )(pick, pin(rows), *out)
        ]
        low += rows.shape[1]
    return out[0]


def outbound_kernel(picks_ref, rows_ref, *refs):
    pick_refs, out_refs = refs[: len(refs) // 2], refs[len(refs) // 2 :]
    for pick_ref, out_ref in zip(pick_refs, out_refs):
        out_ref[...] = matmul(pick_ref[...], rows_ref[...]).astype(bf16)


def outbound_blocks(picks, to_node, rows, shifts, capacity, block):
    rows_dev, width = rows.shape

    def pick_spec(shift):
        def index(slot, picks):
            return jnp.maximum(picks[shift * capacity + slot], 0), 0

        return pl.BlockSpec((block, rows_dev), index)

    return pl.pallas_call(
        outbound_kernel,
        out_shape=[hbm((capacity * block, width), bf16)] * len(shifts),
        grid_spec=pltpu.PrefetchScalarGridSpec(
            num_scalar_prefetch=1,
            grid=(capacity,),
            in_specs=[whole(rows.shape)] + [pick_spec(shift) for shift in shifts],
            out_specs=[pl.BlockSpec((block, width), lambda i, _: (i, 0))] * len(shifts),
        ),
        compiler_params=params(16),
        name="outbound",
    )(picks, pin(rows), *[pin(to_node)] * len(shifts))


def project_kernel(to_node_ref, wq_ref, wk_ref, wv_ref, *refs):
    row_refs, (q_ref, k_ref, v_ref) = refs[:-3], refs[-3:]
    owned = [matmul(to_node_ref[...], ref[...]).astype(bf16) for ref in row_refs]
    owned = jnp.concatenate(owned, axis=1)
    q_ref[...] = matmul(owned, wq_ref[...]).astype(bf16)
    k_ref[...] = matmul(owned, wk_ref[...]).astype(bf16)
    v_ref[...] = matmul(owned, wv_ref[...]).astype(bf16)


def project(to_node, rows, w_query, w_key, w_value, table_rows):
    rows_dev = to_node.shape[0]
    width = w_query.shape[1]
    chunk = 256
    out_spec = pl.BlockSpec((chunk, width), lambda i: (i, 0))
    table = hbm((table_rows, width), bf16)
    return pl.pallas_call(
        project_kernel,
        out_shape=(hbm((rows_dev, width), bf16), table, table),
        grid=(rows_dev // chunk,),
        in_specs=[
            pl.BlockSpec((chunk, rows_dev), lambda i: (i, 0)),
            whole(w_query.shape),
            whole(w_key.shape),
            whole(w_value.shape),
        ]
        + [whole(piece.shape) for piece in rows],
        out_specs=(out_spec, out_spec, out_spec),
        compiler_params=params(20),
        name="project",
    )(pin(to_node), w_query, w_key, w_value, *map(pin, rows))


def remote_kernel(wk_ref, wv_ref, k_in, v_in, *refs):
    row_refs, (k_ref, v_ref) = refs[:-2], refs[-2:]
    rows = jnp.concatenate([ref[...] for ref in row_refs], axis=1)
    k_ref[...] = matmul(rows, wk_ref[...]).astype(bf16)
    v_ref[...] = matmul(rows, wv_ref[...]).astype(bf16)


def remote_project(rows, w_key, w_value, k_table, v_table, first_row):
    chunk = rows[0].shape[0]
    width = w_key.shape[1]
    at = first_row // chunk
    out_spec = pl.BlockSpec((chunk, width), lambda i: (at, 0))
    any_spec = pl.BlockSpec(memory_space=pl.ANY)
    table = hbm(k_table.shape, bf16)
    return pl.pallas_call(
        remote_kernel,
        out_shape=(table, table),
        grid=(1,),
        in_specs=[whole(w_key.shape), whole(w_value.shape), any_spec, any_spec]
        + [whole(piece.shape) for piece in rows],
        out_specs=(out_spec, out_spec),
        input_output_aliases={2: 0, 3: 1},
        compiler_params=params(12),
        name="remote_project",
    )(w_key, w_value, k_table, v_table, *rows)


def split_dot(left, right):
    return lax.dot_general(left, right, NT, preferred_element_type=f32)


def fold(rows, op):
    total = rows[:SUBLANES]
    for at in range(SUBLANES, rows.shape[0], SUBLANES):
        total = op(total, rows[at : at + SUBLANES])
    return total


def entry_specs(block, width, reads):
    return [
        pl.BlockSpec((block, width), lambda i, entries, j=j: (entries[i * reads + j], 0))
        for j in range(reads)
    ]


def entry_args(table, reads):
    return [pin(table)] * reads


def forward_kernel(
    reads,
    entries_ref,
    q_ref,
    gain_ref,
    from_node_ref,
    *refs,
):
    k_refs, v_refs = refs[:reads], refs[reads : 2 * reads]
    out_hbm, mixed_ref, stats_ref, layer_ref, score_ref, prob_ref = refs[2 * reads : -2]
    out_ref, out_sem = refs[-2:]
    block, width = q_ref.shape
    step = pl.program_id(0)
    keys = reads * block
    for head in range(HEADS):
        cols = slice(head * HEAD_DIM, (head + 1) * HEAD_DIM)
        key_rows = jnp.concatenate([ref[:, cols] for ref in k_refs], axis=0)
        score_ref[head] = split_dot(key_rows, q_ref[:, cols])
    for head in range(HEADS):
        top = fold(score_ref[head, :CHUNK, :], jnp.maximum)
        for at in range(CHUNK, keys, CHUNK):
            top = jnp.maximum(top, fold(score_ref[head, at : at + CHUNK, :], jnp.maximum))
        top = jnp.max(top, axis=0, keepdims=True)
        total = jnp.zeros((SUBLANES, block), f32)
        for at in range(0, keys, CHUNK):
            expo = jnp.exp2((score_ref[head, at : at + CHUNK, :] - top) * EXPO)
            score_ref[head, at : at + CHUNK, :] = expo
            total = total + fold(expo, jnp.add)
        inv = 1.0 / jnp.sum(total, axis=0, keepdims=True)
        for at in range(0, keys, CHUNK):
            part = slice(at, at + CHUNK)
            prob_ref[head, part, :] = (score_ref[head, part, :] * inv).astype(bf16)
        stats_ref[2 * head : 2 * head + 1, :] = top
        stats_ref[2 * head + 1 : 2 * head + 2, :] = inv
    for head in range(HEADS):
        cols = slice(head * HEAD_DIM, (head + 1) * HEAD_DIM)
        vals = jnp.concatenate([ref[:, cols] for ref in v_refs], axis=0)
        mixed_ref[:, cols] = lax.dot_general(
            prob_ref[head], vals, TN, preferred_element_type=f32
        )
    mixed = mixed_ref[...]
    inv_rms = lax.rsqrt(jnp.mean(mixed * mixed, axis=1, keepdims=True) + 1e-06)
    rows = pl.ds(pl.multiple_of(step * block, block), block)
    layer_ref[rows, :] = (mixed * inv_rms * gain_ref[...]).astype(bf16)

    @pl.when(step == pl.num_programs(0) - 1)
    def _():
        chunk = 2 * block
        saves = []
        for at in range(0, out_ref.shape[0], chunk):
            part = slice(at, at + chunk)
            out_ref[part, :] = matmul(from_node_ref[part, :], layer_ref[...]).astype(bf16)
            saves.append(
                pltpu.make_async_copy(
                    out_ref.at[part, :], out_hbm.at[part, :], out_sem.at[at // chunk]
                )
            )
            saves[-1].start()
        for save in saves:
            save.wait()


def forward(entries, queries, k_table, v_table, gain, from_node, block, reads):
    rows_dev, width = queries.shape
    return pl.pallas_call(
        functools.partial(forward_kernel, reads),
        out_shape=(
            hbm((rows_dev, width), bf16),
            hbm((rows_dev, width), f32),
            hbm((rows_dev // block * 2 * HEADS, block), f32),
        ),
        grid_spec=pltpu.PrefetchScalarGridSpec(
            num_scalar_prefetch=1,
            grid=(rows_dev // block,),
            in_specs=[
                pl.BlockSpec((block, width), lambda i, _: (i, 0)),
                whole(gain.shape),
                whole(from_node.shape),
            ]
            + entry_specs(block, width, reads) * 2,
            out_specs=(
                pl.BlockSpec(memory_space=pl.ANY),
                pl.BlockSpec((block, width), lambda i, _: (i, 0)),
                pl.BlockSpec((2 * HEADS, block), lambda i, _: (i, 0)),
            ),
            scratch_shapes=[
                pltpu.VMEM((rows_dev, width), bf16),
                pltpu.VMEM((HEADS, reads * block, block), f32),
                pltpu.VMEM((HEADS, reads * block, block), bf16),
                pltpu.VMEM((rows_dev, width), bf16),
                pltpu.SemaphoreType.DMA((rows_dev // (2 * block),)),
            ],
        ),
        compiler_params=params(32),
        name="forward",
    )(
        entries,
        pin(queries),
        gain,
        from_node,
        *entry_args(k_table, reads),
        *entry_args(v_table, reads),
    )


def backward_kernel(
    reads,
    shifts,
    entries_ref,
    to_node_ref,
    cot_ref,
    gain_ref,
    mixed_ref,
    stats_ref,
    q_ref,
    *refs,
):
    k_refs, v_refs = refs[:reads], refs[reads : 2 * reads]
    wk_hbm, wv_hbm, gq_ref, own_k_hbm, own_v_hbm = refs[2 * reads : 2 * reads + 5]
    far_refs = refs[2 * reads + 5 : -14]
    sum_k_ref, sum_v_ref, prob_ref, grad_prob_ref, prob_half_ref = refs[-14:-9]
    grad_score_ref, grad_mix_ref, own_k_ref, own_v_ref, wk_ref, wv_ref = refs[-9:-3]
    w_sem, own_k_sem, own_v_sem = refs[-3:]
    block, width = q_ref.shape
    step = pl.program_id(0)
    own = own_k_ref.shape[0]
    keys = reads * block
    load_wk = pltpu.make_async_copy(wk_hbm, wk_ref, w_sem.at[0])
    load_wv = pltpu.make_async_copy(wv_hbm, wv_ref, w_sem.at[1])
    save_k = pltpu.make_async_copy(own_k_ref, own_k_hbm, own_k_sem)
    save_v = pltpu.make_async_copy(own_v_ref, own_v_hbm, own_v_sem)

    @pl.when(step == 0)
    def _():
        load_wk.start()
        load_wv.start()

    entries = [entries_ref[step * reads + j] * block for j in range(reads)]
    starts = [pl.multiple_of(at, block) for at in entries]
    flags = (pl.num_programs(0) + step) * reads
    fresh = [entries_ref[flags + j] > 0 for j in range(reads)]
    mixed = mixed_ref[...]
    inv_rms = lax.rsqrt(jnp.mean(mixed * mixed, axis=1, keepdims=True) + 1e-06)
    grad_in = matmul(to_node_ref[...], cot_ref[...]) * gain_ref[...]
    inner = jnp.mean(grad_in * mixed, axis=1, keepdims=True)
    grad_mix = inv_rms * (grad_in - mixed * (inv_rms * inv_rms * inner))
    grad_mix_ref[...] = grad_mix.astype(bf16)
    for head in range(HEADS):
        cols = slice(head * HEAD_DIM, (head + 1) * HEAD_DIM)
        key_rows = jnp.concatenate([ref[:, cols] for ref in k_refs], axis=0)
        val_rows = jnp.concatenate([ref[:, cols] for ref in v_refs], axis=0)
        prob_ref[head] = split_dot(key_rows, q_ref[:, cols])
        grad_prob_ref[head] = split_dot(val_rows, grad_mix_ref[:, cols])
    for head in range(HEADS):
        top = stats_ref[2 * head : 2 * head + 1, :]
        inv = stats_ref[2 * head + 1 : 2 * head + 2, :]
        total = jnp.zeros((SUBLANES, block), f32)
        for at in range(0, keys, CHUNK):
            part = slice(at, at + CHUNK)
            prob = jnp.exp2((prob_ref[head, part, :] - top) * EXPO) * inv
            prob_ref[head, part, :] = prob
            prob_half_ref[head, part, :] = prob.astype(bf16)
            total = total + fold(prob * grad_prob_ref[head, part, :], jnp.add)
        delta = jnp.sum(total, axis=0, keepdims=True)
        for at in range(0, keys, CHUNK):
            part = slice(at, at + CHUNK)
            centred = (grad_prob_ref[head, part, :] - delta) * SCALE
            grad_score_ref[head, part, :] = (prob_ref[head, part, :] * centred).astype(bf16)
    for head in range(HEADS):
        cols = slice(head * HEAD_DIM, (head + 1) * HEAD_DIM)
        key_rows = jnp.concatenate([ref[:, cols] for ref in k_refs], axis=0)
        gq = lax.dot_general(grad_score_ref[head], key_rows, TN, preferred_element_type=f32)
        gq_ref[:, cols] = gq.astype(bf16)
        key_term = matmul(grad_score_ref[head], q_ref[:, cols])
        value_term = matmul(prob_half_ref[head], grad_mix_ref[:, cols])
        for j, at in enumerate(starts):
            part = slice(j * block, (j + 1) * block)
            rows = pl.ds(at, block)
            key_sum = jnp.where(fresh[j], 0.0, sum_k_ref[rows, cols])
            value_sum = jnp.where(fresh[j], 0.0, sum_v_ref[rows, cols])
            sum_k_ref[rows, cols] = key_sum + key_term[part]
            sum_v_ref[rows, cols] = value_sum + value_term[part]

    @pl.when(step == pl.num_programs(0) - 1)
    def _():
        own_k_ref[...] = sum_k_ref[:own, :].astype(bf16)
        save_k.start()
        own_v_ref[...] = sum_v_ref[:own, :].astype(bf16)
        save_v.start()
        load_wk.wait()
        load_wv.wait()
        low = 0
        for piece in range(0, len(far_refs), shifts):
            chunk, wide = far_refs[piece].shape
            outs = slice(low, low + wide)
            for at in range(shifts):
                rows = slice(own + at * chunk, own + (at + 1) * chunk)
                total = split_dot(sum_k_ref[rows, :].astype(bf16), wk_ref[outs, :])
                total += split_dot(sum_v_ref[rows, :].astype(bf16), wv_ref[outs, :])
                far_refs[piece + at][...] = total.astype(bf16)
            low += wide
        save_k.wait()
        save_v.wait()


def backward(
    entries,
    to_node,
    cot_rows,
    gain,
    mixed,
    stats,
    queries,
    k_table,
    v_table,
    w_key,
    w_value,
    block,
    reads,
    shifts,
    splits,
):
    rows_dev, width = queries.shape
    table_rows = k_table.shape[0]
    own = hbm((rows_dev, width), bf16)
    far = [((table_rows - rows_dev) // shifts, wide) for wide in splits for _ in range(shifts)]
    grant = min(60, 24 + 10 * table_rows * width // MIB)
    row_spec = pl.BlockSpec((block, width), lambda i, _: (i, 0))
    any_spec = pl.BlockSpec(memory_space=pl.ANY)
    out = pl.pallas_call(
        functools.partial(backward_kernel, reads, shifts),
        out_shape=[own, own, own] + [hbm(shape, bf16) for shape in far],
        grid_spec=pltpu.PrefetchScalarGridSpec(
            num_scalar_prefetch=1,
            grid=(rows_dev // block,),
            in_specs=[
                pl.BlockSpec((block, rows_dev), lambda i, _: (i, 0)),
                whole(cot_rows.shape),
                whole(gain.shape),
                row_spec,
                pl.BlockSpec((2 * HEADS, block), lambda i, _: (i, 0)),
                row_spec,
            ]
            + entry_specs(block, width, reads) * 2
            + [any_spec, any_spec],
            out_specs=[row_spec, any_spec, any_spec] + [whole(shape) for shape in far],
            scratch_shapes=[
                pltpu.VMEM((table_rows, width), f32),
                pltpu.VMEM((table_rows, width), f32),
                pltpu.VMEM((HEADS, reads * block, block), f32),
                pltpu.VMEM((HEADS, reads * block, block), f32),
                pltpu.VMEM((HEADS, reads * block, block), bf16),
                pltpu.VMEM((HEADS, reads * block, block), bf16),
                pltpu.VMEM((block, width), bf16),
                pltpu.VMEM((rows_dev, width), bf16),
                pltpu.VMEM((rows_dev, width), bf16),
                pltpu.VMEM(w_key.shape, bf16),
                pltpu.VMEM(w_value.shape, bf16),
                pltpu.SemaphoreType.DMA((2,)),
                pltpu.SemaphoreType.DMA,
                pltpu.SemaphoreType.DMA,
            ],
        ),
        compiler_params=params(grant),
        name="backward",
    )(
        entries,
        pin(to_node),
        cot_rows,
        gain,
        pin(mixed),
        pin(stats),
        pin(queries),
        *entry_args(k_table, reads),
        *entry_args(v_table, reads),
        pin(w_key),
        pin(w_value),
    )
    pieces = [out[at : at + shifts] for at in range(3, len(out), shifts)]
    return out[0], out[1], out[2], pieces


def own_kernel(q_ref, k_ref, v_ref, wq_ref, wk_ref, wv_ref, out_ref):
    total = split_dot(q_ref[...], wq_ref[...])
    total += split_dot(k_ref[...], wk_ref[...])
    total += split_dot(v_ref[...], wv_ref[...])
    out_ref[...] = total


def own_project(grad_q, own_k, own_v, w_query, w_key, w_value, wide, at):
    rows_dev, width = grad_q.shape
    chunk = 256
    spec = pl.BlockSpec((chunk, width), lambda i: (i, 0))
    w_spec = pl.BlockSpec((wide, width), lambda i: (at, 0), pipeline_mode=pl.Buffered(1))
    return pl.pallas_call(
        own_kernel,
        out_shape=pltpu.VMEM((rows_dev, wide), jnp.dtype(f32)),
        grid=(rows_dev // chunk,),
        in_specs=[spec, spec, spec, w_spec, w_spec, w_spec],
        out_specs=pl.BlockSpec((chunk, wide), lambda i: (i, 0)),
        compiler_params=params(16),
        cost_estimate=LIGHT,
        name="own_project",
    )(pin(grad_q), pin(own_k), pin(own_v), w_query, w_key, w_value)


def collect_kernel(capacity, block, picks_ref, own_ref, from_node_ref, *refs):
    returned, (out_hbm, total_ref, out_ref, out_sem) = refs[:-4], refs[-4:]
    total_ref[...] = own_ref[...]
    for at, ref in enumerate(returned):
        for slot in range(capacity):
            pick = picks_ref[at * capacity + slot]

            @pl.when(pick >= 0)
            def _():
                rows = pl.ds(pl.multiple_of(pick * block, block), block)
                part = ref[slot * block : (slot + 1) * block, :]
                total_ref[rows, :] += part.astype(f32)

    total = total_ref[...].astype(bf16)
    chunk = 2 * block
    saves = []
    for at in range(0, out_ref.shape[0], chunk):
        part = slice(at, at + chunk)
        out_ref[part, :] = matmul(from_node_ref[part, :], total).astype(bf16)
        saves.append(
            pltpu.make_async_copy(
                out_ref.at[part, :], out_hbm.at[part, :], out_sem.at[at // chunk]
            )
        )
        saves[-1].start()
    for save in saves:
        save.wait()


def collect(picks, own, from_node, returned, capacity, block):
    rows_dev, width = own.shape
    return pl.pallas_call(
        functools.partial(collect_kernel, capacity, block),
        out_shape=hbm((rows_dev, width), bf16),
        grid_spec=pltpu.PrefetchScalarGridSpec(
            num_scalar_prefetch=1,
            grid=(1,),
            in_specs=[whole(own.shape), whole(from_node.shape)]
            + [whole(part.shape) for part in returned],
            out_specs=pl.BlockSpec(memory_space=pl.ANY),
            scratch_shapes=[
                pltpu.VMEM((rows_dev, width), f32),
                pltpu.VMEM((rows_dev, width), bf16),
                pltpu.SemaphoreType.DMA((rows_dev // (2 * block),)),
            ],
        ),
        compiler_params=params(14),
        cost_estimate=LIGHT,
        name="collect",
    )(picks, own, from_node, *returned)


def body(
    features, cotangent, loader, w_query, w_key, w_value, norm_gain, send_blocks, tile_lists
):
    row_count = lax.axis_size("row")
    col_count = lax.axis_size("col")
    devices = row_count * col_count
    col = lax.axis_index("col")
    self_index = lax.axis_index("row") * col_count + col
    self_id = self_index.astype(jnp.int32).reshape(1)
    rows_dev, width = features.shape
    per_peer = rows_dev // devices
    block_count = tile_lists.shape[0]
    block = rows_dev // block_count
    capacity = send_blocks.shape[2]
    shifts = col_count - 1
    table_rows = rows_dev + shifts * capacity * block
    reads = 1 + tile_lists.shape[1]
    loader = loader.reshape(devices, rows_dev)
    gain = norm_gain.reshape(1, width)

    splits = (width // 2, width // 2)

    def exchange(rows):
        buffer = rows.reshape(devices, per_peer, rows.shape[1])
        out = lax.all_to_all(buffer, ("row", "col"), split_axis=0, concat_axis=0, tiled=True)
        return out.reshape(rows.shape)

    send_row = lax.dynamic_index_in_dim(send_blocks, self_index, 0, keepdims=False)
    peers = (col + 1 + jnp.arange(shifts, dtype=jnp.int32)) % col_count
    picks = send_row[peers].reshape(-1)
    source = (tile_lists - block_count) // capacity
    shift = (col - source) % col_count
    moved = block_count + (shift - 1) * capacity + (tile_lists - block_count) % capacity
    entries = jnp.where(tile_lists < block_count, tile_lists, moved)
    entries = jnp.concatenate(
        [jnp.arange(block_count, dtype=jnp.int32)[:, None], entries], axis=1
    ).reshape(-1)
    order = jnp.arange(entries.shape[0], dtype=jnp.int32)
    earlier = (entries[:, None] == entries[None, :]) & (order[None, :] < order[:, None])
    first_use = 1 - jnp.max(earlier.astype(jnp.int32), axis=1)
    entries = jnp.concatenate([entries, first_use])

    rows = exchange(send_permute(self_id, loader, features, 2, 0))
    others = [send_permute(self_id, loader, features, 2, 1)]
    to_node, from_node, to_row = index_tables(self_id, loader, rows_dev)
    rows, to_node, from_node, to_row, picks, entries, others = lax.optimization_barrier(
        (rows, to_node, from_node, to_row, picks, entries, others)
    )
    def forward_rows(outgoing, at):
        perm = [(c, (c + at + 1) % col_count) for c in range(col_count)]
        return lax.ppermute(outgoing, "col", perm)

    every = list(range(shifts))
    feature_rows = [rows]
    outgoing = outbound_blocks(picks, to_node, rows, every, capacity, block)
    arrived = [[forward_rows(outgoing[at], at) for at in every]]
    cot_out = send_permute(self_id, loader, cotangent, 1, 0)
    for other in others:
        rows = exchange(other)
        rows, cot_out, arrived = lax.optimization_barrier((rows, cot_out, arrived))
        feature_rows.append(rows)
        outgoing = outbound_blocks(picks, to_node, rows, every, capacity, block)
        arrived.append([forward_rows(outgoing[at], at) for at in every])
    cot_rows = exchange(cot_out)

    queries, k_table, v_table = project(
        to_node, feature_rows, w_query, w_key, w_value, table_rows
    )
    for at in sorted(every, key=lambda at: min(at + 1, shifts - at)):
        parts = [moved[at] for moved in arrived]
        start = rows_dev + at * capacity * block
        k_table, v_table = remote_project(parts, w_key, w_value, k_table, v_table, start)

    layer_rows, mixed, stats = forward(
        entries, queries, k_table, v_table, gain, from_node, block, reads
    )
    layer_back = exchange(layer_rows)
    grad_q, own_k, own_v, far_all = backward(
        entries,
        to_node,
        cot_rows,
        gain,
        mixed,
        stats,
        queries,
        k_table,
        v_table,
        w_key,
        w_value,
        block,
        reads,
        shifts,
        splits,
    )
    returned = []
    for far in far_all:
        moved = []
        for at in range(shifts):
            perm = [(c, (c - at - 1) % col_count) for c in range(col_count)]
            moved.append(lax.ppermute(far[at], "col", perm))
        returned.append(moved)
    grad_back = []
    for at, (wide, moved) in enumerate(zip(splits, returned)):
        own = own_project(grad_q, own_k, own_v, w_query, w_key, w_value, wide, at)
        grad_back.append(exchange(collect(picks, own, from_node, moved, capacity, block)))
    return (permute(to_row, [layer_back]), permute(to_row, grad_back))


def solution(mesh):
    split = P(("row", "col"), None)
    in_specs = (split, split, P(), P(), P(), P(), P(), P(), split)
    return jax.shard_map(
        body, mesh=mesh, in_specs=in_specs, out_specs=(split, split), check_vma=False
    )
```
